32 devices in a mesh: groups: 2 (over y), blk: 4 (over z), det: 2 (over x), sub: 2 (over core).
Axes of the slice: x: 2, y: 2, z: 4, core: 2. Of those that a mesh axis runs over, the one named last changes fastest.
Arguments:
- data: bfloat16 [128, 16, 256], P(('groups', 'blk', 'det')), parts along dimension 0, may hold values from -6 to 6
- templates: bfloat16 [32, 16, 256], P(('groups', 'blk')), parts along dimension 0
- bin_cuts: int32 [32, 15], P(('groups', 'blk')), parts along dimension 0, may hold values from 1 to 2047, as said below
- trig_template: int32 [16, 2, 128], P(('groups', 'blk', 'det'), 'sub'), parts along dimension 0, may hold values from 0 to 15
- trig_pair: int32 [16, 2, 128], P(('groups', 'blk', 'det'), 'sub'), parts along dimension 0, may hold values from 0 to 63, as said below
- trig_tile: int32 [16, 2, 128], P(('groups', 'blk', 'det'), 'sub'), parts along dimension 0, may hold values from 0 to 7
Outputs:
- peak_snr: float32 [128, 2048], P(('groups', 'blk', 'det'), 'sub'), parts along dimension 0
- chi_snr: float32 [16, 2, 128, 128], P(('groups', 'blk', 'det'), 'sub'), parts along dimension 0
The draws below stay inside these ranges and needn't reach their ends.
There are 2 independent parts, one for each index of `groups`. The reference program is written for one: setup_inputs(seed, part) draws one part's arguments, and reference() takes and returns one part's arrays. A program takes and returns all parts, laid end to end along the dimension named above; each array names one. Nothing has to cross between parts.
Inputs may be any that keep to these rules, and one draw needn't show every extreme that they name: `trig_pair`: in each list [b, h], at most 32 entries lie in any one group of 8 consecutive data block ids that starts at a multiple of 8; one such group holds exactly 32 entries of every list. `bin_cuts`: each row is strictly increasing.
All inputs are finite; a program needn't handle non-finite values.
Results may differ from the reference program's by a relative error of at most 0.0035.
Values may be sent and summed in bfloat16 or wider, within the bound.
A program may use at most 64 MiB of HBM per device.

```python
import math
import jax
import jax.numpy as jnp
from jax import lax

FMAJ = 16
FMIN = 128
FREQS = 2048
NBINS = 16
TILE_STEPS = 8
TEMPLATES = 16
PAIR_DEV = 8
BLOCKS = 8
PAIRS = 64
HALVES = 2
TILES = 8
TRIG_DEV = 128
PCAP = 32


def draw_templates(key, part):
    shape = (TEMPLATES, FMAJ, 2 * FMIN)
    base = jax.random.normal(jax.random.fold_in(key, 11), shape, jnp.float32)
    column = jnp.exp(jax.random.uniform(jax.random.fold_in(key, 12), (FMAJ, FMIN), jnp.float32, -1.15, 1.15))
    row_scale = jnp.exp(jax.random.uniform(jax.random.fold_in(key, 13), (TEMPLATES, 1, 1), jnp.float32, -1.15, 1.15))
    column = jnp.concatenate([column, column], axis=1)
    return (base * column[None] * row_scale).astype(jnp.bfloat16)


def draw_bin_cuts(key, part):
    keys = jax.random.split(jax.random.fold_in(key, 21), TEMPLATES)

    def one_row(row_key):
        chosen = jax.random.permutation(row_key, FREQS - 1)[:NBINS - 1].astype(jnp.int32) + 1
        return jnp.sort(chosen)
    return jax.vmap(one_row)(keys).astype(jnp.int32)


def draw_trig_pair(key, part):
    owners = BLOCKS
    slots = owners * PCAP
    lists = BLOCKS * HALVES
    boost = jax.random.randint(jax.random.fold_in(key, 31), (owners,), 0, 4)
    forced = jax.random.randint(jax.random.fold_in(key, 32), (), 0, owners)
    slot_owner = jnp.arange(slots, dtype=jnp.int32) // PCAP
    noise = jax.random.randint(jax.random.fold_in(key, 33), (lists, slots), 0, 1024)
    score = boost[slot_owner][None, :] * 1024 + noise + jnp.where(slot_owner == forced, 8192, 0)[None, :]
    score = score * slots + jnp.arange(slots, dtype=jnp.int32)[None, :]
    unused, picked = lax.top_k(score, TRIG_DEV)
    shuffle_keys = jax.random.split(jax.random.fold_in(key, 34), lists)
    order = jax.vmap(lambda row_key: jax.random.permutation(row_key, TRIG_DEV))(shuffle_keys)
    picked = jnp.take_along_axis(picked, order, axis=1)
    within = jax.random.randint(jax.random.fold_in(key, 35), (lists, TRIG_DEV), 0, PAIR_DEV)
    result = picked // PCAP * PAIR_DEV + within
    return result.reshape(BLOCKS, HALVES, TRIG_DEV).astype(jnp.int32)


def place_ends(drawn, rng, smallest, largest):
    longest = drawn.shape.index(max(drawn.shape))
    spots = []
    for shift in (0, 1):
        where = [jax.random.randint(jax.random.fold_in(rng, axis), (), 0, length) for axis, length in enumerate(drawn.shape)]
        where[longest] = (where[longest] + shift) % drawn.shape[longest]
        spots.append(tuple(where))
    return drawn.at[spots[0]].set(smallest).at[spots[1]].set(largest)


def level_of(stream_key, shape, cuts, smallest, largest):
    loudness, own = 1.0, jax.random.fold_in(stream_key, 6)
    for axis_at, parts in cuts:
        draws = jnp.exp(jax.random.uniform(jax.random.fold_in(own, axis_at), (parts,), jnp.float32, smallest / len(cuts), largest / len(cuts)))
        loudness = loudness * jnp.repeat(draws, shape[axis_at] // parts).reshape([-1 if axis == axis_at else 1 for axis in range(len(shape))])
    return loudness


def scatter_about(stream_key, dims, spread, limit, cuts=(), kind=jnp.bfloat16):
    loudness = level_of(stream_key, dims, cuts, -0.22, 0.18) if cuts else 1.0
    entries = jax.random.normal(stream_key, dims, jnp.float32) * spread * loudness
    return jnp.minimum(jnp.maximum(entries, -limit), limit).astype(kind)


def setup_inputs(seed: int = 0, part: int = 0) -> dict:
    splits = jax.random.split(jax.random.key(seed), 7)
    own_keys = jax.random.split(jax.random.fold_in(splits[6], part), 7)
    data = scatter_about(own_keys[0], (PAIRS, FMAJ, 2 * FMIN), 1.0, 6.0, ((0, 8),))
    templates = draw_templates(jax.random.fold_in(jax.random.fold_in(splits[6], part), 71), part)
    bin_cuts = draw_bin_cuts(jax.random.fold_in(jax.random.fold_in(splits[6], part), 71), part)
    trig_template = place_ends(jax.random.randint(own_keys[3], (BLOCKS, HALVES, TRIG_DEV), 0, TEMPLATES), jax.random.fold_in(own_keys[3], 1), 0, TEMPLATES - 1).astype(jnp.int32)
    trig_pair = draw_trig_pair(jax.random.fold_in(jax.random.fold_in(splits[6], part), 71), part)
    trig_tile = place_ends(jax.random.randint(own_keys[5], (BLOCKS, HALVES, TRIG_DEV), 0, TILES), jax.random.fold_in(own_keys[5], 1), 0, TILES - 1).astype(jnp.int32)
    return {"data": data, "templates": templates, "bin_cuts": bin_cuts, "trig_template": trig_template, "trig_pair": trig_pair, "trig_tile": trig_tile}


def phase_table(rows, cols, period):
    index = jnp.arange(rows, dtype=jnp.int32)[:, None] * jnp.arange(cols, dtype=jnp.int32)[None, :] % period
    angle = index.astype(jnp.float32) * (2.0 * math.pi / period)
    return (jnp.cos(angle), jnp.sin(angle))

def second_matrix(steps, n_minor):
    index = jnp.arange(n_minor, dtype=jnp.int32)[:, None] * steps[None, :] % n_minor
    angle = index.astype(jnp.float32) * (2.0 * math.pi / n_minor)
    cosine = jnp.cos(angle)
    sine = jnp.sin(angle)
    upper = jnp.concatenate([cosine, sine], axis=1)
    lower = jnp.concatenate([-sine, cosine], axis=1)
    return jnp.concatenate([upper, lower], axis=0).astype(jnp.bfloat16)

def make_tables(n_major, n_minor):
    cos_major, sin_major = phase_table(n_major, n_major, n_major)
    twid_cos, twid_sin = phase_table(n_major, n_minor, n_major * n_minor)
    return (cos_major.astype(jnp.bfloat16), sin_major.astype(jnp.bfloat16), twid_cos, twid_sin)

def conj_product(rows, tmpl):
    n_minor = rows.shape[-1] // 2
    data_re = rows[..., :n_minor].astype(jnp.float32)
    data_im = rows[..., n_minor:].astype(jnp.float32)
    tmpl_re = tmpl[..., :n_minor].astype(jnp.float32)
    tmpl_im = tmpl[..., n_minor:].astype(jnp.float32)
    real_part = data_re * tmpl_re + data_im * tmpl_im
    imag_part = data_im * tmpl_re - data_re * tmpl_im
    return jnp.concatenate([real_part, imag_part], axis=-1).astype(jnp.bfloat16)

def first_section(spectra, tables):
    cos_major, sin_major, twid_cos, twid_sin = tables
    n_minor = spectra.shape[-1] // 2
    wide = spectra.astype(jnp.float32)
    cos_part = jnp.einsum('...ic,ia->...ac', wide, cos_major.astype(jnp.float32), precision=lax.Precision.HIGHEST)
    sin_part = jnp.einsum('...ic,ia->...ac', wide, sin_major.astype(jnp.float32), precision=lax.Precision.HIGHEST)
    real_part = cos_part[..., :n_minor] - sin_part[..., n_minor:]
    imag_part = sin_part[..., :n_minor] + cos_part[..., n_minor:]
    turned_re = real_part * twid_cos - imag_part * twid_sin
    turned_im = real_part * twid_sin + imag_part * twid_cos
    return jnp.concatenate([turned_re, turned_im], axis=-1).astype(jnp.bfloat16)

def chi_block(rows, tmpl, cuts, starts, tables, n_bins, n_steps):
    n_major = rows.shape[1]
    n_minor = rows.shape[2] // 2
    spectra = conj_product(rows, tmpl)
    freq = n_minor * jnp.arange(n_major, dtype=jnp.int32)[:, None] + jnp.arange(n_minor, dtype=jnp.int32)[None, :]
    which = lax.optimization_barrier(jnp.sum((cuts[:, :, None, None] <= freq[None, None]).astype(jnp.int32), axis=1))
    member = which[:, None] == jnp.arange(n_bins, dtype=jnp.int32)[None, :, None, None]
    member = jnp.concatenate([member, member], axis=-1)
    masked = jnp.where(member, spectra[:, None], jnp.zeros((), jnp.bfloat16))
    sectioned = first_section(masked, tables)
    steps = starts[:, None] + jnp.arange(n_steps, dtype=jnp.int32)[None, :]
    mats = jax.vmap(lambda values: second_matrix(values, n_minor))(steps)
    binned = jnp.einsum('rbac,rcs->rbas', sectioned.astype(jnp.float32), mats.astype(jnp.float32), precision=lax.Precision.HIGHEST)
    bin_re = binned[..., :n_steps]
    bin_im = binned[..., n_steps:]
    total_re = lax.optimization_barrier(jnp.sum(bin_re, axis=1))
    total_im = lax.optimization_barrier(jnp.sum(bin_im, axis=1))
    norms = lax.optimization_barrier(jnp.sum(jnp.square(tmpl.astype(jnp.float32)), axis=(1, 2)))
    diff_re = bin_re - total_re[:, None] / n_bins
    diff_im = bin_im - total_im[:, None] / n_bins
    chisq = n_bins * lax.optimization_barrier(jnp.sum(diff_re * diff_re + diff_im * diff_im, axis=1)) / norms[:, None, None]
    reduced = chisq / (2.0 * n_bins - 2.0)
    rho = jnp.sqrt(total_re * total_re + total_im * total_im) / jnp.sqrt(norms)[:, None, None]
    weighted = jnp.where(reduced > 1.0, rho * ((1.0 + reduced ** 3) * 0.5) ** (-1.0 / 6.0), rho)
    return jnp.transpose(weighted, (0, 2, 1)).reshape(rows.shape[0], -1)

def reference(data, templates, bin_cuts, trig_template, trig_pair, trig_tile):
    tables = make_tables(FMAJ, FMIN)
    second = second_matrix(jnp.arange(FMIN, dtype=jnp.int32), FMIN)
    norms = lax.optimization_barrier(jnp.sum(jnp.square(templates.astype(jnp.float32)), axis=(1, 2)))

    def scan_step(peak, index):
        spectra = conj_product(data, templates[index][None])
        sectioned = first_section(spectra, tables)
        result = jnp.einsum('pac,cs->pas', sectioned.astype(jnp.float32), second.astype(jnp.float32), precision=lax.Precision.HIGHEST)
        power = (result[..., :FMIN] ** 2 + result[..., FMIN:] ** 2) / norms[index]
        return (jnp.maximum(peak, power), None)
    peak, unused = lax.scan(scan_step, jnp.zeros((PAIRS, FMAJ, FMIN), jnp.float32), jnp.arange(TEMPLATES, dtype=jnp.int32))
    peak_snr = jnp.transpose(jnp.sqrt(peak), (0, 2, 1)).reshape(PAIRS, FREQS)
    pair_ids = trig_pair.reshape(-1, TRIG_DEV).astype(jnp.int32)
    starts = (jnp.arange(HALVES, dtype=jnp.int32)[None, :, None] * (FMIN // HALVES) + trig_tile * TILE_STEPS).reshape(-1, TRIG_DEV)
    tmpl_ids = trig_template.reshape(-1, TRIG_DEV)

    def per_list(packed):
        ids, pairs, first_steps = packed
        return chi_block(data[pairs], templates[ids], bin_cuts[ids], first_steps, tables, NBINS, TILE_STEPS)
    chi = lax.map(per_list, (tmpl_ids, pair_ids, starts))
    chi_snr = chi.reshape(BLOCKS, HALVES, TRIG_DEV, FMAJ * TILE_STEPS)
    return (peak_snr, chi_snr)
```

```python
import functools
import math

import jax
import jax.numpy as jnp
import numpy as np
from jax import lax
from jax.experimental import pallas as pl
from jax.experimental.pallas import tpu as pltpu
from jax.sharding import PartitionSpec as P

MESH = pl.DeviceIdType.MESH
NMAJ = 16
NMIN = 128
NCUT = 16
STEPS = 8
GROUP = 8


def unit_circle(index, period):
    angle = (index % period) * (2.0 * math.pi / period)
    return np.cos(angle), np.sin(angle)


def host_tables(n_sub):
    bf16 = jnp.bfloat16
    major = np.arange(NMAJ)
    minor = np.arange(NMIN)
    cos16, sin16 = unit_circle(major[:, None] * major[None, :], NMAJ)
    eye = np.eye(GROUP)
    first = np.concatenate([np.kron(eye, cos16), np.kron(eye, sin16)], axis=1).astype(bf16)
    twc, tws = unit_circle(major[:, None] * minor[None, :], NMAJ * NMIN)
    twiddle = np.concatenate([twc, tws], axis=1).astype(np.float32)
    n_half = NMIN // n_sub
    second = []
    for half in range(n_sub):
        steps = half * n_half + np.arange(n_half)
        cosine, sine = unit_circle(steps[:, None] * minor[None, :], NMIN)
        real_rows = np.concatenate([cosine, -sine], axis=1)
        imag_rows = np.concatenate([sine, cosine], axis=1)
        second.append(np.concatenate([real_rows, imag_rows], axis=0))
    second = np.stack(second).astype(bf16)
    times = np.arange(NMAJ * STEPS)
    cosine, sine = unit_circle(minor[:, None] * times[None, :], NMAJ * NMIN)
    tile_dft = np.concatenate(
        [np.concatenate([cosine, sine], axis=1), np.concatenate([-sine, cosine], axis=1)], axis=0
    ).astype(bf16)
    rowc, rows = unit_circle(major[:, None] * (times % NMAJ)[None, :], NMAJ)
    row_phase = np.tile(np.concatenate([rowc, rows], axis=1), (GROUP, 1)).astype(bf16)
    starts = np.arange(NMIN // STEPS) * STEPS
    phc, phs = unit_circle(starts[:, None] * minor[None, :], NMIN)
    tile_phase = np.concatenate([phc, phs], axis=1).astype(np.float32)[:, None, :]
    return first, twiddle, second, tile_dft, row_phase, tile_phase


def swap_blocks(x):
    sub = lax.broadcasted_iota(jnp.int32, x.shape, 0)
    grp = lax.broadcasted_iota(jnp.int32, x.shape, 1) // NMAJ
    rows, lanes = x.shape
    for bit in (1, 2, 4):
        up = pltpu.roll(pltpu.roll(x, rows - bit, 0), NMAJ * bit, 1)
        down = pltpu.roll(pltpu.roll(x, bit, 0), lanes - NMAJ * bit, 1)
        sb, gb = (sub & bit) != 0, (grp & bit) != 0
        x = jnp.where(jnp.logical_and(jnp.logical_not(sb), gb), up,
                      jnp.where(jnp.logical_and(sb, jnp.logical_not(gb)), down, x))
    return x


def conj_product(data, tmpl):
    dr, di = data[..., :NMIN], data[..., NMIN:]
    tr, ti = tmpl[..., :NMIN], tmpl[..., NMIN:]
    return dr * tr + di * ti, di * tr - dr * ti


def gather_kernel(n_blk, n_det, n_sub, *refs):
    (ids_k_in, ids_p_in, ids_t_in, own_in, tmpl_in, cuts_in, first_in, twiddle_in, second_in, tile_dft_in,
     row_phase_in, tile_phase_in, peak_out, z_out, hot_out, between_out, keep_out, spin_out, rnorm_out,
     tile_dft, row_phase, data4, tmpl4, cuts, ids_k, ids_p, ids_t, ids_v, first, twiddle, second, tile_phase,
     cut_rows, norm_tab, turned,
     local_sem, z_send, z_recv, x_send, x_recv, s_send, s_recv, tz_send, tz_recv, ts_send, ts_recv,
     cz_send, cz_recv) = refs
    f32, bf16 = jnp.float32, jnp.bfloat16
    b = lax.axis_index("blk")
    d = lax.axis_index("det")
    half = lax.axis_index("sub")
    other = n_sub - 1 - half
    pairs = own_in.shape[0]
    kb = tmpl_in.shape[0]
    n_cut = cuts_in.shape[1]
    n_tmpl = n_blk * kb
    n_trig = ids_k_in.shape[2]
    n_grp = n_trig // GROUP
    hp, hk = pairs // n_sub, kb // n_sub
    own = b * n_det + d

    barrier = pltpu.get_barrier_semaphore()
    for dz in range(1, n_blk):
        pl.semaphore_signal(barrier, inc=1, device_id={"blk": lax.rem(b + dz, n_blk)}, device_id_type=MESH)
    for dx in range(1, n_det):
        pl.semaphore_signal(barrier, inc=1, device_id={"det": lax.rem(d + dx, n_det)}, device_id_type=MESH)
    pl.semaphore_signal(barrier, inc=1, device_id={"sub": other}, device_id_type=MESH)

    moves = [(tmpl_in, tmpl4.at[pl.ds(b * kb, kb)]), (own_in, data4.at[pl.ds(own * pairs, pairs)]),
             (cuts_in, cuts.at[b]), (first_in, first), (twiddle_in, twiddle), (second_in.at[half], second),
             (tile_dft_in, tile_dft), (row_phase_in, row_phase), (tile_phase_in, tile_phase), (ids_k_in, ids_k),
             (ids_p_in, ids_p), (ids_t_in, ids_t), (ids_k_in, ids_v)]
    fetches = [pltpu.make_async_copy(src, dst, local_sem.at[i]) for i, (src, dst) in enumerate(moves)]
    for copy in fetches:
        copy.start()
    for copy in fetches[:3]:
        copy.wait()
    pl.semaphore_wait(barrier, n_blk + n_det - 1)

    def remote(ref, send, recv, where):
        copy = pltpu.make_async_remote_copy(src_ref=ref, dst_ref=ref, send_sem=send, recv_sem=recv,
                                            device_id=where, device_id_type=MESH)
        copy.start()
        return copy

    def partner(step):
        index = b
        bit = 1
        while bit <= step:
            if step & bit:
                index = index + bit * (1 - 2 * lax.rem(b // bit, 2))
            bit *= 2
        return index

    def data_half(place):
        return data4.at[pl.ds(place * pairs + half * hp, hp)]

    def tmpl_half(place):
        return tmpl4.at[pl.ds(place * kb + half * hk, hk)]

    z_copies, t_copies, c_copies, x_copies, s_copies, ts_copies = {}, {}, {}, {}, {}, {}
    for dz in range(n_blk - 1, 0, -1):
        where = {"blk": partner(dz)}
        t_copies[dz] = remote(tmpl_half(b), tz_send.at[dz], tz_recv.at[dz], where)
        c_copies[dz] = remote(cuts.at[b], cz_send.at[dz], cz_recv.at[dz], where)
    for dz in range(n_blk - 1, 0, -1):
        where = {"blk": partner(dz)}
        z_copies[dz] = remote(data_half(own), z_send.at[dz], z_recv.at[dz], where)
    for dx in range(1, n_det):
        x_copies[0, dx] = remote(data_half(own), x_send.at[0, dx], x_recv.at[0, dx],
                                 {"det": lax.rem(d + dx, n_det)})
    for copy in fetches[3:]:
        copy.wait()

    wide = data4[pl.ds(own * pairs, pairs)].astype(f32)
    twc = jnp.broadcast_to(twiddle[:, :NMIN][None], (pairs, NMAJ, NMIN)).reshape(pairs * NMAJ, NMIN)
    tws = jnp.broadcast_to(twiddle[:, NMIN:][None], (pairs, NMAJ, NMIN)).reshape(pairs * NMAJ, NMIN)
    n_half = second.shape[0] // 2

    def peak_of(src_b, peak):
        def one_template(k, peak):
            row = tmpl4[src_b * kb + k].astype(f32)
            norm = jnp.sum(jnp.sum(row * row, axis=0, keepdims=True), axis=1, keepdims=True)
            norm_tab[src_b * kb + k] = jnp.broadcast_to(norm, (1, NMIN))
            real, imag = conj_product(wide, row[None])
            real = real.reshape(pairs * NMAJ, NMIN).astype(bf16)
            imag = imag.reshape(pairs * NMAJ, NMIN).astype(bf16)
            stacked = jnp.concatenate(
                [jnp.concatenate([real, imag], axis=1), jnp.concatenate([-imag, real], axis=1)], axis=0
            )
            section = jnp.dot(first[...], stacked, preferred_element_type=f32)
            sr, si = section[:, :NMIN], section[:, NMIN:]
            bent = jnp.concatenate([sr * twc - si * tws, sr * tws + si * twc], axis=1).astype(bf16)
            snr = lax.dot_general(second[...], bent, (((1,), (1,)), ((), ())), preferred_element_type=f32)
            power = snr[:n_half] * snr[:n_half] + snr[n_half:] * snr[n_half:]
            return jnp.maximum(peak, power * (1.0 / norm))

        return lax.fori_loop(0, kb, one_template, peak, unroll=True)

    peak = peak_of(b, jnp.zeros((n_half, pairs * NMAJ), f32))
    for dz in range(n_blk - 1, 0, -1):
        t_copies[dz].wait_recv()
        src_b = partner(dz)
        ts_copies[dz] = remote(tmpl_half(src_b), ts_send.at[dz], ts_recv.at[dz], {"sub": other})
    for dz in range(n_blk - 1, 0, -1):
        z_copies[dz].wait_recv()
        src_b = partner(dz)
        block = data_half(src_b * n_det + d)
        for dx in range(1, n_det):
            x_copies[dz, dx] = remote(block, x_send.at[dz, dx], x_recv.at[dz, dx],
                                      {"det": lax.rem(d + dx, n_det)})
        s_copies[dz, 0] = remote(block, s_send.at[dz, 0], s_recv.at[dz, 0], {"sub": other})
        ts_copies[dz].wait_recv()
        peak = peak_of(src_b, peak)

    for copy in c_copies.values():
        copy.wait_recv()

    cut_rows[...] = jnp.zeros(cut_rows.shape, f32)
    cut_rows[:, NCUT - 1:NCUT] = jnp.full((n_tmpl, 1), NMAJ, f32)
    for blk in range(n_blk):
        cut_rows[blk * kb:(blk + 1) * kb, 0:n_cut] = (cuts[blk] >> 7).astype(f32)
        cut_rows[blk * kb:(blk + 1) * kb, 64:64 + n_cut] = (cuts[blk] & (NMIN - 1)).astype(f32)
    is_k = lax.broadcasted_iota(jnp.int32, (n_tmpl, n_trig), 0) == jnp.broadcast_to(ids_v[0], (n_tmpl, n_trig))
    pick_k = is_k.astype(f32).astype(bf16)

    def by_trigger(table):
        return lax.dot_general(pick_k, table, (((0,), (0,)), ((), ())), preferred_element_type=f32)

    trig_cuts = by_trigger(cut_rows[...].astype(bf16))
    rest = 1.0 / norm_tab[...].reshape(n_tmpl, NMIN)
    scale = jnp.zeros((n_trig, NMIN), f32)
    for _ in range(3):
        piece = rest.astype(bf16)
        rest = rest - piece.astype(f32)
        scale = scale + by_trigger(piece)
    rnorm_out[...] = scale

    lane = lax.broadcasted_iota(jnp.int32, (n_trig, NMIN), 1)
    spread = (
        (lax.broadcasted_iota(jnp.int32, (NMIN, 2 * NMIN), 0) < 64)
        == (lax.broadcasted_iota(jnp.int32, (NMIN, 2 * NMIN), 1) < NMIN)
    ).astype(f32).astype(bf16)
    base = ((lax.broadcasted_iota(jnp.int32, (n_trig, NMIN), 0) % GROUP) * NMAJ).astype(f32)
    at = lane.astype(f32)
    last = base
    stacks = ([], [], [])
    for r in range(NCUT):
        mine = jnp.where((lane & 63) == r, trig_cuts, 0.0).astype(bf16)
        wide_cuts = jnp.dot(mine, spread, preferred_element_type=f32)
        row = wide_cuts[:, :NMIN] + base
        low = wide_cuts[:, NMIN:]
        marks = (at == row, jnp.logical_and(at >= last, at < row), at < low)
        last = row
        for stack, mark in zip(stacks, marks):
            stack.append(mark.astype(f32).reshape(n_grp, GROUP, NMIN))
        if r % 2 == 1:
            for stack, out in zip(stacks, (hot_out, between_out, keep_out)):
                both = jnp.concatenate(stack[-2:], axis=1).astype(bf16)
                out[:, (r - 1) * GROUP:(r + 1) * GROUP, :] = both
    for q in range(n_grp):
        spin_out[q] = jnp.dot(hot_out[q], row_phase[...], preferred_element_type=f32)

    def prepare(n, carry):
        k = ids_k[0, 0, n]
        row = tmpl4[k].astype(f32)
        phase = tile_phase[half * (tile_phase.shape[0] // n_sub) + ids_t[0, 0, n]]
        pc, ps = phase[:, :NMIN], phase[:, NMIN:]
        tr, ti = row[:, :NMIN], row[:, NMIN:]
        turned[n, :, :NMIN] = tr * pc + ti * ps
        turned[n, :, NMIN:] = tr * ps - ti * pc
        return carry

    order = [0] + list(range(n_blk - 1, 0, -1))
    bounds = [n_trig * i // n_blk for i in range(n_blk + 1)]
    for turn_at, dz in enumerate(order):
        lax.fori_loop(bounds[turn_at], bounds[turn_at + 1], prepare, 0, unroll=8)
        src_b = partner(dz)
        for dx in range(1, n_det):
            x_copies[dz, dx].wait_recv()
            block = data_half(src_b * n_det + lax.rem(d + n_det - dx, n_det))
            s_copies[dz, dx] = remote(block, s_send.at[dz, dx], s_recv.at[dz, dx], {"sub": other})

    swapped = swap_blocks(jnp.sqrt(peak))
    for u in range(n_half // 8):
        peak_out[:, u * 128:(u + 1) * 128] = swapped[8 * u:8 * u + 8, :]
    for copy in s_copies.values():
        copy.wait_recv()

    def filtered(n, carry):
        rows = data4[ids_p[0, 0, n]].astype(f32)
        dr, di = rows[:, :NMIN], rows[:, NMIN:]
        wr, wi = turned[n, :, :NMIN], turned[n, :, NMIN:]
        z_out[n] = jnp.concatenate([dr * wr - di * wi, dr * wi + di * wr], axis=1).astype(bf16)
        return carry

    lax.fori_loop(0, n_trig, filtered, 0, unroll=16)

    for group in (z_copies, t_copies, c_copies, x_copies, s_copies, ts_copies):
        for copy in group.values():
            copy.wait_send()


def chi_kernel(z_in, hot_in, between_in, keep_in, spin_in, rnorm_in, tile_dft, row_phase, peak_in, peak_out, chi_out):
    f32, bf16 = jnp.float32, jnp.bfloat16
    n_grp = hot_in.shape[0]
    peak_out[...] = peak_in[...]
    at = lax.broadcasted_iota(jnp.int32, (GROUP * NCUT, NMIN), 1)
    row = lax.broadcasted_iota(jnp.int32, (GROUP * NCUT, NMIN), 0)
    step = ((at == row).astype(f32) - (at == row - GROUP).astype(f32)).astype(bf16)
    own_rows = lax.broadcasted_iota(jnp.int32, (2 * GROUP, NMIN), 0)
    whole = (lax.broadcasted_iota(jnp.int32, (2 * GROUP, NMIN), 1) // NMAJ == own_rows).astype(f32).astype(bf16)
    whole = jnp.concatenate([whole, jnp.zeros_like(whole)], axis=1)
    own_turn = row_phase[...].astype(f32)

    def rotate(v, w):
        vr, vi, wr, wi = v[:, :NMIN], v[:, NMIN:], w[:, :NMIN], w[:, NMIN:]
        return jnp.concatenate([vr * wr - vi * wi, vr * wi + vi * wr], axis=1).astype(bf16)

    def one_group(q, carry):
        z = z_in[pl.ds(q * GROUP, GROUP)].reshape(GROUP * NMAJ, 2 * NMIN)
        keep = keep_in[q]
        part = jnp.dot(hot_in[q], z, preferred_element_type=f32).astype(bf16) * jnp.concatenate([keep, keep], axis=1)
        moved = jnp.dot(jnp.concatenate([z, part], axis=0), tile_dft[...], preferred_element_type=f32)
        rows = GROUP * NMAJ
        parts = jnp.concatenate([rotate(moved[:rows], own_turn), rotate(moved[rows:], spin_in[q])], axis=0)
        mix = jnp.concatenate([jnp.concatenate([between_in[q], step], axis=1), whole], axis=0)
        bins = jnp.dot(mix, parts, preferred_element_type=f32)
        br, bi = bins[:rows, :NMIN], bins[:rows, NMIN:]
        energy = jnp.sum((br * br + bi * bi).reshape(NCUT, GROUP, NMIN), axis=0)
        tr, ti = bins[rows:rows + GROUP, :NMIN], bins[rows:rows + GROUP, NMIN:]
        loud = tr * tr + ti * ti
        rnorm = rnorm_in[pl.ds(pl.multiple_of(q * GROUP, GROUP), GROUP), :]
        reduced = jnp.maximum(energy - loud * (1.0 / NCUT), 0.0) * (NCUT / (2.0 * NCUT - 2.0)) * rnorm
        rho = jnp.sqrt(loud * rnorm)
        bend = jnp.exp(jnp.log((1.0 + reduced * reduced * reduced) * 0.5) * (-1.0 / 6.0))
        chi_out[0, 0, pl.ds(pl.multiple_of(q * GROUP, GROUP), GROUP), :] = jnp.where(reduced > 1.0, rho * bend, rho)
        return carry

    lax.fori_loop(0, n_grp, one_group, 0, unroll=8)


def fused(sizes, ids_k, ids_p, ids_t, own, tmpl, cuts, tables):
    n_blk, n_det, n_sub = sizes
    n_tmpl = n_blk * tmpl.shape[0]
    n_trig = ids_k.shape[-1]
    n_grp = n_trig // GROUP
    hbm = pl.BlockSpec(memory_space=pltpu.HBM)
    vmem = pl.BlockSpec(memory_space=pltpu.VMEM)
    dma = pltpu.SemaphoreType.DMA
    f32, bf16 = jnp.float32, jnp.bfloat16
    n_half = tables[2].shape[1] // 2
    peak_shape = (own.shape[0], n_half * NMAJ)
    rows = GROUP * NCUT
    made = [
        (peak_shape, f32),
        ((n_trig, NMAJ, 2 * NMIN), bf16),
        ((n_grp, rows, NMIN), bf16),
        ((n_grp, rows, NMIN), bf16),
        ((n_grp, rows, NMIN), bf16),
        ((n_grp, rows, 2 * NMIN), f32),
        ((n_trig, NMIN), f32),
        (tables[3].shape, tables[3].dtype),
        (tables[4].shape, tables[4].dtype),
    ]
    scratch = [
        pltpu.VMEM((n_blk * n_det * own.shape[0],) + own.shape[1:], own.dtype),
        pltpu.VMEM((n_tmpl,) + tmpl.shape[1:], tmpl.dtype),
        pltpu.VMEM((n_blk,) + cuts.shape, cuts.dtype),
    ]
    scratch += [pltpu.SMEM(ids_k.shape, jnp.int32)] * 3
    scratch += [pltpu.VMEM(ids_k.shape, jnp.int32)]
    for i in (0, 1, 2, 5):
        table = tables[i]
        scratch.append(pltpu.VMEM(table.shape[1:] if i == 2 else table.shape, table.dtype))
    scratch += [
        pltpu.VMEM((n_tmpl, NMIN), f32),
        pltpu.VMEM((n_tmpl, 1, NMIN), f32),
        pltpu.VMEM((n_trig, NMAJ, 2 * NMIN), f32),
        dma((13,)),
        dma((n_blk,)), dma((n_blk,)),
        dma((n_blk, n_det)), dma((n_blk, n_det)),
        dma((n_blk, n_det)), dma((n_blk, n_det)),
        dma((n_blk,)), dma((n_blk,)),
        dma((n_blk,)), dma((n_blk,)),
        dma((n_blk,)), dma((n_blk,)),
    ]
    peak, z, hot, between, keep, spin, rnorm, tile_dft, row_phase = pl.pallas_call(
        functools.partial(gather_kernel, n_blk, n_det, n_sub),
        out_shape=[pltpu.VMEM(shape, dtype) for shape, dtype in made],
        in_specs=[hbm] * 12,
        out_specs=[vmem] * len(made),
        scratch_shapes=scratch,
        compiler_params=pltpu.CompilerParams(
            collective_id=0, has_side_effects=True, vmem_limit_bytes=24 * 1024 * 1024
        ),
        name="gather_and_peak",
    )(ids_k, ids_p, ids_t, own, tmpl, cuts, *tables)
    return pl.pallas_call(
        chi_kernel,
        out_shape=(
            jax.ShapeDtypeStruct(peak_shape, f32),
            jax.ShapeDtypeStruct(ids_k.shape + (STEPS * NMAJ,), f32),
        ),
        in_specs=[vmem] * 9,
        out_specs=(vmem, vmem),
        compiler_params=pltpu.CompilerParams(vmem_limit_bytes=24 * 1024 * 1024),
        name="chi",
    )(z, hot, between, keep, spin, rnorm, tile_dft, row_phase, peak)


def body(sizes, data, templates, bin_cuts, trig_template, trig_pair, trig_tile):
    tables = tuple(jnp.asarray(t) for t in host_tables(sizes[2]))
    peak, chi = fused(sizes, trig_template, trig_pair, trig_tile, data, templates, bin_cuts, tables)
    return peak, chi


def solution(mesh):
    sizes = (mesh.shape["blk"], mesh.shape["det"], mesh.shape["sub"])
    return jax.shard_map(
        functools.partial(body, sizes),
        mesh=mesh,
        in_specs=(
            P(("groups", "blk", "det"), None, None),
            P(("groups", "blk"), None, None),
            P(("groups", "blk"), None),
            P(("groups", "blk", "det"), "sub", None),
            P(("groups", "blk", "det"), "sub", None),
            P(("groups", "blk", "det"), "sub", None),
        ),
        out_specs=(
            P(("groups", "blk", "det"), "sub"),
            P(("groups", "blk", "det"), "sub", None, None),
        ),
        check_vma=False,
    )
```

```python
import functools
import math

import jax
import jax.numpy as jnp
import numpy as np
from jax import lax
from jax.experimental import pallas as pl
from jax.experimental.pallas import tpu as pltpu
from jax.sharding import PartitionSpec as P

MESH = pl.DeviceIdType.MESH
NMAJ = 16
NMIN = 128
NCUT = 16
STEPS = 8
GROUP = 8


def unit_circle(index, period):
    angle = (index % period) * (2.0 * math.pi / period)
    return np.cos(angle), np.sin(angle)


def host_tables(n_sub):
    bf16 = jnp.bfloat16
    major = np.arange(NMAJ)
    minor = np.arange(NMIN)
    cos16, sin16 = unit_circle(major[:, None] * major[None, :], NMAJ)
    eye = np.eye(GROUP)
    first = np.concatenate([np.kron(eye, cos16), np.kron(eye, sin16)], axis=1).astype(bf16)
    twc, tws = unit_circle(major[:, None] * minor[None, :], NMAJ * NMIN)
    twiddle = np.concatenate([twc, tws], axis=1).astype(np.float32)
    n_half = NMIN // n_sub
    second = []
    for half in range(n_sub):
        steps = half * n_half + np.arange(n_half)
        cosine, sine = unit_circle(steps[:, None] * minor[None, :], NMIN)
        real_rows = np.concatenate([cosine, -sine], axis=1)
        imag_rows = np.concatenate([sine, cosine], axis=1)
        second.append(np.concatenate([real_rows, imag_rows], axis=0))
    second = np.stack(second).astype(bf16)
    times = np.arange(NMAJ * STEPS)
    cosine, sine = unit_circle(minor[:, None] * times[None, :], NMAJ * NMIN)
    tile_dft = np.concatenate(
        [np.concatenate([cosine, sine], axis=1), np.concatenate([-sine, cosine], axis=1)], axis=0
    ).astype(bf16)
    rowc, rows = unit_circle(major[:, None] * (times % NMAJ)[None, :], NMAJ)
    row_phase = np.tile(np.concatenate([rowc, rows], axis=1), (GROUP, 1)).astype(bf16)
    starts = np.arange(NMIN // STEPS) * STEPS
    phc, phs = unit_circle(starts[:, None] * minor[None, :], NMIN)
    tile_phase = np.concatenate([phc, phs], axis=1).astype(np.float32)[:, None, :]
    return first, twiddle, second, tile_dft, row_phase, tile_phase


def swap_blocks(x):
    sub = lax.broadcasted_iota(jnp.int32, x.shape, 0)
    grp = lax.broadcasted_iota(jnp.int32, x.shape, 1) // NMAJ
    rows, lanes = x.shape
    for bit in (1, 2, 4):
        up = pltpu.roll(pltpu.roll(x, rows - bit, 0), NMAJ * bit, 1)
        down = pltpu.roll(pltpu.roll(x, bit, 0), lanes - NMAJ * bit, 1)
        sb, gb = (sub & bit) != 0, (grp & bit) != 0
        x = jnp.where(jnp.logical_and(jnp.logical_not(sb), gb), up,
                      jnp.where(jnp.logical_and(sb, jnp.logical_not(gb)), down, x))
    return x


def conj_product(data, tmpl):
    dr, di = data[..., :NMIN], data[..., NMIN:]
    tr, ti = tmpl[..., :NMIN], tmpl[..., NMIN:]
    return dr * tr + di * ti, di * tr - dr * ti


def gather_kernel(n_blk, n_det, n_sub, *refs):
    (ids_k_in, ids_p_in, ids_t_in, own_in, tmpl_in, cuts_in, first_in, twiddle_in, second_in, tile_dft_in,
     row_phase_in, tile_phase_in, peak_out, z_out, hot_out, between_out, keep_out, spin_out, rnorm_out,
     tile_dft, row_phase, data4, tmpl4, cuts, ids_k, ids_p, ids_t, ids_v, first, twiddle, second, tile_phase,
     cut_rows, norm_tab, turned,
     local_sem, z_send, z_recv, x_send, x_recv, s_send, s_recv, tz_send, tz_recv, ts_send, ts_recv,
     cz_send, cz_recv) = refs
    f32, bf16 = jnp.float32, jnp.bfloat16
    b = lax.axis_index("blk")
    d = lax.axis_index("det")
    half = lax.axis_index("sub")
    other = n_sub - 1 - half
    pairs = own_in.shape[0]
    kb = tmpl_in.shape[0]
    n_cut = cuts_in.shape[1]
    n_tmpl = n_blk * kb
    n_trig = ids_k_in.shape[2]
    n_grp = n_trig // GROUP
    hp, hk = pairs // n_sub, kb // n_sub
    own = b * n_det + d

    barrier = pltpu.get_barrier_semaphore()
    for dz in range(1, n_blk):
        pl.semaphore_signal(barrier, inc=1, device_id={"blk": lax.rem(b + dz, n_blk)}, device_id_type=MESH)
    for dx in range(1, n_det):
        pl.semaphore_signal(barrier, inc=1, device_id={"det": lax.rem(d + dx, n_det)}, device_id_type=MESH)
    pl.semaphore_signal(barrier, inc=1, device_id={"sub": other}, device_id_type=MESH)

    moves = [(tmpl_in, tmpl4.at[pl.ds(b * kb, kb)]), (own_in, data4.at[pl.ds(own * pairs, pairs)]),
             (cuts_in, cuts.at[b]), (first_in, first), (twiddle_in, twiddle), (second_in.at[half], second),
             (tile_dft_in, tile_dft), (row_phase_in, row_phase), (tile_phase_in, tile_phase), (ids_k_in, ids_k),
             (ids_p_in, ids_p), (ids_t_in, ids_t), (ids_k_in, ids_v)]
    fetches = [pltpu.make_async_copy(src, dst, local_sem.at[i]) for i, (src, dst) in enumerate(moves)]
    for copy in fetches:
        copy.start()
    for copy in fetches[:3]:
        copy.wait()
    pl.semaphore_wait(barrier, n_blk + n_det - 1)

    def remote(ref, send, recv, where):
        copy = pltpu.make_async_remote_copy(src_ref=ref, dst_ref=ref, send_sem=send, recv_sem=recv,
                                            device_id=where, device_id_type=MESH)
        copy.start()
        return copy

    def partner(step):
        index = b
        bit = 1
        while bit <= step:
            if step & bit:
                index = index + bit * (1 - 2 * lax.rem(b // bit, 2))
            bit *= 2
        return index

    def data_half(place):
        return data4.at[pl.ds(place * pairs + half * hp, hp)]

    def tmpl_half(place):
        return tmpl4.at[pl.ds(place * kb + half * hk, hk)]

    z_copies, t_copies, c_copies, x_copies, s_copies, ts_copies = {}, {}, {}, {}, {}, {}
    for dz in range(n_blk - 1, 0, -1):
        where = {"blk": partner(dz)}
        t_copies[dz] = remote(tmpl_half(b), tz_send.at[dz], tz_recv.at[dz], where)
        c_copies[dz] = remote(cuts.at[b], cz_send.at[dz], cz_recv.at[dz], where)
    for dz in range(n_blk - 1, 0, -1):
        where = {"blk": partner(dz)}
        z_copies[dz] = remote(data_half(own), z_send.at[dz], z_recv.at[dz], where)
    for dx in range(1, n_det):
        x_copies[0, dx] = remote(data_half(own), x_send.at[0, dx], x_recv.at[0, dx],
                                 {"det": lax.rem(d + dx, n_det)})
    for copy in fetches[3:]:
        copy.wait()

    wide = data4[pl.ds(own * pairs, pairs)].astype(f32)
    twc = jnp.broadcast_to(twiddle[:, :NMIN][None], (pairs, NMAJ, NMIN)).reshape(pairs * NMAJ, NMIN)
    tws = jnp.broadcast_to(twiddle[:, NMIN:][None], (pairs, NMAJ, NMIN)).reshape(pairs * NMAJ, NMIN)
    n_half = second.shape[0] // 2

    def peak_of(src_b, peak):
        def one_template(k, peak):
            row = tmpl4[src_b * kb + k].astype(f32)
            norm = jnp.sum(jnp.sum(row * row, axis=0, keepdims=True), axis=1, keepdims=True)
            norm_tab[src_b * kb + k] = jnp.broadcast_to(norm, (1, NMIN))
            real, imag = conj_product(wide, row[None])
            real = real.reshape(pairs * NMAJ, NMIN).astype(bf16)
            imag = imag.reshape(pairs * NMAJ, NMIN).astype(bf16)
            stacked = jnp.concatenate(
                [jnp.concatenate([real, imag], axis=1), jnp.concatenate([-imag, real], axis=1)], axis=0
            )
            section = jnp.dot(first[...], stacked, preferred_element_type=f32)
            sr, si = section[:, :NMIN], section[:, NMIN:]
            bent = jnp.concatenate([sr * twc - si * tws, sr * tws + si * twc], axis=1).astype(bf16)
            snr = lax.dot_general(second[...], bent, (((1,), (1,)), ((), ())), preferred_element_type=f32)
            power = snr[:n_half] * snr[:n_half] + snr[n_half:] * snr[n_half:]
            return jnp.maximum(peak, power * (1.0 / norm))

        return lax.fori_loop(0, kb, one_template, peak, unroll=True)

    peak = peak_of(b, jnp.zeros((n_half, pairs * NMAJ), f32))
    for dz in range(n_blk - 1, 0, -1):
        t_copies[dz].wait_recv()
        src_b = partner(dz)
        ts_copies[dz] = remote(tmpl_half(src_b), ts_send.at[dz], ts_recv.at[dz], {"sub": other})
    for dz in range(n_blk - 1, 0, -1):
        z_copies[dz].wait_recv()
        src_b = partner(dz)
        block = data_half(src_b * n_det + d)
        for dx in range(1, n_det):
            x_copies[dz, dx] = remote(block, x_send.at[dz, dx], x_recv.at[dz, dx],
                                      {"det": lax.rem(d + dx, n_det)})
        s_copies[dz, 0] = remote(block, s_send.at[dz, 0], s_recv.at[dz, 0], {"sub": other})
        ts_copies[dz].wait_recv()
        peak = peak_of(src_b, peak)

    for copy in c_copies.values():
        copy.wait_recv()

    cut_rows[...] = jnp.zeros(cut_rows.shape, f32)
    cut_rows[:, NCUT - 1:NCUT] = jnp.full((n_tmpl, 1), NMAJ, f32)
    for blk in range(n_blk):
        cut_rows[blk * kb:(blk + 1) * kb, 0:n_cut] = (cuts[blk] >> 7).astype(f32)
        cut_rows[blk * kb:(blk + 1) * kb, 64:64 + n_cut] = (cuts[blk] & (NMIN - 1)).astype(f32)
    is_k = lax.broadcasted_iota(jnp.int32, (n_tmpl, n_trig), 0) == jnp.broadcast_to(ids_v[0], (n_tmpl, n_trig))
    pick_k = is_k.astype(f32).astype(bf16)

    def by_trigger(table):
        return lax.dot_general(pick_k, table, (((0,), (0,)), ((), ())), preferred_element_type=f32)

    trig_cuts = by_trigger(cut_rows[...].astype(bf16))
    rest = 1.0 / norm_tab[...].reshape(n_tmpl, NMIN)
    scale = jnp.zeros((n_trig, NMIN), f32)
    for _ in range(3):
        piece = rest.astype(bf16)
        rest = rest - piece.astype(f32)
        scale = scale + by_trigger(piece)
    rnorm_out[...] = scale

    lane = lax.broadcasted_iota(jnp.int32, (n_trig, NMIN), 1)
    spread = (
        (lax.broadcasted_iota(jnp.int32, (NMIN, 2 * NMIN), 0) < 64)
        == (lax.broadcasted_iota(jnp.int32, (NMIN, 2 * NMIN), 1) < NMIN)
    ).astype(f32).astype(bf16)
    base = ((lax.broadcasted_iota(jnp.int32, (n_trig, NMIN), 0) % GROUP) * NMAJ).astype(f32)
    at = lane.astype(f32)
    last = base
    stacks = ([], [], [])
    for r in range(NCUT):
        mine = jnp.where((lane & 63) == r, trig_cuts, 0.0).astype(bf16)
        wide_cuts = jnp.dot(mine, spread, preferred_element_type=f32)
        row = wide_cuts[:, :NMIN] + base
        low = wide_cuts[:, NMIN:]
        marks = (at == row, jnp.logical_and(at >= last, at < row), at < low)
        last = row
        for stack, mark in zip(stacks, marks):
            stack.append(mark.astype(f32).reshape(n_grp, GROUP, NMIN))
        if r % 2 == 1:
            for stack, out in zip(stacks, (hot_out, between_out, keep_out)):
                both = jnp.concatenate(stack[-2:], axis=1).astype(bf16)
                out[:, (r - 1) * GROUP:(r + 1) * GROUP, :] = both
    for q in range(n_grp):
        spin_out[q] = jnp.dot(hot_out[q], row_phase[...], preferred_element_type=f32)

    def prepare(n, carry):
        k = ids_k[0, 0, n]
        row = tmpl4[k].astype(f32)
        phase = tile_phase[half * (tile_phase.shape[0] // n_sub) + ids_t[0, 0, n]]
        pc, ps = phase[:, :NMIN], phase[:, NMIN:]
        tr, ti = row[:, :NMIN], row[:, NMIN:]
        turned[n, :, :NMIN] = tr * pc + ti * ps
        turned[n, :, NMIN:] = tr * ps - ti * pc
        return carry

    order = [0] + list(range(n_blk - 1, 0, -1))
    bounds = [n_trig * i // n_blk for i in range(n_blk + 1)]
    for turn_at, dz in enumerate(order):
        lax.fori_loop(bounds[turn_at], bounds[turn_at + 1], prepare, 0, unroll=8)
        src_b = partner(dz)
        for dx in range(1, n_det):
            x_copies[dz, dx].wait_recv()
            block = data_half(src_b * n_det + lax.rem(d + n_det - dx, n_det))
            s_copies[dz, dx] = remote(block, s_send.at[dz, dx], s_recv.at[dz, dx], {"sub": other})

    swapped = swap_blocks(jnp.sqrt(peak))
    for u in range(n_half // 8):
        peak_out[:, u * 128:(u + 1) * 128] = swapped[8 * u:8 * u + 8, :]
    for copy in s_copies.values():
        copy.wait_recv()

    def filtered(n, carry):
        rows = data4[ids_p[0, 0, n]].astype(f32)
        dr, di = rows[:, :NMIN], rows[:, NMIN:]
        wr, wi = turned[n, :, :NMIN], turned[n, :, NMIN:]
        z_out[n] = jnp.concatenate([dr * wr - di * wi, dr * wi + di * wr], axis=1).astype(bf16)
        return carry

    lax.fori_loop(0, n_trig, filtered, 0, unroll=16)

    for group in (z_copies, t_copies, c_copies, x_copies, s_copies, ts_copies):
        for copy in group.values():
            copy.wait_send()


def chi_kernel(z_in, hot_in, between_in, keep_in, spin_in, rnorm_in, tile_dft, row_phase, peak_in, peak_out, chi_out):
    f32, bf16 = jnp.float32, jnp.bfloat16
    n_grp = hot_in.shape[0]
    peak_out[...] = peak_in[...]
    at = lax.broadcasted_iota(jnp.int32, (GROUP * NCUT, NMIN), 1)
    row = lax.broadcasted_iota(jnp.int32, (GROUP * NCUT, NMIN), 0)
    step = ((at == row).astype(f32) - (at == row - GROUP).astype(f32)).astype(bf16)
    own_rows = lax.broadcasted_iota(jnp.int32, (2 * GROUP, NMIN), 0)
    whole = (lax.broadcasted_iota(jnp.int32, (2 * GROUP, NMIN), 1) // NMAJ == own_rows).astype(f32).astype(bf16)
    whole = jnp.concatenate([whole, jnp.zeros_like(whole)], axis=1)
    own_turn = row_phase[...].astype(f32)

    def rotate(v, w):
        vr, vi, wr, wi = v[:, :NMIN], v[:, NMIN:], w[:, :NMIN], w[:, NMIN:]
        return jnp.concatenate([vr * wr - vi * wi, vr * wi + vi * wr], axis=1).astype(bf16)

    def one_group(q, carry):
        z = z_in[pl.ds(q * GROUP, GROUP)].reshape(GROUP * NMAJ, 2 * NMIN)
        keep = keep_in[q]
        part = jnp.dot(hot_in[q], z, preferred_element_type=f32).astype(bf16) * jnp.concatenate([keep, keep], axis=1)
        moved = jnp.dot(jnp.concatenate([z, part], axis=0), tile_dft[...], preferred_element_type=f32)
        rows = GROUP * NMAJ
        parts = jnp.concatenate([rotate(moved[:rows], own_turn), rotate(moved[rows:], spin_in[q])], axis=0)
        mix = jnp.concatenate([jnp.concatenate([between_in[q], step], axis=1), whole], axis=0)
        bins = jnp.dot(mix, parts, preferred_element_type=f32)
        br, bi = bins[:rows, :NMIN], bins[:rows, NMIN:]
        energy = jnp.sum((br * br + bi * bi).reshape(NCUT, GROUP, NMIN), axis=0)
        tr, ti = bins[rows:rows + GROUP, :NMIN], bins[rows:rows + GROUP, NMIN:]
        loud = tr * tr + ti * ti
        rnorm = rnorm_in[pl.ds(pl.multiple_of(q * GROUP, GROUP), GROUP), :]
        reduced = jnp.maximum(energy - loud * (1.0 / NCUT), 0.0) * (NCUT / (2.0 * NCUT - 2.0)) * rnorm
        rho = jnp.sqrt(loud * rnorm)
        bend = jnp.exp(jnp.log((1.0 + reduced * reduced * reduced) * 0.5) * (-1.0 / 6.0))
        chi_out[0, 0, pl.ds(pl.multiple_of(q * GROUP, GROUP), GROUP), :] = jnp.where(reduced > 1.0, rho * bend, rho)
        return carry

    lax.fori_loop(0, n_grp, one_group, 0, unroll=8)


def fused(sizes, ids_k, ids_p, ids_t, own, tmpl, cuts, tables):
    n_blk, n_det, n_sub = sizes
    n_tmpl = n_blk * tmpl.shape[0]
    n_trig = ids_k.shape[-1]
    n_grp = n_trig // GROUP
    hbm = pl.BlockSpec(memory_space=pltpu.HBM)
    vmem = pl.BlockSpec(memory_space=pltpu.VMEM)
    dma = pltpu.SemaphoreType.DMA
    f32, bf16 = jnp.float32, jnp.bfloat16
    n_half = tables[2].shape[1] // 2
    peak_shape = (own.shape[0], n_half * NMAJ)
    rows = GROUP * NCUT
    made = [
        (peak_shape, f32),
        ((n_trig, NMAJ, 2 * NMIN), bf16),
        ((n_grp, rows, NMIN), bf16),
        ((n_grp, rows, NMIN), bf16),
        ((n_grp, rows, NMIN), bf16),
        ((n_grp, rows, 2 * NMIN), f32),
        ((n_trig, NMIN), f32),
        (tables[3].shape, tables[3].dtype),
        (tables[4].shape, tables[4].dtype),
    ]
    scratch = [
        pltpu.VMEM((n_blk * n_det * own.shape[0],) + own.shape[1:], own.dtype),
        pltpu.VMEM((n_tmpl,) + tmpl.shape[1:], tmpl.dtype),
        pltpu.VMEM((n_blk,) + cuts.shape, cuts.dtype),
    ]
    scratch += [pltpu.SMEM(ids_k.shape, jnp.int32)] * 3
    scratch += [pltpu.VMEM(ids_k.shape, jnp.int32)]
    for i in (0, 1, 2, 5):
        table = tables[i]
        scratch.append(pltpu.VMEM(table.shape[1:] if i == 2 else table.shape, table.dtype))
    scratch += [
        pltpu.VMEM((n_tmpl, NMIN), f32),
        pltpu.VMEM((n_tmpl, 1, NMIN), f32),
        pltpu.VMEM((n_trig, NMAJ, 2 * NMIN), f32),
        dma((13,)),
        dma((n_blk,)), dma((n_blk,)),
        dma((n_blk, n_det)), dma((n_blk, n_det)),
        dma((n_blk, n_det)), dma((n_blk, n_det)),
        dma((n_blk,)), dma((n_blk,)),
        dma((n_blk,)), dma((n_blk,)),
        dma((n_blk,)), dma((n_blk,)),
    ]
    peak, z, hot, between, keep, spin, rnorm, tile_dft, row_phase = pl.pallas_call(
        functools.partial(gather_kernel, n_blk, n_det, n_sub),
        out_shape=[pltpu.VMEM(shape, dtype) for shape, dtype in made],
        in_specs=[hbm] * 12,
        out_specs=[vmem] * len(made),
        scratch_shapes=scratch,
        compiler_params=pltpu.CompilerParams(
            collective_id=0, has_side_effects=True, vmem_limit_bytes=24 * 1024 * 1024
        ),
        name="gather_and_peak",
    )(*(pltpu.with_memory_space_constraint(x, pltpu.HBM) for x in (ids_k, ids_p, ids_t, own, tmpl, cuts, *tables)))
    return pl.pallas_call(
        chi_kernel,
        out_shape=(
            jax.ShapeDtypeStruct(peak_shape, f32),
            jax.ShapeDtypeStruct(ids_k.shape + (STEPS * NMAJ,), f32),
        ),
        in_specs=[vmem] * 9,
        out_specs=(vmem, vmem),
        compiler_params=pltpu.CompilerParams(vmem_limit_bytes=24 * 1024 * 1024),
        name="chi",
    )(z, hot, between, keep, spin, rnorm, tile_dft, row_phase, peak)


def body(sizes, data, templates, bin_cuts, trig_template, trig_pair, trig_tile):
    tables = tuple(jnp.asarray(t) for t in host_tables(sizes[2]))
    peak, chi = fused(sizes, trig_template, trig_pair, trig_tile, data, templates, bin_cuts, tables)
    return peak, chi


def solution(mesh):
    sizes = (mesh.shape["blk"], mesh.shape["det"], mesh.shape["sub"])
    return jax.shard_map(
        functools.partial(body, sizes),
        mesh=mesh,
        in_specs=(
            P(("groups", "blk", "det"), None, None),
            P(("groups", "blk"), None, None),
            P(("groups", "blk"), None),
            P(("groups", "blk", "det"), "sub", None),
            P(("groups", "blk", "det"), "sub", None),
            P(("groups", "blk", "det"), "sub", None),
        ),
        out_specs=(
            P(("groups", "blk", "det"), "sub"),
            P(("groups", "blk", "det"), "sub", None, None),
        ),
        check_vma=False,
    )
```

```python
import functools
import math

import jax
import jax.numpy as jnp
import numpy as np
from jax import lax
from jax.experimental import pallas as pl
from jax.experimental.pallas import tpu as pltpu
from jax.sharding import PartitionSpec as P

MESH = pl.DeviceIdType.MESH
NMAJ = 16
NMIN = 128
NCUT = 16
STEPS = 8
GROUP = 8
BATCH = 8


def unit_circle(index, period):
    angle = (index % period) * (2.0 * math.pi / period)
    return np.cos(angle), np.sin(angle)


def host_tables(n_sub):
    bf16 = jnp.bfloat16
    major = np.arange(NMAJ)
    minor = np.arange(NMIN)
    cos16, sin16 = unit_circle(major[:, None] * major[None, :], NMAJ)
    eye = np.eye(GROUP)
    first = np.concatenate([np.kron(eye, cos16), np.kron(eye, sin16)], axis=1).astype(bf16)
    twc, tws = unit_circle(major[:, None] * minor[None, :], NMAJ * NMIN)
    twiddle = np.concatenate([twc, tws], axis=1).astype(np.float32)
    n_half = NMIN // n_sub
    second = []
    for half in range(n_sub):
        steps = half * n_half + np.arange(n_half)
        cosine, sine = unit_circle(steps[:, None] * minor[None, :], NMIN)
        real_rows = np.concatenate([cosine, -sine], axis=1)
        imag_rows = np.concatenate([sine, cosine], axis=1)
        second.append(np.concatenate([real_rows, imag_rows], axis=0))
    second = np.stack(second).astype(bf16)
    times = np.arange(NMAJ * STEPS)
    cosine, sine = unit_circle(minor[:, None] * times[None, :], NMAJ * NMIN)
    tile_dft = np.concatenate(
        [np.concatenate([cosine, sine], axis=1), np.concatenate([-sine, cosine], axis=1)], axis=0
    ).astype(bf16)
    rowc, rows = unit_circle(major[:, None] * (times % NMAJ)[None, :], NMAJ)
    row_phase = np.tile(np.concatenate([rowc, rows], axis=1), (GROUP, 1)).astype(bf16)
    starts = np.arange(NMIN // STEPS) * STEPS
    phc, phs = unit_circle(starts[:, None] * minor[None, :], NMIN)
    tile_phase = np.concatenate([phc, phs], axis=1).astype(np.float32)[:, None, :]
    return first, twiddle, second, tile_dft, row_phase, tile_phase


def swap_blocks(x):
    sub = lax.broadcasted_iota(jnp.int32, x.shape, 0)
    grp = lax.broadcasted_iota(jnp.int32, x.shape, 1) // NMAJ
    rows, lanes = x.shape
    for bit in (1, 2, 4):
        up = pltpu.roll(pltpu.roll(x, rows - bit, 0), NMAJ * bit, 1)
        down = pltpu.roll(pltpu.roll(x, bit, 0), lanes - NMAJ * bit, 1)
        sb, gb = (sub & bit) != 0, (grp & bit) != 0
        x = jnp.where(jnp.logical_and(jnp.logical_not(sb), gb), up,
                      jnp.where(jnp.logical_and(sb, jnp.logical_not(gb)), down, x))
    return x


def conj_product(data, tmpl):
    dr, di = data[..., :NMIN], data[..., NMIN:]
    tr, ti = tmpl[..., :NMIN], tmpl[..., NMIN:]
    return dr * tr + di * ti, di * tr - dr * ti


def gather_kernel(n_blk, n_det, n_sub, *refs):
    (ids_k_in, ids_p_in, ids_t_in, own_in, tmpl_in, cuts_in, first_in, twiddle_in, second_in, tile_dft_in,
     row_phase_in, tile_phase_in, peak_out, z_out, hot_out, between_out, keep_out, spin_out, rnorm_out,
     tile_dft, row_phase, data4, tmpl4, cuts, ids_k, ids_p, ids_t, ids_v, first, twiddle, second, tile_phase,
     cut_rows, norm_tab, turned,
     local_sem, z_send, z_recv, x_send, x_recv, s_send, s_recv, tz_send, tz_recv, ts_send, ts_recv,
     cz_send, cz_recv) = refs
    f32, bf16 = jnp.float32, jnp.bfloat16
    b = lax.axis_index("blk")
    d = lax.axis_index("det")
    half = lax.axis_index("sub")
    other = n_sub - 1 - half
    pairs = own_in.shape[0]
    kb = tmpl_in.shape[0]
    n_cut = cuts_in.shape[1]
    n_tmpl = n_blk * kb
    n_trig = ids_k_in.shape[2]
    n_grp = n_trig // GROUP
    hp, hk = pairs // n_sub, kb // n_sub
    own = b * n_det + d

    barrier = pltpu.get_barrier_semaphore()
    for dz in range(1, n_blk):
        pl.semaphore_signal(barrier, inc=1, device_id={"blk": lax.rem(b + dz, n_blk)}, device_id_type=MESH)
    for dx in range(1, n_det):
        pl.semaphore_signal(barrier, inc=1, device_id={"det": lax.rem(d + dx, n_det)}, device_id_type=MESH)
    pl.semaphore_signal(barrier, inc=1, device_id={"sub": other}, device_id_type=MESH)

    moves = [(tmpl_in, tmpl4.at[pl.ds(b * kb, kb)]), (own_in, data4.at[pl.ds(own * pairs, pairs)]),
             (cuts_in, cuts.at[b]), (first_in, first), (twiddle_in, twiddle), (second_in.at[half], second),
             (tile_dft_in, tile_dft), (row_phase_in, row_phase), (tile_phase_in, tile_phase), (ids_k_in, ids_k),
             (ids_p_in, ids_p), (ids_t_in, ids_t), (ids_k_in, ids_v)]
    fetches = [pltpu.make_async_copy(src, dst, local_sem.at[i]) for i, (src, dst) in enumerate(moves)]
    for copy in fetches:
        copy.start()
    for copy in fetches[:3]:
        copy.wait()
    pl.semaphore_wait(barrier, n_blk + n_det - 1)

    def remote(ref, send, recv, where):
        copy = pltpu.make_async_remote_copy(src_ref=ref, dst_ref=ref, send_sem=send, recv_sem=recv,
                                            device_id=where, device_id_type=MESH)
        copy.start()
        return copy

    def partner(step):
        index = b
        bit = 1
        while bit <= step:
            if step & bit:
                index = index + bit * (1 - 2 * lax.rem(b // bit, 2))
            bit *= 2
        return index

    def data_half(place):
        return data4.at[pl.ds(place * pairs + half * hp, hp)]

    def tmpl_half(place):
        return tmpl4.at[pl.ds(place * kb + half * hk, hk)]

    z_copies, t_copies, c_copies, x_copies, s_copies, ts_copies = {}, {}, {}, {}, {}, {}
    for dz in range(n_blk - 1, 0, -1):
        where = {"blk": partner(dz)}
        t_copies[dz] = remote(tmpl_half(b), tz_send.at[dz], tz_recv.at[dz], where)
        c_copies[dz] = remote(cuts.at[b], cz_send.at[dz], cz_recv.at[dz], where)
    for dz in range(n_blk - 1, 0, -1):
        where = {"blk": partner(dz)}
        z_copies[dz] = remote(data_half(own), z_send.at[dz], z_recv.at[dz], where)
    for dx in range(1, n_det):
        x_copies[0, dx] = remote(data_half(own), x_send.at[0, dx], x_recv.at[0, dx],
                                 {"det": lax.rem(d + dx, n_det)})
    for copy in fetches[3:]:
        copy.wait()

    wide = data4[pl.ds(own * pairs, pairs)].astype(f32)
    twc = jnp.broadcast_to(twiddle[:, :NMIN][None], (pairs, NMAJ, NMIN)).reshape(pairs * NMAJ, NMIN)
    tws = jnp.broadcast_to(twiddle[:, NMIN:][None], (pairs, NMAJ, NMIN)).reshape(pairs * NMAJ, NMIN)
    n_half = second.shape[0] // 2

    def peak_of(src_b, peak):
        def one_template(k, peak):
            row = tmpl4[src_b * kb + k].astype(f32)
            norm = jnp.sum(jnp.sum(row * row, axis=0, keepdims=True), axis=1, keepdims=True)
            norm_tab[src_b * kb + k] = jnp.broadcast_to(norm, (1, NMIN))
            real, imag = conj_product(wide, row[None])
            real = real.reshape(pairs * NMAJ, NMIN).astype(bf16)
            imag = imag.reshape(pairs * NMAJ, NMIN).astype(bf16)
            stacked = jnp.concatenate(
                [jnp.concatenate([real, imag], axis=1), jnp.concatenate([-imag, real], axis=1)], axis=0
            )
            section = jnp.dot(first[...], stacked, preferred_element_type=f32)
            sr, si = section[:, :NMIN], section[:, NMIN:]
            bent = jnp.concatenate([sr * twc - si * tws, sr * tws + si * twc], axis=1).astype(bf16)
            snr = lax.dot_general(second[...], bent, (((1,), (1,)), ((), ())), preferred_element_type=f32)
            power = snr[:n_half] * snr[:n_half] + snr[n_half:] * snr[n_half:]
            return jnp.maximum(peak, power * (1.0 / norm))

        return lax.fori_loop(0, kb, one_template, peak, unroll=True)

    peak = peak_of(b, jnp.zeros((n_half, pairs * NMAJ), f32))
    for dz in range(n_blk - 1, 0, -1):
        t_copies[dz].wait_recv()
        src_b = partner(dz)
        ts_copies[dz] = remote(tmpl_half(src_b), ts_send.at[dz], ts_recv.at[dz], {"sub": other})
    for dz in range(n_blk - 1, 0, -1):
        z_copies[dz].wait_recv()
        src_b = partner(dz)
        block = data_half(src_b * n_det + d)
        for dx in range(1, n_det):
            x_copies[dz, dx] = remote(block, x_send.at[dz, dx], x_recv.at[dz, dx],
                                      {"det": lax.rem(d + dx, n_det)})
        s_copies[dz, 0] = remote(block, s_send.at[dz, 0], s_recv.at[dz, 0], {"sub": other})
        ts_copies[dz].wait_recv()
        peak = peak_of(src_b, peak)

    for copy in c_copies.values():
        copy.wait_recv()

    cut_rows[...] = jnp.zeros(cut_rows.shape, f32)
    cut_rows[:, NCUT - 1:NCUT] = jnp.full((n_tmpl, 1), NMAJ, f32)
    for blk in range(n_blk):
        cut_rows[blk * kb:(blk + 1) * kb, 0:n_cut] = (cuts[blk] >> 7).astype(f32)
        cut_rows[blk * kb:(blk + 1) * kb, 64:64 + n_cut] = (cuts[blk] & (NMIN - 1)).astype(f32)
    is_k = lax.broadcasted_iota(jnp.int32, (n_tmpl, n_trig), 0) == jnp.broadcast_to(ids_v[0], (n_tmpl, n_trig))
    pick_k = is_k.astype(f32).astype(bf16)

    def by_trigger(table):
        return lax.dot_general(pick_k, table, (((0,), (0,)), ((), ())), preferred_element_type=f32)

    trig_cuts = by_trigger(cut_rows[...].astype(bf16))
    rest = 1.0 / norm_tab[...].reshape(n_tmpl, NMIN)
    scale = jnp.zeros((n_trig, NMIN), f32)
    for _ in range(3):
        piece = rest.astype(bf16)
        rest = rest - piece.astype(f32)
        scale = scale + by_trigger(piece)
    rnorm_out[...] = scale

    lane = lax.broadcasted_iota(jnp.int32, (n_trig, NMIN), 1)
    spread = (
        (lax.broadcasted_iota(jnp.int32, (NMIN, 2 * NMIN), 0) < 64)
        == (lax.broadcasted_iota(jnp.int32, (NMIN, 2 * NMIN), 1) < NMIN)
    ).astype(f32).astype(bf16)
    base = ((lax.broadcasted_iota(jnp.int32, (n_trig, NMIN), 0) % GROUP) * NMAJ).astype(f32)
    at = lane.astype(f32)
    last = base
    stacks = ([], [], [])
    for r in range(NCUT):
        mine = jnp.where((lane & 63) == r, trig_cuts, 0.0).astype(bf16)
        wide_cuts = jnp.dot(mine, spread, preferred_element_type=f32)
        row = wide_cuts[:, :NMIN] + base
        low = wide_cuts[:, NMIN:]
        marks = (at == row, jnp.logical_and(at >= last, at < row), at < low)
        last = row
        for stack, mark in zip(stacks, marks):
            stack.append(mark.astype(f32).reshape(n_grp, GROUP, NMIN))
        if r % 2 == 1:
            for stack, out in zip(stacks, (hot_out, between_out, keep_out)):
                both = jnp.concatenate(stack[-2:], axis=1).astype(bf16)
                out[:, (r - 1) * GROUP:(r + 1) * GROUP, :] = both
    for q in range(n_grp):
        spin_out[q] = jnp.dot(hot_out[q], row_phase[...], preferred_element_type=f32)

    def prepare(n, carry):
        k = ids_k[0, 0, n]
        row = tmpl4[k].astype(f32)
        phase = tile_phase[half * (tile_phase.shape[0] // n_sub) + ids_t[0, 0, n]]
        pc, ps = phase[:, :NMIN], phase[:, NMIN:]
        tr, ti = row[:, :NMIN], row[:, NMIN:]
        turned[n, :, :NMIN] = tr * pc + ti * ps
        turned[n, :, NMIN:] = tr * ps - ti * pc
        return carry

    order = [0] + list(range(n_blk - 1, 0, -1))
    bounds = [n_trig * i // n_blk for i in range(n_blk + 1)]
    for turn_at, dz in enumerate(order):
        lax.fori_loop(bounds[turn_at], bounds[turn_at + 1], prepare, 0, unroll=8)
        src_b = partner(dz)
        for dx in range(1, n_det):
            x_copies[dz, dx].wait_recv()
            block = data_half(src_b * n_det + lax.rem(d + n_det - dx, n_det))
            s_copies[dz, dx] = remote(block, s_send.at[dz, dx], s_recv.at[dz, dx], {"sub": other})

    swapped = swap_blocks(jnp.sqrt(peak))
    for u in range(n_half // 8):
        peak_out[:, u * 128:(u + 1) * 128] = swapped[8 * u:8 * u + 8, :]
    for copy in s_copies.values():
        copy.wait_recv()

    def filtered(n, carry):
        rows = data4[ids_p[0, 0, n]].astype(f32)
        dr, di = rows[:, :NMIN], rows[:, NMIN:]
        wr, wi = turned[n, :, :NMIN], turned[n, :, NMIN:]
        z_out[n] = jnp.concatenate([dr * wr - di * wi, dr * wi + di * wr], axis=1).astype(bf16)
        return carry

    lax.fori_loop(0, n_trig, filtered, 0, unroll=16)

    for group in (z_copies, t_copies, c_copies, x_copies, s_copies, ts_copies):
        for copy in group.values():
            copy.wait_send()


def chi_kernel(z_in, hot_in, between_in, keep_in, spin_in, rnorm_in, tile_dft, row_phase, peak_in, peak_out, chi_out):
    f32, bf16 = jnp.float32, jnp.bfloat16
    n_grp = hot_in.shape[0]
    peak_out[...] = peak_in[...]
    at = lax.broadcasted_iota(jnp.int32, (GROUP * NCUT, NMIN), 1)
    row = lax.broadcasted_iota(jnp.int32, (GROUP * NCUT, NMIN), 0)
    step = ((at == row).astype(f32) - (at == row - GROUP).astype(f32)).astype(bf16)
    own_rows = lax.broadcasted_iota(jnp.int32, (2 * GROUP, NMIN), 0)
    whole = (lax.broadcasted_iota(jnp.int32, (2 * GROUP, NMIN), 1) // NMAJ == own_rows).astype(f32).astype(bf16)
    whole = jnp.concatenate([whole, jnp.zeros_like(whole)], axis=1)
    own_turn = row_phase[...].astype(f32)

    def rotate(v, w):
        vr, vi, wr, wi = v[:, :NMIN], v[:, NMIN:], w[:, :NMIN], w[:, NMIN:]
        return jnp.concatenate([vr * wr - vi * wi, vr * wi + vi * wr], axis=1).astype(bf16)

    def one_batch(t, carry):
        rows = GROUP * NMAJ
        qs = [t * BATCH + i for i in range(BATCH)]
        zs = [z_in[pl.ds(q * GROUP, GROUP)].reshape(rows, 2 * NMIN) for q in qs]
        picks = [jnp.dot(hot_in[q], z, preferred_element_type=f32) for q, z in zip(qs, zs)]
        parts = []
        for q, pick in zip(qs, picks):
            keep = keep_in[q]
            parts.append(pick.astype(bf16) * jnp.concatenate([keep, keep], axis=1))
        moved = [jnp.dot(jnp.concatenate([z, part], axis=0), tile_dft[...], preferred_element_type=f32) for z, part in zip(zs, parts)]
        turned = [jnp.concatenate([rotate(m[:rows], own_turn), rotate(m[rows:], spin_in[q])], axis=0) for q, m in zip(qs, moved)]
        bins = []
        for q, turn in zip(qs, turned):
            mix = jnp.concatenate([jnp.concatenate([between_in[q], step], axis=1), whole], axis=0)
            bins.append(jnp.dot(mix, turn, preferred_element_type=f32))
        for q, bn in zip(qs, bins):
            br, bi = bn[:rows, :NMIN], bn[:rows, NMIN:]
            energy = jnp.sum((br * br + bi * bi).reshape(NCUT, GROUP, NMIN), axis=0)
            tr, ti = bn[rows:rows + GROUP, :NMIN], bn[rows:rows + GROUP, NMIN:]
            loud = tr * tr + ti * ti
            at_q = pl.multiple_of(q * GROUP, GROUP)
            rnorm = rnorm_in[pl.ds(at_q, GROUP), :]
            reduced = jnp.maximum(energy - loud * (1.0 / NCUT), 0.0) * (NCUT / (2.0 * NCUT - 2.0)) * rnorm
            rho = jnp.sqrt(loud * rnorm)
            bend = jnp.exp(jnp.log((1.0 + reduced * reduced * reduced) * 0.5) * (-1.0 / 6.0))
            chi_out[0, 0, pl.ds(at_q, GROUP), :] = jnp.where(reduced > 1.0, rho * bend, rho)
        return carry

    lax.fori_loop(0, n_grp // BATCH, one_batch, 0, unroll=True)


def fused(sizes, ids_k, ids_p, ids_t, own, tmpl, cuts, tables):
    n_blk, n_det, n_sub = sizes
    n_tmpl = n_blk * tmpl.shape[0]
    n_trig = ids_k.shape[-1]
    n_grp = n_trig // GROUP
    hbm = pl.BlockSpec(memory_space=pltpu.HBM)
    vmem = pl.BlockSpec(memory_space=pltpu.VMEM)
    dma = pltpu.SemaphoreType.DMA
    f32, bf16 = jnp.float32, jnp.bfloat16
    n_half = tables[2].shape[1] // 2
    peak_shape = (own.shape[0], n_half * NMAJ)
    rows = GROUP * NCUT
    made = [
        (peak_shape, f32),
        ((n_trig, NMAJ, 2 * NMIN), bf16),
        ((n_grp, rows, NMIN), bf16),
        ((n_grp, rows, NMIN), bf16),
        ((n_grp, rows, NMIN), bf16),
        ((n_grp, rows, 2 * NMIN), f32),
        ((n_trig, NMIN), f32),
        (tables[3].shape, tables[3].dtype),
        (tables[4].shape, tables[4].dtype),
    ]
    scratch = [
        pltpu.VMEM((n_blk * n_det * own.shape[0],) + own.shape[1:], own.dtype),
        pltpu.VMEM((n_tmpl,) + tmpl.shape[1:], tmpl.dtype),
        pltpu.VMEM((n_blk,) + cuts.shape, cuts.dtype),
    ]
    scratch += [pltpu.SMEM(ids_k.shape, jnp.int32)] * 3
    scratch += [pltpu.VMEM(ids_k.shape, jnp.int32)]
    for i in (0, 1, 2, 5):
        table = tables[i]
        scratch.append(pltpu.VMEM(table.shape[1:] if i == 2 else table.shape, table.dtype))
    scratch += [
        pltpu.VMEM((n_tmpl, NMIN), f32),
        pltpu.VMEM((n_tmpl, 1, NMIN), f32),
        pltpu.VMEM((n_trig, NMAJ, 2 * NMIN), f32),
        dma((13,)),
        dma((n_blk,)), dma((n_blk,)),
        dma((n_blk, n_det)), dma((n_blk, n_det)),
        dma((n_blk, n_det)), dma((n_blk, n_det)),
        dma((n_blk,)), dma((n_blk,)),
        dma((n_blk,)), dma((n_blk,)),
        dma((n_blk,)), dma((n_blk,)),
    ]
    peak, z, hot, between, keep, spin, rnorm, tile_dft, row_phase = pl.pallas_call(
        functools.partial(gather_kernel, n_blk, n_det, n_sub),
        out_shape=[pltpu.VMEM(shape, dtype) for shape, dtype in made],
        in_specs=[hbm] * 12,
        out_specs=[vmem] * len(made),
        scratch_shapes=scratch,
        compiler_params=pltpu.CompilerParams(
            collective_id=0, has_side_effects=True, vmem_limit_bytes=24 * 1024 * 1024
        ),
        name="gather_and_peak",
    )(*(pltpu.with_memory_space_constraint(x, pltpu.HBM) for x in (ids_k, ids_p, ids_t, own, tmpl, cuts, *tables)))
    return pl.pallas_call(
        chi_kernel,
        out_shape=(
            jax.ShapeDtypeStruct(peak_shape, f32),
            jax.ShapeDtypeStruct(ids_k.shape + (STEPS * NMAJ,), f32),
        ),
        in_specs=[vmem] * 9,
        out_specs=(vmem, vmem),
        compiler_params=pltpu.CompilerParams(vmem_limit_bytes=24 * 1024 * 1024),
        name="chi",
    )(z, hot, between, keep, spin, rnorm, tile_dft, row_phase, peak)


def body(sizes, data, templates, bin_cuts, trig_template, trig_pair, trig_tile):
    tables = tuple(jnp.asarray(t) for t in host_tables(sizes[2]))
    peak, chi = fused(sizes, trig_template, trig_pair, trig_tile, data, templates, bin_cuts, tables)
    return peak, chi


def solution(mesh):
    sizes = (mesh.shape["blk"], mesh.shape["det"], mesh.shape["sub"])
    return jax.shard_map(
        functools.partial(body, sizes),
        mesh=mesh,
        in_specs=(
            P(("groups", "blk", "det"), None, None),
            P(("groups", "blk"), None, None),
            P(("groups", "blk"), None),
            P(("groups", "blk", "det"), "sub", None),
            P(("groups", "blk", "det"), "sub", None),
            P(("groups", "blk", "det"), "sub", None),
        ),
        out_specs=(
            P(("groups", "blk", "det"), "sub"),
            P(("groups", "blk", "det"), "sub", None, None),
        ),
        check_vma=False,
    )
```

```python
import functools
import math

import jax
import jax.numpy as jnp
import numpy as np
from jax import lax
from jax.experimental import pallas as pl
from jax.experimental.pallas import tpu as pltpu
from jax.sharding import PartitionSpec as P

MESH = pl.DeviceIdType.MESH
NMAJ = 16
NMIN = 128
NCUT = 16
STEPS = 8
GROUP = 8
BATCH = 8
PRE = 2


def unit_circle(index, period):
    angle = (index % period) * (2.0 * math.pi / period)
    return np.cos(angle), np.sin(angle)


def host_tables(n_sub):
    bf16 = jnp.bfloat16
    major = np.arange(NMAJ)
    minor = np.arange(NMIN)
    cos16, sin16 = unit_circle(major[:, None] * major[None, :], NMAJ)
    eye = np.eye(GROUP)
    first = np.concatenate([np.kron(eye, cos16), np.kron(eye, sin16)], axis=1).astype(bf16)
    twc, tws = unit_circle(major[:, None] * minor[None, :], NMAJ * NMIN)
    twiddle = np.concatenate([twc, tws], axis=1).astype(np.float32)
    n_half = NMIN // n_sub
    second = []
    for half in range(n_sub):
        steps = half * n_half + np.arange(n_half)
        cosine, sine = unit_circle(steps[:, None] * minor[None, :], NMIN)
        real_rows = np.concatenate([cosine, -sine], axis=1)
        imag_rows = np.concatenate([sine, cosine], axis=1)
        second.append(np.concatenate([real_rows, imag_rows], axis=0))
    second = np.stack(second).astype(bf16)
    times = np.arange(NMAJ * STEPS)
    cosine, sine = unit_circle(minor[:, None] * times[None, :], NMAJ * NMIN)
    tile_dft = np.concatenate(
        [np.concatenate([cosine, sine], axis=1), np.concatenate([-sine, cosine], axis=1)], axis=0
    ).astype(bf16)
    rowc, rows = unit_circle(major[:, None] * (times % NMAJ)[None, :], NMAJ)
    row_phase = np.tile(np.concatenate([rowc, rows], axis=1), (GROUP, 1)).astype(bf16)
    starts = np.arange(NMIN // STEPS) * STEPS
    phc, phs = unit_circle(starts[:, None] * minor[None, :], NMIN)
    tile_phase = np.concatenate([phc, phs], axis=1).astype(np.float32)[:, None, :]
    fixed = np.concatenate([first, row_phase, tile_dft], axis=0)
    wide = np.concatenate([twiddle[:, None, :], tile_phase], axis=0)
    return fixed, second, wide


def swap_blocks(x):
    sub = lax.broadcasted_iota(jnp.int32, x.shape, 0)
    grp = lax.broadcasted_iota(jnp.int32, x.shape, 1) // NMAJ
    rows, lanes = x.shape
    for bit in (1, 2, 4):
        up = pltpu.roll(pltpu.roll(x, rows - bit, 0), NMAJ * bit, 1)
        down = pltpu.roll(pltpu.roll(x, bit, 0), lanes - NMAJ * bit, 1)
        sb, gb = (sub & bit) != 0, (grp & bit) != 0
        x = jnp.where(jnp.logical_and(jnp.logical_not(sb), gb), up,
                      jnp.where(jnp.logical_and(sb, jnp.logical_not(gb)), down, x))
    return x


def conj_product(data, tmpl):
    dr, di = data[..., :NMIN], data[..., NMIN:]
    tr, ti = tmpl[..., :NMIN], tmpl[..., NMIN:]
    return dr * tr + di * ti, di * tr - dr * ti


def gather_kernel(n_blk, n_det, n_sub, *refs):
    (ids_k_in, ids_p_in, ids_t_in, own_in, tmpl_in, cuts_in, fixed_in, second_in, wide_in,
     peak_out, z_out, hot_out, between_out, keep_out, spin_out, rnorm_out, fixed,
     data4, tmpl4, cuts, ids_k, ids_p, ids_t, ids_v, second, wide_tab, cut_rows, norm_tab, turned,
     local_sem, data_send, tmpl_send, cuts_send, cuts_recv, tz_recv, tx_recv, ts_recv, x_recv, z_recv, zx_recv,
     xz_recv, s_recv) = refs
    f32, bf16 = jnp.float32, jnp.bfloat16
    b = lax.axis_index("blk")
    d = lax.axis_index("det")
    half = lax.axis_index("sub")
    other = n_sub - 1 - half
    pairs = own_in.shape[0]
    kb = tmpl_in.shape[0]
    n_cut = cuts_in.shape[1]
    n_tmpl = n_blk * kb
    n_trig = ids_k_in.shape[2]
    n_grp = n_trig // GROUP
    hp, hk = pairs // n_sub, kb // n_sub
    ha = hp // 2
    share = math.gcd(hk, n_det)
    hq = hk // share
    own = b * n_det + d

    barrier = pltpu.get_barrier_semaphore()
    for dz in range(1, n_blk):
        pl.semaphore_signal(barrier, inc=1, device_id={"blk": lax.rem(b + dz, n_blk)}, device_id_type=MESH)
    for dx in range(1, n_det):
        pl.semaphore_signal(barrier, inc=1, device_id={"det": lax.rem(d + dx, n_det)}, device_id_type=MESH)
    pl.semaphore_signal(barrier, inc=1, device_id={"sub": other}, device_id_type=MESH)

    moves = [(own_in, data4.at[pl.ds(own * pairs, pairs)]), (tmpl_in, tmpl4.at[pl.ds(b * kb, kb)]),
             (cuts_in, cuts.at[b]), (fixed_in, fixed), (wide_in, wide_tab), (second_in.at[half], second),
             (ids_k_in, ids_k), (ids_p_in, ids_p), (ids_t_in, ids_t), (ids_k_in, ids_v)]
    fetches = [pltpu.make_async_copy(src, dst, local_sem.at[i]) for i, (src, dst) in enumerate(moves)]
    for copy in fetches:
        copy.start()
    for copy in fetches[:3]:
        copy.wait()
    pl.semaphore_wait(barrier, n_blk + n_det - 1)

    def remote(ref, send, recv, where):
        copy = pltpu.make_async_remote_copy(src_ref=ref, dst_ref=ref, send_sem=send.at[0], recv_sem=recv,
                                            device_id=where, device_id_type=MESH)
        copy.start()
        return copy

    def partner(step):
        index = b
        bit = 1
        while bit <= step:
            if step & bit:
                index = index + bit * (1 - 2 * lax.rem(b // bit, 2))
            bit *= 2
        return index

    def data_part(place, first, count):
        return data4.at[pl.ds(place * pairs + half * hp + first, count)]

    def tmpl_part(place, first, count):
        return tmpl4.at[pl.ds(place * kb + half * hk + first, count)]

    def column(dx):
        return lax.rem(d + dx, n_det)

    def other_half(place):
        remote(data_part(place, 0, hp), data_send, s_recv.at[0], {"sub": other})

    steps = list(range(n_blk - 1, 0, -1))
    far = [dz for dz in steps if dz > 1]
    pieces = {dz: ([(0, ha), (ha, hp - ha)] if dz > 1 else [(0, 0), (0, hp)]) for dz in steps}
    x_own, z_early, z_late, relay_x, relay_z, t_z, t_x, t_s = {}, {}, {}, {}, {}, {}, {}, {}
    for dx in range(1, n_det):
        x_own[dx] = remote(data_part(own, 0, hp), data_send, x_recv.at[dx - 1], {"det": column(dx)})
    mine = lax.rem(d, share) * hq
    for dz in steps:
        t_z[dz] = remote(tmpl_part(b, mine, hq), tmpl_send, tz_recv.at[dz - 1], {"blk": partner(dz)})
    for dz in far:
        z_early[dz] = remote(data_part(own, *pieces[dz][0]), data_send, z_recv.at[0, dz - 1], {"blk": partner(dz)})
    for dz in steps[::-1]:
        z_late[dz] = remote(data_part(own, *pieces[dz][1]), data_send, z_recv.at[1, dz - 1], {"blk": partner(dz)})
    for dz in steps:
        remote(cuts.at[b], cuts_send, cuts_recv.at[0], {"blk": partner(dz)})
    for copy in fetches[3:]:
        copy.wait()

    n_fixed = NMAJ * GROUP
    wide = data4[pl.ds(own * pairs, pairs)].astype(f32)
    twiddle = wide_tab[:NMAJ].reshape(NMAJ, 2 * NMIN)
    twc = jnp.broadcast_to(twiddle[:, :NMIN][None], (pairs, NMAJ, NMIN)).reshape(pairs * NMAJ, NMIN)
    tws = jnp.broadcast_to(twiddle[:, NMIN:][None], (pairs, NMAJ, NMIN)).reshape(pairs * NMAJ, NMIN)
    n_half = second.shape[0] // 2

    def peak_of(src_b, peak):
        norms, stacks, bents = [], [], []
        for k in range(kb):
            row = tmpl4[src_b * kb + k].astype(f32)
            norm = jnp.sum(jnp.sum(row * row, axis=0, keepdims=True), axis=1, keepdims=True)
            norm_tab[src_b * kb + k] = jnp.broadcast_to(norm, (1, NMIN))
            norms.append(norm)
            real, imag = conj_product(wide, row[None])
            real = real.reshape(pairs * NMAJ, NMIN).astype(bf16)
            imag = imag.reshape(pairs * NMAJ, NMIN).astype(bf16)
            stacks.append(jnp.concatenate(
                [jnp.concatenate([real, imag], axis=1), jnp.concatenate([-imag, real], axis=1)], axis=0
            ))
        sections = [jnp.dot(fixed[:n_fixed, :], stack, preferred_element_type=f32) for stack in stacks]
        for section in sections:
            sr, si = section[:, :NMIN], section[:, NMIN:]
            bents.append(jnp.concatenate([sr * twc - si * tws, sr * tws + si * twc], axis=1).astype(bf16))
        snrs = [lax.dot_general(second[...], bent, (((1,), (1,)), ((), ())), preferred_element_type=f32)
                for bent in bents]
        for snr, norm in zip(snrs, norms):
            power = snr[:n_half] * snr[:n_half] + snr[n_half:] * snr[n_half:]
            peak = jnp.maximum(peak, power * (1.0 / norm))
        return peak

    peak = peak_of(b, jnp.zeros((n_half, pairs * NMAJ), f32))

    for dz in steps:
        t_z[dz].wait_recv()
        for j in range(1, share):
            to = d - lax.rem(d, share) + lax.rem(d + j, share)
            t_x[dz, j] = remote(tmpl_part(partner(dz), mine, hq), tmpl_send, tx_recv.at[dz - 1, j - 1], {"det": to})
    for dx in range(1, n_det):
        x_own[dx].wait_recv()
        place = b * n_det + column(n_det - dx)
        for dz in steps:
            relay_z[dz, dx] = remote(data_part(place, *pieces[dz][1]), data_send, xz_recv.at[dz - 1, dx - 1],
                                     {"blk": partner(dz)})
        other_half(place)
    for dz in far:
        z_early[dz].wait_recv()
        for dx in range(1, n_det):
            relay_x[dz, dx] = remote(data_part(partner(dz) * n_det + d, *pieces[dz][0]), data_send,
                                     zx_recv.at[dz - 1, dx - 1], {"det": column(dx)})

    every = pltpu.make_async_copy(cuts.at[pl.ds(0, n_blk - 1)], cuts.at[pl.ds(0, n_blk - 1)], cuts_recv.at[0])
    every.wait()
    cut_rows[...] = jnp.zeros(cut_rows.shape, f32)
    cut_rows[:, NCUT - 1:NCUT] = jnp.full((n_tmpl, 1), NMAJ, f32)
    for blk in range(n_blk):
        cut_rows[blk * kb:(blk + 1) * kb, 0:n_cut] = (cuts[blk] >> 7).astype(f32)
        cut_rows[blk * kb:(blk + 1) * kb, 64:64 + n_cut] = (cuts[blk] & (NMIN - 1)).astype(f32)
    is_k = lax.broadcasted_iota(jnp.int32, (n_tmpl, n_trig), 0) == jnp.broadcast_to(ids_v[0], (n_tmpl, n_trig))
    pick_k = is_k.astype(f32).astype(bf16)

    def by_trigger(table):
        return lax.dot_general(pick_k, table, (((0,), (0,)), ((), ())), preferred_element_type=f32)

    trig_cuts = by_trigger(cut_rows[...].astype(bf16))
    lane = lax.broadcasted_iota(jnp.int32, (n_trig, NMIN), 1)
    spread = (
        (lax.broadcasted_iota(jnp.int32, (NMIN, 2 * NMIN), 0) < 64)
        == (lax.broadcasted_iota(jnp.int32, (NMIN, 2 * NMIN), 1) < NMIN)
    ).astype(f32).astype(bf16)
    base = ((lax.broadcasted_iota(jnp.int32, (n_trig, NMIN), 0) % GROUP) * NMAJ).astype(f32)
    at = lane.astype(f32)

    def cut_masks(first, count, last):
        spans = []
        for r in range(first, first + count):
            only = jnp.where((lane & 63) == r, trig_cuts, 0.0).astype(bf16)
            spans.append(jnp.dot(only, spread, preferred_element_type=f32))
        stacks = ([], [], [])
        for i, span in enumerate(spans):
            row = span[:, :NMIN] + base
            marks = (at == row, jnp.logical_and(at >= last, at < row), at < span[:, NMIN:])
            last = row
            for stack, mark in zip(stacks, marks):
                stack.append(mark.astype(f32).reshape(n_grp, GROUP, NMIN))
            if i % 2 == 1:
                rows = slice((first + i - 1) * GROUP, (first + i + 1) * GROUP)
                for stack, out in zip(stacks, (hot_out, between_out, keep_out)):
                    out[:, rows, :] = jnp.concatenate(stack[-2:], axis=1).astype(bf16)
        return last

    last = cut_masks(0, NCUT // 2, base)
    for dz in steps:
        for j in range(1, share):
            t_x[dz, j].wait_recv()
        t_s[dz] = remote(tmpl_part(partner(dz), 0, hk), tmpl_send, ts_recv.at[dz - 1], {"sub": other})
    cut_masks(NCUT // 2, NCUT // 2, last)
    for dz in steps[::-1]:
        z_late[dz].wait_recv()
        other_half(partner(dz) * n_det + d)
    for q in range(n_grp):
        spin_out[q] = jnp.dot(hot_out[q], fixed[n_fixed:2 * n_fixed, :], preferred_element_type=f32)

    def prepare(n, carry):
        k = ids_k[0, 0, n]
        row = tmpl4[k].astype(f32)
        phase = wide_tab[NMAJ + half * ((wide_tab.shape[0] - NMAJ) // n_sub) + ids_t[0, 0, n]]
        pc, ps = phase[:, :NMIN], phase[:, NMIN:]
        tr, ti = row[:, :NMIN], row[:, NMIN:]
        turned[n, :, :NMIN] = tr * pc + ti * ps
        turned[n, :, NMIN:] = tr * ps - ti * pc
        return carry

    def relayed():
        for dz in steps[::-1]:
            for dx in range(1, n_det):
                relay_z[dz, dx].wait_recv()
                if dz > 1:
                    relay_x[dz, dx].wait_recv()
                other_half(partner(dz) * n_det + column(n_det - dx))

    for at_step, dz in enumerate(steps):
        if at_step == PRE:
            relayed()
        t_s[dz].wait_recv()
        peak = peak_of(partner(dz), peak)
    if len(steps) <= PRE:
        relayed()
    lax.fori_loop(0, n_trig, prepare, 0, unroll=16)

    rest = 1.0 / norm_tab[...].reshape(n_tmpl, NMIN)
    scale = jnp.zeros((n_trig, NMIN), f32)
    for _ in range(3):
        piece = rest.astype(bf16)
        rest = rest - piece.astype(f32)
        scale = scale + by_trigger(piece)
    rnorm_out[...] = scale

    swapped = swap_blocks(jnp.sqrt(peak))
    for u in range(n_half // 8):
        peak_out[:, u * 128:(u + 1) * 128] = swapped[8 * u:8 * u + 8, :]

    n_data = (n_blk * n_det - 1) * hp
    some = data4.at[pl.ds(0, n_data)]
    pltpu.make_async_copy(some, some, s_recv.at[0]).wait()

    def filtered(n, carry):
        rows = data4[ids_p[0, 0, n]].astype(f32)
        dr, di = rows[:, :NMIN], rows[:, NMIN:]
        wr, wi = turned[n, :, :NMIN], turned[n, :, NMIN:]
        z_out[n] = jnp.concatenate([dr * wr - di * wi, dr * wi + di * wr], axis=1).astype(bf16)
        return carry

    lax.fori_loop(0, n_trig, filtered, 0, unroll=16)

    some = data4.at[pl.ds(0, 2 * n_data)]
    pltpu.make_async_copy(some, some, data_send.at[0]).wait()
    some = tmpl4.at[pl.ds(0, 2 * (n_blk - 1) * hk)]
    pltpu.make_async_copy(some, some, tmpl_send.at[0]).wait()
    some = cuts.at[pl.ds(0, n_blk - 1)]
    pltpu.make_async_copy(some, some, cuts_send.at[0]).wait()


def chi_kernel(z_in, hot_in, between_in, keep_in, spin_in, rnorm_in, fixed, peak_in, peak_out, chi_out, chi_rows, sem):
    f32, bf16 = jnp.float32, jnp.bfloat16
    n_grp = hot_in.shape[0]
    n_fixed = NMAJ * GROUP
    save_peak = pltpu.make_async_copy(peak_in, peak_out, sem.at[0])
    save_peak.start()
    at = lax.broadcasted_iota(jnp.int32, (GROUP * NCUT, NMIN), 1)
    row = lax.broadcasted_iota(jnp.int32, (GROUP * NCUT, NMIN), 0)
    step = ((at == row).astype(f32) - (at == row - GROUP).astype(f32)).astype(bf16)
    own_rows = lax.broadcasted_iota(jnp.int32, (2 * GROUP, NMIN), 0)
    whole = (lax.broadcasted_iota(jnp.int32, (2 * GROUP, NMIN), 1) // NMAJ == own_rows).astype(f32).astype(bf16)
    whole = jnp.concatenate([whole, jnp.zeros_like(whole)], axis=1)
    own_turn = fixed[n_fixed:2 * n_fixed, :].astype(f32)

    def rotate(v, w):
        vr, vi, wr, wi = v[:, :NMIN], v[:, NMIN:], w[:, :NMIN], w[:, NMIN:]
        return jnp.concatenate([vr * wr - vi * wi, vr * wi + vi * wr], axis=1).astype(bf16)

    def one_batch(t):
        rows = GROUP * NMAJ
        qs = [t * BATCH + i for i in range(BATCH)]
        zs = [z_in[pl.ds(q * GROUP, GROUP)].reshape(rows, 2 * NMIN) for q in qs]
        picks = [jnp.dot(hot_in[q], z, preferred_element_type=f32) for q, z in zip(qs, zs)]
        parts = []
        for q, pick in zip(qs, picks):
            keep = keep_in[q]
            parts.append(pick.astype(bf16) * jnp.concatenate([keep, keep], axis=1))
        moved = [jnp.dot(jnp.concatenate([z, part], axis=0), fixed[2 * n_fixed:, :], preferred_element_type=f32) for z, part in zip(zs, parts)]
        turned = [jnp.concatenate([rotate(m[:rows], own_turn), rotate(m[rows:], spin_in[q])], axis=0) for q, m in zip(qs, moved)]
        bins = []
        for q, turn in zip(qs, turned):
            mix = jnp.concatenate([jnp.concatenate([between_in[q], step], axis=1), whole], axis=0)
            bins.append(jnp.dot(mix, turn, preferred_element_type=f32))
        for q, bn in zip(qs, bins):
            br, bi = bn[:rows, :NMIN], bn[:rows, NMIN:]
            energy = jnp.sum((br * br + bi * bi).reshape(NCUT, GROUP, NMIN), axis=0)
            tr, ti = bn[rows:rows + GROUP, :NMIN], bn[rows:rows + GROUP, NMIN:]
            loud = tr * tr + ti * ti
            at_q = q * GROUP
            rnorm = rnorm_in[pl.ds(at_q, GROUP), :]
            reduced = jnp.maximum(energy - loud * (1.0 / NCUT), 0.0) * (NCUT / (2.0 * NCUT - 2.0)) * rnorm
            rho = jnp.sqrt(loud * rnorm)
            bend = jnp.exp(jnp.log((1.0 + reduced * reduced * reduced) * 0.5) * (-1.0 / 6.0))
            chi_rows[pl.ds(at_q, GROUP), :] = jnp.where(reduced > 1.0, rho * bend, rho)

    saves = []
    for t in range(n_grp // BATCH):
        one_batch(t)
        part = pl.ds(t * BATCH * GROUP, BATCH * GROUP)
        saves.append(pltpu.make_async_copy(chi_rows.at[part], chi_out.at[0, 0, part], sem.at[1 + t]))
        saves[-1].start()
    save_peak.wait()
    for save in saves:
        save.wait()


def fused(sizes, ids_k, ids_p, ids_t, own, tmpl, cuts, tables):
    n_blk, n_det, n_sub = sizes
    fixed, second, wide = tables
    n_tmpl = n_blk * tmpl.shape[0]
    n_trig = ids_k.shape[-1]
    n_grp = n_trig // GROUP
    hbm = pl.BlockSpec(memory_space=pltpu.HBM)
    vmem = pl.BlockSpec(memory_space=pltpu.VMEM)
    dma = pltpu.SemaphoreType.DMA
    f32, bf16 = jnp.float32, jnp.bfloat16
    n_half = second.shape[1] // 2
    peak_shape = (own.shape[0], n_half * NMAJ)
    rows = GROUP * NCUT
    share = math.gcd(tmpl.shape[0] // n_sub, n_det)
    made = [
        (peak_shape, f32),
        ((n_trig, NMAJ, 2 * NMIN), bf16),
        ((n_grp, rows, NMIN), bf16),
        ((n_grp, rows, NMIN), bf16),
        ((n_grp, rows, NMIN), bf16),
        ((n_grp, rows, 2 * NMIN), f32),
        ((n_trig, NMIN), f32),
        (fixed.shape, fixed.dtype),
    ]
    scratch = [
        pltpu.VMEM((n_blk * n_det * own.shape[0],) + own.shape[1:], own.dtype),
        pltpu.VMEM((n_tmpl,) + tmpl.shape[1:], tmpl.dtype),
        pltpu.VMEM((n_blk,) + cuts.shape, cuts.dtype),
    ]
    scratch += [pltpu.SMEM(ids_k.shape, jnp.int32)] * 3
    scratch += [
        pltpu.VMEM(ids_k.shape, jnp.int32),
        pltpu.VMEM(second.shape[1:], second.dtype),
        pltpu.VMEM(wide.shape, wide.dtype),
        pltpu.VMEM((n_tmpl, NMIN), f32),
        pltpu.VMEM((n_tmpl, 1, NMIN), f32),
        pltpu.VMEM((n_trig, NMAJ, 2 * NMIN), f32),
        dma((10,)), dma((1,)), dma((1,)), dma((1,)), dma((1,)),
        dma((n_blk - 1,)), dma((n_blk - 1, max(share - 1, 1))), dma((n_blk - 1,)),
        dma((n_det - 1,)), dma((2, n_blk - 1)), dma((n_blk - 1, n_det - 1)), dma((n_blk - 1, n_det - 1)), dma((1,)),
    ]
    made_refs = pl.pallas_call(
        functools.partial(gather_kernel, n_blk, n_det, n_sub),
        out_shape=[pltpu.VMEM(shape, dtype) for shape, dtype in made],
        in_specs=[hbm] * 9,
        out_specs=[vmem] * len(made),
        scratch_shapes=scratch,
        compiler_params=pltpu.CompilerParams(
            collective_id=0, has_side_effects=True, vmem_limit_bytes=32 * 1024 * 1024
        ),
        name="gather_and_peak",
    )(*(pltpu.with_memory_space_constraint(x, pltpu.HBM)
        for x in (ids_k, ids_p, ids_t, own, tmpl, cuts, fixed, second, wide)))
    return pl.pallas_call(
        chi_kernel,
        out_shape=(
            jax.ShapeDtypeStruct(peak_shape, f32),
            jax.ShapeDtypeStruct(ids_k.shape + (STEPS * NMAJ,), f32),
        ),
        in_specs=[vmem] * len(made),
        out_specs=(hbm, hbm),
        scratch_shapes=[pltpu.VMEM((n_trig, STEPS * NMAJ), f32), dma((1 + n_grp // BATCH,))],
        compiler_params=pltpu.CompilerParams(vmem_limit_bytes=24 * 1024 * 1024),
        name="chi",
    )(*made_refs[1:], made_refs[0])


def body(sizes, data, templates, bin_cuts, trig_template, trig_pair, trig_tile):
    tables = tuple(jnp.asarray(t) for t in host_tables(sizes[2]))
    peak, chi = fused(sizes, trig_template, trig_pair, trig_tile, data, templates, bin_cuts, tables)
    return peak, chi


def solution(mesh):
    sizes = (mesh.shape["blk"], mesh.shape["det"], mesh.shape["sub"])
    return jax.shard_map(
        functools.partial(body, sizes),
        mesh=mesh,
        in_specs=(
            P(("groups", "blk", "det"), None, None),
            P(("groups", "blk"), None, None),
            P(("groups", "blk"), None),
            P(("groups", "blk", "det"), "sub", None),
            P(("groups", "blk", "det"), "sub", None),
            P(("groups", "blk", "det"), "sub", None),
        ),
        out_specs=(
            P(("groups", "blk", "det"), "sub"),
            P(("groups", "blk", "det"), "sub", None, None),
        ),
        check_vma=False,
    )
```

```python
import functools
import math

import jax
import jax.numpy as jnp
import numpy as np
from jax import lax
from jax.experimental import pallas as pl
from jax.experimental.pallas import tpu as pltpu
from jax.sharding import PartitionSpec as P

MESH = pl.DeviceIdType.MESH
NMAJ = 16
NMIN = 128
NCUT = 16
STEPS = 8
GROUP = 8
BATCH = 8
PRE = 2


def unit_circle(index, period):
    angle = (index % period) * (2.0 * math.pi / period)
    return np.cos(angle), np.sin(angle)


def host_tables(n_sub):
    bf16 = jnp.bfloat16
    major = np.arange(NMAJ)
    minor = np.arange(NMIN)
    cos16, sin16 = unit_circle(major[:, None] * major[None, :], NMAJ)
    eye = np.eye(GROUP)
    first = np.concatenate([np.kron(eye, cos16), np.kron(eye, sin16)], axis=1).astype(bf16)
    twc, tws = unit_circle(major[:, None] * minor[None, :], NMAJ * NMIN)
    twiddle = np.concatenate([twc, tws], axis=1).astype(np.float32)
    n_half = NMIN // n_sub
    second = []
    for half in range(n_sub):
        steps = half * n_half + np.arange(n_half)
        cosine, sine = unit_circle(steps[:, None] * minor[None, :], NMIN)
        real_rows = np.concatenate([cosine, -sine], axis=1)
        imag_rows = np.concatenate([sine, cosine], axis=1)
        second.append(np.concatenate([real_rows, imag_rows], axis=0))
    second = np.stack(second).astype(bf16)
    times = np.arange(NMAJ * STEPS)
    cosine, sine = unit_circle(minor[:, None] * times[None, :], NMAJ * NMIN)
    tile_dft = np.concatenate(
        [np.concatenate([cosine, sine], axis=1), np.concatenate([-sine, cosine], axis=1)], axis=0
    ).astype(bf16)
    rowc, rows = unit_circle(major[:, None] * (times % NMAJ)[None, :], NMAJ)
    row_phase = np.tile(np.concatenate([rowc, rows], axis=1), (GROUP, 1)).astype(bf16)
    starts = np.arange(NMIN // STEPS) * STEPS
    phc, phs = unit_circle(starts[:, None] * minor[None, :], NMIN)
    tile_phase = np.concatenate([phc, phs], axis=1).astype(np.float32)[:, None, :]
    fixed = np.concatenate([first, row_phase, tile_dft], axis=0)
    wide = np.concatenate([twiddle[:, None, :], tile_phase], axis=0)
    return fixed, second, wide


def swap_blocks(x):
    sub = lax.broadcasted_iota(jnp.int32, x.shape, 0)
    grp = lax.broadcasted_iota(jnp.int32, x.shape, 1) // NMAJ
    rows, lanes = x.shape
    for bit in (1, 2, 4):
        up = pltpu.roll(pltpu.roll(x, rows - bit, 0), NMAJ * bit, 1)
        down = pltpu.roll(pltpu.roll(x, bit, 0), lanes - NMAJ * bit, 1)
        sb, gb = (sub & bit) != 0, (grp & bit) != 0
        x = jnp.where(jnp.logical_and(jnp.logical_not(sb), gb), up,
                      jnp.where(jnp.logical_and(sb, jnp.logical_not(gb)), down, x))
    return x


def conj_product(data, tmpl):
    dr, di = data[..., :NMIN], data[..., NMIN:]
    tr, ti = tmpl[..., :NMIN], tmpl[..., NMIN:]
    return dr * tr + di * ti, di * tr - dr * ti


def gather_kernel(n_blk, n_det, n_sub, *refs):
    (ids_k_in, ids_p_in, ids_t_in, own_in, tmpl_in, cuts_in, fixed_in, second_in, wide_in,
     peak_out, z_out, hot_out, between_out, keep_out, spin_out, rnorm_out, fixed,
     data4, tmpl4, cuts, ids_k, ids_p, ids_t, ids_v, second, wide_tab, cut_rows, norm_tab, turned,
     local_sem, data_send, tmpl_send, cuts_send, cuts_recv, t_recv, ts_recv, x_recv, z_recv, zx_recv,
     xz_recv, s_recv, blk_in, det_in, sub_in) = refs
    f32, bf16 = jnp.float32, jnp.bfloat16
    b = lax.axis_index("blk")
    d = lax.axis_index("det")
    half = lax.axis_index("sub")
    other = n_sub - 1 - half
    pairs = own_in.shape[0]
    kb = tmpl_in.shape[0]
    n_cut = cuts_in.shape[1]
    n_tmpl = n_blk * kb
    n_trig = ids_k_in.shape[2]
    n_grp = n_trig // GROUP
    hp, hk = pairs // n_sub, kb // n_sub
    ha = hp // 2
    own = b * n_det + d
    early, late = (0, ha), (ha, hp - ha)

    moves = [(own_in, data4.at[pl.ds(own * pairs, pairs)]), (tmpl_in, tmpl4.at[pl.ds(b * kb, kb)]),
             (cuts_in, cuts.at[b]), (fixed_in, fixed), (wide_in, wide_tab), (second_in.at[half], second),
             (ids_k_in, ids_k), (ids_p_in, ids_p), (ids_t_in, ids_t), (ids_k_in, ids_v)]
    fetches = [pltpu.make_async_copy(src, dst, local_sem.at[i]) for i, (src, dst) in enumerate(moves)]
    for copy in fetches[:3]:
        copy.start()

    barrier = pltpu.get_barrier_semaphore()

    def tell(sem, where):
        pl.semaphore_signal(sem, inc=1, device_id=where, device_id_type=MESH)

    for q in range(n_blk - 1, 0, -1):
        pl.when(b < q)(functools.partial(tell, barrier, {"blk": q}))
    for c in range(n_det - 1, 0, -1):
        pl.when(d < c)(functools.partial(tell, barrier, {"det": c}))
    pl.when(half == n_sub - 1)(functools.partial(tell, barrier, {"sub": other}))
    lower = b + d + (n_sub - 1 - half)
    pl.when(lower > 0)(lambda: pl.semaphore_wait(barrier, lower))
    for q in range(n_blk - 1):
        pl.when(b > q)(functools.partial(tell, blk_in.at[lax.rem(b - q - 1 + n_blk, n_blk)], {"blk": q}))
    for c in range(n_det - 1):
        pl.when(d > c)(functools.partial(tell, det_in.at[lax.rem(d - c - 1 + n_det, n_det)], {"det": c}))
    pl.when(half == 0)(functools.partial(tell, sub_in.at[0], {"sub": other}))
    for copy in fetches[3:]:
        copy.start()
    for copy in fetches[:3]:
        copy.wait()

    def remote(ref, send, recv, where):
        pltpu.make_async_remote_copy(src_ref=ref, dst_ref=ref, send_sem=send.at[0], recv_sem=recv,
                                     device_id=where, device_id_type=MESH).start()

    def arrived(ref, sem):
        pltpu.make_async_copy(ref, ref, sem).wait()

    def data_part(place, first, count):
        return data4.at[pl.ds(place * pairs + half * hp + first, count)]

    def tmpl_part(place):
        return tmpl4.at[pl.ds(place * kb + half * hk, hk)]

    def column(dx):
        return lax.rem(d + dx, n_det)

    def other_half(place):
        remote(data_part(place, 0, hp), data_send, s_recv.at[0], {"sub": other})

    peers = []
    for i in range(n_blk - 1):
        higher = (i + n_blk - b) // n_blk
        q = i + higher
        peers.append((q, higher, lax.rem(q - b - 1 + n_blk, n_blk), lax.rem(b - q - 1 + n_blk, n_blk)))

    def send_x(dx):
        remote(data_part(own, 0, hp), data_send, x_recv.at[n_det - 1 - dx], {"det": column(dx)})

    def send_z(q, there):
        where = {"blk": q}
        remote(tmpl_part(b), tmpl_send, t_recv.at[there], where)
        remote(data_part(own, *early), data_send, z_recv.at[0, there], where)
        remote(data_part(own, *late), data_send, z_recv.at[1, there], where)
        remote(cuts.at[b], cuts_send, cuts_recv.at[0], where)

    for dx in range(1, n_det):
        pl.when(column(dx) < d)(functools.partial(send_x, dx))
    for q, higher, here, there in peers:
        pl.when(higher == 0)(functools.partial(send_z, q, there))
    for copy in fetches[3:]:
        copy.wait()

    n_fixed = NMAJ * GROUP
    wide = data4[pl.ds(own * pairs, pairs)].astype(f32)
    twiddle = wide_tab[:NMAJ].reshape(NMAJ, 2 * NMIN)
    twc = jnp.broadcast_to(twiddle[:, :NMIN][None], (pairs, NMAJ, NMIN)).reshape(pairs * NMAJ, NMIN)
    tws = jnp.broadcast_to(twiddle[:, NMIN:][None], (pairs, NMAJ, NMIN)).reshape(pairs * NMAJ, NMIN)
    n_half = second.shape[0] // 2

    def peak_of(src_b, peak):
        norms, stacks, bents = [], [], []
        for k in range(kb):
            row = tmpl4[src_b * kb + k].astype(f32)
            norm = jnp.sum(jnp.sum(row * row, axis=0, keepdims=True), axis=1, keepdims=True)
            norm_tab[src_b * kb + k] = jnp.broadcast_to(norm, (1, NMIN))
            norms.append(norm)
            real, imag = conj_product(wide, row[None])
            real = real.reshape(pairs * NMAJ, NMIN).astype(bf16)
            imag = imag.reshape(pairs * NMAJ, NMIN).astype(bf16)
            stacks.append(jnp.concatenate(
                [jnp.concatenate([real, imag], axis=1), jnp.concatenate([-imag, real], axis=1)], axis=0
            ))
        sections = [jnp.dot(fixed[:n_fixed, :], stack, preferred_element_type=f32) for stack in stacks]
        for section in sections:
            sr, si = section[:, :NMIN], section[:, NMIN:]
            bents.append(jnp.concatenate([sr * twc - si * tws, sr * tws + si * twc], axis=1).astype(bf16))
        snrs = [lax.dot_general(second[...], bent, (((1,), (1,)), ((), ())), preferred_element_type=f32)
                for bent in bents]
        for snr, norm in zip(snrs, norms):
            power = snr[:n_half] * snr[:n_half] + snr[n_half:] * snr[n_half:]
            peak = jnp.maximum(peak, power * (1.0 / norm))
        return peak

    peak = peak_of(b, jnp.zeros((n_half, pairs * NMAJ), f32))

    def answer_x(dx):
        pl.semaphore_wait(det_in.at[dx - 1], 1)
        send_x(dx)

    def answer_z(q, here, there):
        pl.semaphore_wait(blk_in.at[here], 1)
        send_z(q, there)

    for dx in range(1, n_det):
        pl.when(column(dx) > d)(functools.partial(answer_x, dx))
    for q, higher, here, there in peers:
        pl.when(higher == 1)(functools.partial(answer_z, q, here, there))
    pl.when(half == n_sub - 1)(lambda: pl.semaphore_wait(sub_in.at[0], 1))

    for dx in range(1, n_det):
        place = b * n_det + column(dx)
        arrived(data_part(place, 0, hp), x_recv.at[dx - 1])
        for q, higher, here, there in peers:
            remote(data_part(place, *late), data_send, xz_recv.at[there, dx - 1], {"blk": q})
        other_half(place)
    for q, higher, here, there in peers:
        arrived(tmpl_part(q), t_recv.at[here])
        remote(tmpl_part(q), tmpl_send, ts_recv.at[here], {"sub": other})
        arrived(data_part(q * n_det + d, *early), z_recv.at[0, here])
        for dx in range(1, n_det):
            remote(data_part(q * n_det + d, *early), data_send, zx_recv.at[here, n_det - 1 - dx], {"det": column(dx)})

    arrived(cuts.at[pl.ds(0, n_blk - 1)], cuts_recv.at[0])
    cut_rows[...] = jnp.zeros(cut_rows.shape, f32)
    cut_rows[:, NCUT - 1:NCUT] = jnp.full((n_tmpl, 1), NMAJ, f32)
    for blk in range(n_blk):
        cut_rows[blk * kb:(blk + 1) * kb, 0:n_cut] = (cuts[blk] >> 7).astype(f32)
        cut_rows[blk * kb:(blk + 1) * kb, 64:64 + n_cut] = (cuts[blk] & (NMIN - 1)).astype(f32)
    is_k = lax.broadcasted_iota(jnp.int32, (n_tmpl, n_trig), 0) == jnp.broadcast_to(ids_v[0], (n_tmpl, n_trig))
    pick_k = is_k.astype(f32).astype(bf16)

    def by_trigger(table):
        return lax.dot_general(pick_k, table, (((0,), (0,)), ((), ())), preferred_element_type=f32)

    trig_cuts = by_trigger(cut_rows[...].astype(bf16))
    lane = lax.broadcasted_iota(jnp.int32, (n_trig, NMIN), 1)
    spread = (
        (lax.broadcasted_iota(jnp.int32, (NMIN, 2 * NMIN), 0) < 64)
        == (lax.broadcasted_iota(jnp.int32, (NMIN, 2 * NMIN), 1) < NMIN)
    ).astype(f32).astype(bf16)
    base = ((lax.broadcasted_iota(jnp.int32, (n_trig, NMIN), 0) % GROUP) * NMAJ).astype(f32)
    at = lane.astype(f32)

    def cut_masks(first, count, last):
        spans = []
        for r in range(first, first + count):
            only = jnp.where((lane & 63) == r, trig_cuts, 0.0).astype(bf16)
            spans.append(jnp.dot(only, spread, preferred_element_type=f32))
        stacks = ([], [], [])
        for i, span in enumerate(spans):
            row = span[:, :NMIN] + base
            marks = (at == row, jnp.logical_and(at >= last, at < row), at < span[:, NMIN:])
            last = row
            for stack, mark in zip(stacks, marks):
                stack.append(mark.astype(f32).reshape(n_grp, GROUP, NMIN))
            if i % 2 == 1:
                rows = slice((first + i - 1) * GROUP, (first + i + 1) * GROUP)
                for stack, out in zip(stacks, (hot_out, between_out, keep_out)):
                    out[:, rows, :] = jnp.concatenate(stack[-2:], axis=1).astype(bf16)
        return last

    last = cut_masks(0, NCUT // 2, base)
    for q, higher, here, there in peers:
        arrived(data_part(q * n_det + d, *late), z_recv.at[1, here])
        other_half(q * n_det + d)
    cut_masks(NCUT // 2, NCUT // 2, last)
    for q in range(n_grp):
        spin_out[q] = jnp.dot(hot_out[q], fixed[n_fixed:2 * n_fixed, :], preferred_element_type=f32)

    def prepare(n, carry):
        k = ids_k[0, 0, n]
        row = tmpl4[k].astype(f32)
        phase = wide_tab[NMAJ + half * ((wide_tab.shape[0] - NMAJ) // n_sub) + ids_t[0, 0, n]]
        pc, ps = phase[:, :NMIN], phase[:, NMIN:]
        tr, ti = row[:, :NMIN], row[:, NMIN:]
        turned[n, :, :NMIN] = tr * pc + ti * ps
        turned[n, :, NMIN:] = tr * ps - ti * pc
        return carry

    def relayed():
        for q, higher, here, there in peers:
            for dx in range(1, n_det):
                place = q * n_det + column(dx)
                arrived(data_part(place, *late), xz_recv.at[here, dx - 1])
                arrived(data_part(place, *early), zx_recv.at[here, dx - 1])
                other_half(place)

    for i, (q, higher, here, there) in enumerate(peers):
        if i == PRE:
            relayed()
        arrived(tmpl4.at[pl.ds(q * kb + other * hk, hk)], ts_recv.at[here])
        peak = peak_of(q, peak)
    if len(peers) <= PRE:
        relayed()
    lax.fori_loop(0, n_trig, prepare, 0, unroll=16)

    rest = 1.0 / norm_tab[...].reshape(n_tmpl, NMIN)
    scale = jnp.zeros((n_trig, NMIN), f32)
    for _ in range(3):
        piece = rest.astype(bf16)
        rest = rest - piece.astype(f32)
        scale = scale + by_trigger(piece)
    rnorm_out[...] = scale

    swapped = swap_blocks(jnp.sqrt(peak))
    for u in range(n_half // 8):
        peak_out[:, u * 128:(u + 1) * 128] = swapped[8 * u:8 * u + 8, :]

    n_data = (n_blk * n_det - 1) * hp
    some = data4.at[pl.ds(0, n_data)]
    pltpu.make_async_copy(some, some, s_recv.at[0]).wait()

    def filtered(n, carry):
        rows = data4[ids_p[0, 0, n]].astype(f32)
        dr, di = rows[:, :NMIN], rows[:, NMIN:]
        wr, wi = turned[n, :, :NMIN], turned[n, :, NMIN:]
        z_out[n] = jnp.concatenate([dr * wr - di * wi, dr * wi + di * wr], axis=1).astype(bf16)
        return carry

    lax.fori_loop(0, n_trig, filtered, 0, unroll=16)

    some = data4.at[pl.ds(0, 2 * n_data)]
    pltpu.make_async_copy(some, some, data_send.at[0]).wait()
    some = tmpl4.at[pl.ds(0, 2 * (n_blk - 1) * hk)]
    pltpu.make_async_copy(some, some, tmpl_send.at[0]).wait()
    some = cuts.at[pl.ds(0, n_blk - 1)]
    pltpu.make_async_copy(some, some, cuts_send.at[0]).wait()


def chi_kernel(z_in, hot_in, between_in, keep_in, spin_in, rnorm_in, fixed, peak_in, peak_out, chi_out, chi_rows, sem):
    f32, bf16 = jnp.float32, jnp.bfloat16
    n_grp = hot_in.shape[0]
    n_fixed = NMAJ * GROUP
    save_peak = pltpu.make_async_copy(peak_in, peak_out, sem.at[0])
    save_peak.start()
    at = lax.broadcasted_iota(jnp.int32, (GROUP * NCUT, NMIN), 1)
    row = lax.broadcasted_iota(jnp.int32, (GROUP * NCUT, NMIN), 0)
    step = ((at == row).astype(f32) - (at == row - GROUP).astype(f32)).astype(bf16)
    own_rows = lax.broadcasted_iota(jnp.int32, (2 * GROUP, NMIN), 0)
    whole = (lax.broadcasted_iota(jnp.int32, (2 * GROUP, NMIN), 1) // NMAJ == own_rows).astype(f32).astype(bf16)
    whole = jnp.concatenate([whole, jnp.zeros_like(whole)], axis=1)
    own_turn = fixed[n_fixed:2 * n_fixed, :].astype(f32)

    def rotate(v, w):
        vr, vi, wr, wi = v[:, :NMIN], v[:, NMIN:], w[:, :NMIN], w[:, NMIN:]
        return jnp.concatenate([vr * wr - vi * wi, vr * wi + vi * wr], axis=1).astype(bf16)

    def one_batch(t):
        rows = GROUP * NMAJ
        qs = [t * BATCH + i for i in range(BATCH)]
        zs = [z_in[pl.ds(q * GROUP, GROUP)].reshape(rows, 2 * NMIN) for q in qs]
        picks = [jnp.dot(hot_in[q], z, preferred_element_type=f32) for q, z in zip(qs, zs)]
        parts = []
        for q, pick in zip(qs, picks):
            keep = keep_in[q]
            parts.append(pick.astype(bf16) * jnp.concatenate([keep, keep], axis=1))
        moved = [jnp.dot(jnp.concatenate([z, part], axis=0), fixed[2 * n_fixed:, :], preferred_element_type=f32) for z, part in zip(zs, parts)]
        turned = [jnp.concatenate([rotate(m[:rows], own_turn), rotate(m[rows:], spin_in[q])], axis=0) for q, m in zip(qs, moved)]
        bins = []
        for q, turn in zip(qs, turned):
            mix = jnp.concatenate([jnp.concatenate([between_in[q], step], axis=1), whole], axis=0)
            bins.append(jnp.dot(mix, turn, preferred_element_type=f32))
        for q, bn in zip(qs, bins):
            br, bi = bn[:rows, :NMIN], bn[:rows, NMIN:]
            energy = jnp.sum((br * br + bi * bi).reshape(NCUT, GROUP, NMIN), axis=0)
            tr, ti = bn[rows:rows + GROUP, :NMIN], bn[rows:rows + GROUP, NMIN:]
            loud = tr * tr + ti * ti
            at_q = q * GROUP
            rnorm = rnorm_in[pl.ds(at_q, GROUP), :]
            reduced = jnp.maximum(energy - loud * (1.0 / NCUT), 0.0) * (NCUT / (2.0 * NCUT - 2.0)) * rnorm
            rho = jnp.sqrt(loud * rnorm)
            bend = jnp.exp(jnp.log((1.0 + reduced * reduced * reduced) * 0.5) * (-1.0 / 6.0))
            chi_rows[pl.ds(at_q, GROUP), :] = jnp.where(reduced > 1.0, rho * bend, rho)

    saves = []
    for t in range(n_grp // BATCH):
        one_batch(t)
        part = pl.ds(t * BATCH * GROUP, BATCH * GROUP)
        saves.append(pltpu.make_async_copy(chi_rows.at[part], chi_out.at[0, 0, part], sem.at[1 + t]))
        saves[-1].start()
    save_peak.wait()
    for save in saves:
        save.wait()


def fused(sizes, ids_k, ids_p, ids_t, own, tmpl, cuts, tables):
    n_blk, n_det, n_sub = sizes
    fixed, second, wide = tables
    n_tmpl = n_blk * tmpl.shape[0]
    n_trig = ids_k.shape[-1]
    n_grp = n_trig // GROUP
    hbm = pl.BlockSpec(memory_space=pltpu.HBM)
    vmem = pl.BlockSpec(memory_space=pltpu.VMEM)
    dma = pltpu.SemaphoreType.DMA
    f32, bf16 = jnp.float32, jnp.bfloat16
    n_half = second.shape[1] // 2
    peak_shape = (own.shape[0], n_half * NMAJ)
    rows = GROUP * NCUT
    made = [
        (peak_shape, f32),
        ((n_trig, NMAJ, 2 * NMIN), bf16),
        ((n_grp, rows, NMIN), bf16),
        ((n_grp, rows, NMIN), bf16),
        ((n_grp, rows, NMIN), bf16),
        ((n_grp, rows, 2 * NMIN), f32),
        ((n_trig, NMIN), f32),
        (fixed.shape, fixed.dtype),
    ]
    scratch = [
        pltpu.VMEM((n_blk * n_det * own.shape[0],) + own.shape[1:], own.dtype),
        pltpu.VMEM((n_tmpl,) + tmpl.shape[1:], tmpl.dtype),
        pltpu.VMEM((n_blk,) + cuts.shape, cuts.dtype),
    ]
    scratch += [pltpu.SMEM(ids_k.shape, jnp.int32)] * 3
    scratch += [
        pltpu.VMEM(ids_k.shape, jnp.int32),
        pltpu.VMEM(second.shape[1:], second.dtype),
        pltpu.VMEM(wide.shape, wide.dtype),
        pltpu.VMEM((n_tmpl, NMIN), f32),
        pltpu.VMEM((n_tmpl, 1, NMIN), f32),
        pltpu.VMEM((n_trig, NMAJ, 2 * NMIN), f32),
        dma((10,)), dma((1,)), dma((1,)), dma((1,)), dma((1,)),
        dma((n_blk - 1,)), dma((n_blk - 1,)), dma((n_det - 1,)), dma((2, n_blk - 1)),
        dma((n_blk - 1, n_det - 1)), dma((n_blk - 1, n_det - 1)), dma((1,)),
        pltpu.SemaphoreType.REGULAR((n_blk - 1,)), pltpu.SemaphoreType.REGULAR((n_det - 1,)),
        pltpu.SemaphoreType.REGULAR((1,)),
    ]
    made_refs = pl.pallas_call(
        functools.partial(gather_kernel, n_blk, n_det, n_sub),
        out_shape=[pltpu.VMEM(shape, dtype) for shape, dtype in made],
        in_specs=[hbm] * 9,
        out_specs=[vmem] * len(made),
        scratch_shapes=scratch,
        compiler_params=pltpu.CompilerParams(
            collective_id=0, has_side_effects=True, vmem_limit_bytes=32 * 1024 * 1024
        ),
        name="gather_and_peak",
    )(*(pltpu.with_memory_space_constraint(x, pltpu.HBM)
        for x in (ids_k, ids_p, ids_t, own, tmpl, cuts, fixed, second, wide)))
    return pl.pallas_call(
        chi_kernel,
        out_shape=(
            jax.ShapeDtypeStruct(peak_shape, f32),
            jax.ShapeDtypeStruct(ids_k.shape + (STEPS * NMAJ,), f32),
        ),
        in_specs=[vmem] * len(made),
        out_specs=(hbm, hbm),
        scratch_shapes=[pltpu.VMEM((n_trig, STEPS * NMAJ), f32), dma((1 + n_grp // BATCH,))],
        compiler_params=pltpu.CompilerParams(vmem_limit_bytes=24 * 1024 * 1024),
        name="chi",
    )(*made_refs[1:], made_refs[0])


def body(sizes, data, templates, bin_cuts, trig_template, trig_pair, trig_tile):
    tables = tuple(jnp.asarray(t) for t in host_tables(sizes[2]))
    peak, chi = fused(sizes, trig_template, trig_pair, trig_tile, data, templates, bin_cuts, tables)
    return peak, chi


def solution(mesh):
    sizes = (mesh.shape["blk"], mesh.shape["det"], mesh.shape["sub"])
    return jax.shard_map(
        functools.partial(body, sizes),
        mesh=mesh,
        in_specs=(
            P(("groups", "blk", "det"), None, None),
            P(("groups", "blk"), None, None),
            P(("groups", "blk"), None),
            P(("groups", "blk", "det"), "sub", None),
            P(("groups", "blk", "det"), "sub", None),
            P(("groups", "blk", "det"), "sub", None),
        ),
        out_specs=(
            P(("groups", "blk", "det"), "sub"),
            P(("groups", "blk", "det"), "sub", None, None),
        ),
        check_vma=False,
    )
```

```python
import functools
import math

import jax
import jax.numpy as jnp
import numpy as np
from jax import lax
from jax.experimental import pallas as pl
from jax.experimental.pallas import tpu as pltpu
from jax.sharding import PartitionSpec as P

MESH = pl.DeviceIdType.MESH
NMAJ = 16
NMIN = 128
NCUT = 16
STEPS = 8
GROUP = 8
BATCH = 8
PRE = 2


def unit_circle(index, period):
    angle = (index % period) * (2.0 * math.pi / period)
    return np.cos(angle), np.sin(angle)


def host_tables(n_sub):
    bf16 = jnp.bfloat16
    major = np.arange(NMAJ)
    minor = np.arange(NMIN)
    cos16, sin16 = unit_circle(major[:, None] * major[None, :], NMAJ)
    eye = np.eye(GROUP)
    first = np.concatenate([np.kron(eye, cos16), np.kron(eye, sin16)], axis=1).astype(bf16)
    twc, tws = unit_circle(major[:, None] * minor[None, :], NMAJ * NMIN)
    twiddle = np.concatenate([twc, tws], axis=1).astype(np.float32)
    n_half = NMIN // n_sub
    second = []
    for half in range(n_sub):
        steps = half * n_half + np.arange(n_half)
        cosine, sine = unit_circle(steps[:, None] * minor[None, :], NMIN)
        real_rows = np.concatenate([cosine, -sine], axis=1)
        imag_rows = np.concatenate([sine, cosine], axis=1)
        second.append(np.concatenate([real_rows, imag_rows], axis=0))
    second = np.stack(second).astype(bf16)
    times = np.arange(NMAJ * STEPS)
    cosine, sine = unit_circle(minor[:, None] * times[None, :], NMAJ * NMIN)
    tile_dft = np.concatenate(
        [np.concatenate([cosine, sine], axis=1), np.concatenate([-sine, cosine], axis=1)], axis=0
    ).astype(bf16)
    rowc, rows = unit_circle(major[:, None] * (times % NMAJ)[None, :], NMAJ)
    row_phase = np.tile(np.concatenate([rowc, rows], axis=1), (GROUP, 1)).astype(bf16)
    starts = np.arange(NMIN // STEPS) * STEPS
    phc, phs = unit_circle(starts[:, None] * minor[None, :], NMIN)
    tile_phase = np.concatenate([phc, phs], axis=1).astype(np.float32)[:, None, :]
    fixed = np.concatenate([first, row_phase, tile_dft], axis=0)
    wide = np.concatenate([twiddle[:, None, :], tile_phase], axis=0)
    return fixed, second, wide


def swap_blocks(x):
    sub = lax.broadcasted_iota(jnp.int32, x.shape, 0)
    grp = lax.broadcasted_iota(jnp.int32, x.shape, 1) // NMAJ
    rows, lanes = x.shape
    for bit in (1, 2, 4):
        up = pltpu.roll(pltpu.roll(x, rows - bit, 0), NMAJ * bit, 1)
        down = pltpu.roll(pltpu.roll(x, bit, 0), lanes - NMAJ * bit, 1)
        sb, gb = (sub & bit) != 0, (grp & bit) != 0
        x = jnp.where(jnp.logical_and(jnp.logical_not(sb), gb), up,
                      jnp.where(jnp.logical_and(sb, jnp.logical_not(gb)), down, x))
    return x


def conj_product(data, tmpl):
    dr, di = data[..., :NMIN], data[..., NMIN:]
    tr, ti = tmpl[..., :NMIN], tmpl[..., NMIN:]
    return dr * tr + di * ti, di * tr - dr * ti


def gather_kernel(n_blk, n_det, n_sub, *refs):
    (ids_k_in, ids_p_in, ids_t_in, own_in, tmpl_in, cuts_in, fixed_in, second_in, wide_in,
     peak_out, z_out, hot_out, between_out, keep_out, spin_out, rnorm_out, fixed,
     data4, tmpl4, cuts, ids_k, ids_p, ids_t, ids_v, second, wide_tab, cut_rows, norm_tab, turned,
     local_sem, data_send, tmpl_send, cuts_send, cuts_recv, t_recv, ts_recv, x_recv, z_recv, zx_recv,
     xz_recv, s_recv, blk_in, det_in, sub_in) = refs
    f32, bf16 = jnp.float32, jnp.bfloat16
    b = lax.axis_index("blk")
    d = lax.axis_index("det")
    half = lax.axis_index("sub")
    other = n_sub - 1 - half
    pairs = own_in.shape[0]
    kb = tmpl_in.shape[0]
    n_cut = cuts_in.shape[1]
    n_tmpl = n_blk * kb
    n_trig = ids_k_in.shape[2]
    n_grp = n_trig // GROUP
    hp, hk = pairs // n_sub, kb // n_sub
    ha = hp // 2
    own = b * n_det + d
    early, late = (0, ha), (ha, hp - ha)

    moves = [(own_in, data4.at[pl.ds(own * pairs, pairs)]), (tmpl_in, tmpl4.at[pl.ds(b * kb, kb)]),
             (cuts_in, cuts.at[b]), (fixed_in, fixed), (wide_in, wide_tab), (second_in.at[half], second),
             (ids_k_in, ids_k), (ids_p_in, ids_p), (ids_t_in, ids_t), (ids_k_in, ids_v)]
    fetches = [pltpu.make_async_copy(src, dst, local_sem.at[i]) for i, (src, dst) in enumerate(moves)]
    for copy in fetches[:3]:
        copy.start()

    barrier = pltpu.get_barrier_semaphore()

    def tell(sem, where):
        pl.semaphore_signal(sem, inc=1, device_id=where, device_id_type=MESH)

    for q in range(n_blk - 1, 0, -1):
        pl.when(b < q)(functools.partial(tell, barrier, {"blk": q}))
    for c in range(n_det - 1, 0, -1):
        pl.when(d < c)(functools.partial(tell, barrier, {"det": c}))
    pl.when(half == n_sub - 1)(functools.partial(tell, barrier, {"sub": other}))
    lower = b + d + (n_sub - 1 - half)
    pl.when(lower > 0)(lambda: pl.semaphore_wait(barrier, lower))
    for q in range(n_blk - 1):
        pl.when(b > q)(functools.partial(tell, blk_in.at[lax.rem(b - q - 1 + n_blk, n_blk)], {"blk": q}))
    for c in range(n_det - 1):
        pl.when(d > c)(functools.partial(tell, det_in.at[lax.rem(d - c - 1 + n_det, n_det)], {"det": c}))
    pl.when(half == 0)(functools.partial(tell, sub_in.at[0], {"sub": other}))
    for copy in fetches[3:]:
        copy.start()

    def remote(ref, send, recv, where):
        pltpu.make_async_remote_copy(src_ref=ref, dst_ref=ref, send_sem=send.at[0], recv_sem=recv,
                                     device_id=where, device_id_type=MESH).start()

    def arrived(ref, sem):
        pltpu.make_async_copy(ref, ref, sem).wait()

    def data_part(place, first, count):
        return data4.at[pl.ds(place * pairs + half * hp + first, count)]

    def tmpl_part(place):
        return tmpl4.at[pl.ds(place * kb + half * hk, hk)]

    def column(dx):
        return lax.rem(d + dx, n_det)

    def other_half(place):
        remote(data_part(place, 0, hp), data_send, s_recv.at[0], {"sub": other})

    peers = []
    for i in range(n_blk - 1):
        higher = (i + n_blk - b) // n_blk
        q = i + higher
        peers.append((q, higher, lax.rem(q - b - 1 + n_blk, n_blk), lax.rem(b - q - 1 + n_blk, n_blk)))

    def remote_own(first, count, recv, where):
        pltpu.make_async_remote_copy(src_ref=own_in.at[pl.ds(half * hp + first, count)],
                                     dst_ref=data_part(own, first, count), send_sem=data_send.at[0], recv_sem=recv,
                                     device_id=where, device_id_type=MESH).start()

    def send_x(dx):
        remote_own(0, hp, x_recv.at[n_det - 1 - dx], {"det": column(dx)})

    def send_z(q, there):
        where = {"blk": q}
        pltpu.make_async_remote_copy(src_ref=tmpl_in.at[pl.ds(half * hk + 0, hk)], dst_ref=tmpl_part(b),
                                     send_sem=tmpl_send.at[0], recv_sem=t_recv.at[there],
                                     device_id=where, device_id_type=MESH).start()
        remote_own(*early, z_recv.at[0, there], where)
        remote_own(*late, z_recv.at[1, there], where)
        pltpu.make_async_remote_copy(src_ref=cuts_in, dst_ref=cuts.at[b], send_sem=cuts_send.at[0],
                                     recv_sem=cuts_recv.at[0], device_id=where, device_id_type=MESH).start()

    for dx in range(1, n_det):
        pl.when(column(dx) < d)(functools.partial(send_x, dx))
    for q, higher, here, there in peers:
        pl.when(higher == 0)(functools.partial(send_z, q, there))
    for copy in fetches:
        copy.wait()

    n_fixed = NMAJ * GROUP
    wide = data4[pl.ds(own * pairs, pairs)].astype(f32)
    twiddle = wide_tab[:NMAJ].reshape(NMAJ, 2 * NMIN)
    twc = jnp.broadcast_to(twiddle[:, :NMIN][None], (pairs, NMAJ, NMIN)).reshape(pairs * NMAJ, NMIN)
    tws = jnp.broadcast_to(twiddle[:, NMIN:][None], (pairs, NMAJ, NMIN)).reshape(pairs * NMAJ, NMIN)
    n_half = second.shape[0] // 2

    def peak_of(src_b, peak):
        norms, stacks, bents = [], [], []
        for k in range(kb):
            row = tmpl4[src_b * kb + k].astype(f32)
            norm = jnp.sum(jnp.sum(row * row, axis=0, keepdims=True), axis=1, keepdims=True)
            norm_tab[src_b * kb + k] = jnp.broadcast_to(norm, (1, NMIN))
            norms.append(norm)
            real, imag = conj_product(wide, row[None])
            real = real.reshape(pairs * NMAJ, NMIN).astype(bf16)
            imag = imag.reshape(pairs * NMAJ, NMIN).astype(bf16)
            stacks.append(jnp.concatenate(
                [jnp.concatenate([real, imag], axis=1), jnp.concatenate([-imag, real], axis=1)], axis=0
            ))
        sections = [jnp.dot(fixed[:n_fixed, :], stack, preferred_element_type=f32) for stack in stacks]
        for section in sections:
            sr, si = section[:, :NMIN], section[:, NMIN:]
            bents.append(jnp.concatenate([sr * twc - si * tws, sr * tws + si * twc], axis=1).astype(bf16))
        snrs = [lax.dot_general(second[...], bent, (((1,), (1,)), ((), ())), preferred_element_type=f32)
                for bent in bents]
        for snr, norm in zip(snrs, norms):
            power = snr[:n_half] * snr[:n_half] + snr[n_half:] * snr[n_half:]
            peak = jnp.maximum(peak, power * (1.0 / norm))
        return peak

    peak = peak_of(b, jnp.zeros((n_half, pairs * NMAJ), f32))

    def answer_x(dx):
        pl.semaphore_wait(det_in.at[dx - 1], 1)
        send_x(dx)

    def answer_z(q, here, there):
        pl.semaphore_wait(blk_in.at[here], 1)
        send_z(q, there)

    for dx in range(1, n_det):
        pl.when(column(dx) > d)(functools.partial(answer_x, dx))
    for q, higher, here, there in peers:
        pl.when(higher == 1)(functools.partial(answer_z, q, here, there))
    pl.when(half == n_sub - 1)(lambda: pl.semaphore_wait(sub_in.at[0], 1))

    for dx in range(1, n_det):
        place = b * n_det + column(dx)
        arrived(data_part(place, 0, hp), x_recv.at[dx - 1])
        for q, higher, here, there in peers:
            remote(data_part(place, *late), data_send, xz_recv.at[there, dx - 1], {"blk": q})
        other_half(place)
    for q, higher, here, there in peers:
        arrived(tmpl_part(q), t_recv.at[here])
        remote(tmpl_part(q), tmpl_send, ts_recv.at[here], {"sub": other})
        arrived(data_part(q * n_det + d, *early), z_recv.at[0, here])
        for dx in range(1, n_det):
            remote(data_part(q * n_det + d, *early), data_send, zx_recv.at[here, n_det - 1 - dx], {"det": column(dx)})

    arrived(cuts.at[pl.ds(0, n_blk - 1)], cuts_recv.at[0])
    cut_rows[...] = jnp.zeros(cut_rows.shape, f32)
    cut_rows[:, NCUT - 1:NCUT] = jnp.full((n_tmpl, 1), NMAJ, f32)
    for blk in range(n_blk):
        cut_rows[blk * kb:(blk + 1) * kb, 0:n_cut] = (cuts[blk] >> 7).astype(f32)
        cut_rows[blk * kb:(blk + 1) * kb, 64:64 + n_cut] = (cuts[blk] & (NMIN - 1)).astype(f32)
    is_k = lax.broadcasted_iota(jnp.int32, (n_tmpl, n_trig), 0) == jnp.broadcast_to(ids_v[0], (n_tmpl, n_trig))
    pick_k = is_k.astype(f32).astype(bf16)

    def by_trigger(table):
        return lax.dot_general(pick_k, table, (((0,), (0,)), ((), ())), preferred_element_type=f32)

    trig_cuts = by_trigger(cut_rows[...].astype(bf16))
    lane = lax.broadcasted_iota(jnp.int32, (n_trig, NMIN), 1)
    spread = (
        (lax.broadcasted_iota(jnp.int32, (NMIN, 2 * NMIN), 0) < 64)
        == (lax.broadcasted_iota(jnp.int32, (NMIN, 2 * NMIN), 1) < NMIN)
    ).astype(f32).astype(bf16)
    base = ((lax.broadcasted_iota(jnp.int32, (n_trig, NMIN), 0) % GROUP) * NMAJ).astype(f32)
    at = lane.astype(f32)

    def cut_masks(first, count, last):
        spans = []
        for r in range(first, first + count):
            only = jnp.where((lane & 63) == r, trig_cuts, 0.0).astype(bf16)
            spans.append(jnp.dot(only, spread, preferred_element_type=f32))
        stacks = ([], [], [])
        for i, span in enumerate(spans):
            row = span[:, :NMIN] + base
            marks = (at == row, jnp.logical_and(at >= last, at < row), at < span[:, NMIN:])
            last = row
            for stack, mark in zip(stacks, marks):
                stack.append(mark.astype(f32).reshape(n_grp, GROUP, NMIN))
            if i % 2 == 1:
                rows = slice((first + i - 1) * GROUP, (first + i + 1) * GROUP)
                for stack, out in zip(stacks, (hot_out, between_out, keep_out)):
                    out[:, rows, :] = jnp.concatenate(stack[-2:], axis=1).astype(bf16)
        return last

    last = cut_masks(0, NCUT // 2, base)
    for q, higher, here, there in peers:
        arrived(data_part(q * n_det + d, *late), z_recv.at[1, here])
        other_half(q * n_det + d)
    cut_masks(NCUT // 2, NCUT // 2, last)
    for q in range(n_grp):
        spin_out[q] = jnp.dot(hot_out[q], fixed[n_fixed:2 * n_fixed, :], preferred_element_type=f32)

    def prepare(n, carry):
        k = ids_k[0, 0, n]
        row = tmpl4[k].astype(f32)
        phase = wide_tab[NMAJ + half * ((wide_tab.shape[0] - NMAJ) // n_sub) + ids_t[0, 0, n]]
        pc, ps = phase[:, :NMIN], phase[:, NMIN:]
        tr, ti = row[:, :NMIN], row[:, NMIN:]
        turned[n, :, :NMIN] = tr * pc + ti * ps
        turned[n, :, NMIN:] = tr * ps - ti * pc
        return carry

    def relayed():
        for q, higher, here, there in peers:
            for dx in range(1, n_det):
                place = q * n_det + column(dx)
                arrived(data_part(place, *late), xz_recv.at[here, dx - 1])
                arrived(data_part(place, *early), zx_recv.at[here, dx - 1])
                other_half(place)

    for i, (q, higher, here, there) in enumerate(peers):
        if i == PRE:
            relayed()
        arrived(tmpl4.at[pl.ds(q * kb + other * hk, hk)], ts_recv.at[here])
        peak = peak_of(q, peak)
    if len(peers) <= PRE:
        relayed()
    lax.fori_loop(0, n_trig, prepare, 0, unroll=16)

    rest = 1.0 / norm_tab[...].reshape(n_tmpl, NMIN)
    scale = jnp.zeros((n_trig, NMIN), f32)
    for _ in range(3):
        piece = rest.astype(bf16)
        rest = rest - piece.astype(f32)
        scale = scale + by_trigger(piece)
    rnorm_out[...] = scale

    swapped = swap_blocks(jnp.sqrt(peak))
    for u in range(n_half // 8):
        peak_out[:, u * 128:(u + 1) * 128] = swapped[8 * u:8 * u + 8, :]

    n_data = (n_blk * n_det - 1) * hp
    some = data4.at[pl.ds(0, n_data)]
    pltpu.make_async_copy(some, some, s_recv.at[0]).wait()

    def filtered(n, carry):
        rows = data4[ids_p[0, 0, n]].astype(f32)
        dr, di = rows[:, :NMIN], rows[:, NMIN:]
        wr, wi = turned[n, :, :NMIN], turned[n, :, NMIN:]
        z_out[n] = jnp.concatenate([dr * wr - di * wi, dr * wi + di * wr], axis=1).astype(bf16)
        return carry

    lax.fori_loop(0, n_trig, filtered, 0, unroll=16)

    some = data4.at[pl.ds(0, 2 * n_data)]
    pltpu.make_async_copy(some, some, data_send.at[0]).wait()
    some = tmpl4.at[pl.ds(0, 2 * (n_blk - 1) * hk)]
    pltpu.make_async_copy(some, some, tmpl_send.at[0]).wait()
    some = cuts.at[pl.ds(0, n_blk - 1)]
    pltpu.make_async_copy(some, some, cuts_send.at[0]).wait()


def chi_kernel(z_in, hot_in, between_in, keep_in, spin_in, rnorm_in, fixed, peak_in, peak_out, chi_out, chi_rows, sem):
    f32, bf16 = jnp.float32, jnp.bfloat16
    n_grp = hot_in.shape[0]
    n_fixed = NMAJ * GROUP
    save_peak = pltpu.make_async_copy(peak_in, peak_out, sem.at[0])
    save_peak.start()
    at = lax.broadcasted_iota(jnp.int32, (GROUP * NCUT, NMIN), 1)
    row = lax.broadcasted_iota(jnp.int32, (GROUP * NCUT, NMIN), 0)
    step = ((at == row).astype(f32) - (at == row - GROUP).astype(f32)).astype(bf16)
    own_rows = lax.broadcasted_iota(jnp.int32, (2 * GROUP, NMIN), 0)
    whole = (lax.broadcasted_iota(jnp.int32, (2 * GROUP, NMIN), 1) // NMAJ == own_rows).astype(f32).astype(bf16)
    whole = jnp.concatenate([whole, jnp.zeros_like(whole)], axis=1)
    own_turn = fixed[n_fixed:2 * n_fixed, :].astype(f32)

    def rotate(v, w):
        vr, vi, wr, wi = v[:, :NMIN], v[:, NMIN:], w[:, :NMIN], w[:, NMIN:]
        return jnp.concatenate([vr * wr - vi * wi, vr * wi + vi * wr], axis=1).astype(bf16)

    def one_batch(t):
        rows = GROUP * NMAJ
        qs = [t * BATCH + i for i in range(BATCH)]
        zs = [z_in[pl.ds(q * GROUP, GROUP)].reshape(rows, 2 * NMIN) for q in qs]
        picks = [jnp.dot(hot_in[q], z, preferred_element_type=f32) for q, z in zip(qs, zs)]
        parts = []
        for q, pick in zip(qs, picks):
            keep = keep_in[q]
            parts.append(pick.astype(bf16) * jnp.concatenate([keep, keep], axis=1))
        moved = [jnp.dot(jnp.concatenate([z, part], axis=0), fixed[2 * n_fixed:, :], preferred_element_type=f32) for z, part in zip(zs, parts)]
        turned = [jnp.concatenate([rotate(m[:rows], own_turn), rotate(m[rows:], spin_in[q])], axis=0) for q, m in zip(qs, moved)]
        bins = []
        for q, turn in zip(qs, turned):
            mix = jnp.concatenate([jnp.concatenate([between_in[q], step], axis=1), whole], axis=0)
            bins.append(jnp.dot(mix, turn, preferred_element_type=f32))
        for q, bn in zip(qs, bins):
            br, bi = bn[:rows, :NMIN], bn[:rows, NMIN:]
            energy = jnp.sum((br * br + bi * bi).reshape(NCUT, GROUP, NMIN), axis=0)
            tr, ti = bn[rows:rows + GROUP, :NMIN], bn[rows:rows + GROUP, NMIN:]
            loud = tr * tr + ti * ti
            at_q = q * GROUP
            rnorm = rnorm_in[pl.ds(at_q, GROUP), :]
            reduced = jnp.maximum(energy - loud * (1.0 / NCUT), 0.0) * (NCUT / (2.0 * NCUT - 2.0)) * rnorm
            rho = jnp.sqrt(loud * rnorm)
            bend = jnp.exp(jnp.log((1.0 + reduced * reduced * reduced) * 0.5) * (-1.0 / 6.0))
            chi_rows[pl.ds(at_q, GROUP), :] = jnp.where(reduced > 1.0, rho * bend, rho)

    saves = []
    for t in range(n_grp // BATCH):
        one_batch(t)
        part = pl.ds(t * BATCH * GROUP, BATCH * GROUP)
        saves.append(pltpu.make_async_copy(chi_rows.at[part], chi_out.at[0, 0, part], sem.at[1 + t]))
        saves[-1].start()
    save_peak.wait()
    for save in saves:
        save.wait()


def fused(sizes, ids_k, ids_p, ids_t, own, tmpl, cuts, tables):
    n_blk, n_det, n_sub = sizes
    fixed, second, wide = tables
    n_tmpl = n_blk * tmpl.shape[0]
    n_trig = ids_k.shape[-1]
    n_grp = n_trig // GROUP
    hbm = pl.BlockSpec(memory_space=pltpu.HBM)
    vmem = pl.BlockSpec(memory_space=pltpu.VMEM)
    dma = pltpu.SemaphoreType.DMA
    f32, bf16 = jnp.float32, jnp.bfloat16
    n_half = second.shape[1] // 2
    peak_shape = (own.shape[0], n_half * NMAJ)
    rows = GROUP * NCUT
    made = [
        (peak_shape, f32),
        ((n_trig, NMAJ, 2 * NMIN), bf16),
        ((n_grp, rows, NMIN), bf16),
        ((n_grp, rows, NMIN), bf16),
        ((n_grp, rows, NMIN), bf16),
        ((n_grp, rows, 2 * NMIN), f32),
        ((n_trig, NMIN), f32),
        (fixed.shape, fixed.dtype),
    ]
    scratch = [
        pltpu.VMEM((n_blk * n_det * own.shape[0],) + own.shape[1:], own.dtype),
        pltpu.VMEM((n_tmpl,) + tmpl.shape[1:], tmpl.dtype),
        pltpu.VMEM((n_blk,) + cuts.shape, cuts.dtype),
    ]
    scratch += [pltpu.SMEM(ids_k.shape, jnp.int32)] * 3
    scratch += [
        pltpu.VMEM(ids_k.shape, jnp.int32),
        pltpu.VMEM(second.shape[1:], second.dtype),
        pltpu.VMEM(wide.shape, wide.dtype),
        pltpu.VMEM((n_tmpl, NMIN), f32),
        pltpu.VMEM((n_tmpl, 1, NMIN), f32),
        pltpu.VMEM((n_trig, NMAJ, 2 * NMIN), f32),
        dma((10,)), dma((1,)), dma((1,)), dma((1,)), dma((1,)),
        dma((n_blk - 1,)), dma((n_blk - 1,)), dma((n_det - 1,)), dma((2, n_blk - 1)),
        dma((n_blk - 1, n_det - 1)), dma((n_blk - 1, n_det - 1)), dma((1,)),
        pltpu.SemaphoreType.REGULAR((n_blk - 1,)), pltpu.SemaphoreType.REGULAR((n_det - 1,)),
        pltpu.SemaphoreType.REGULAR((1,)),
    ]
    made_refs = pl.pallas_call(
        functools.partial(gather_kernel, n_blk, n_det, n_sub),
        out_shape=[pltpu.VMEM(shape, dtype) for shape, dtype in made],
        in_specs=[hbm] * 9,
        out_specs=[vmem] * len(made),
        scratch_shapes=scratch,
        compiler_params=pltpu.CompilerParams(
            collective_id=0, has_side_effects=True, vmem_limit_bytes=32 * 1024 * 1024
        ),
        name="gather_and_peak",
    )(*(pltpu.with_memory_space_constraint(x, pltpu.HBM)
        for x in (ids_k, ids_p, ids_t, own, tmpl, cuts, fixed, second, wide)))
    return pl.pallas_call(
        chi_kernel,
        out_shape=(
            jax.ShapeDtypeStruct(peak_shape, f32),
            jax.ShapeDtypeStruct(ids_k.shape + (STEPS * NMAJ,), f32),
        ),
        in_specs=[vmem] * len(made),
        out_specs=(hbm, hbm),
        scratch_shapes=[pltpu.VMEM((n_trig, STEPS * NMAJ), f32), dma((1 + n_grp // BATCH,))],
        compiler_params=pltpu.CompilerParams(vmem_limit_bytes=24 * 1024 * 1024),
        name="chi",
    )(*made_refs[1:], made_refs[0])


def body(sizes, data, templates, bin_cuts, trig_template, trig_pair, trig_tile):
    tables = tuple(jnp.asarray(t) for t in host_tables(sizes[2]))
    peak, chi = fused(sizes, trig_template, trig_pair, trig_tile, data, templates, bin_cuts, tables)
    return peak, chi


def solution(mesh):
    sizes = (mesh.shape["blk"], mesh.shape["det"], mesh.shape["sub"])
    return jax.shard_map(
        functools.partial(body, sizes),
        mesh=mesh,
        in_specs=(
            P(("groups", "blk", "det"), None, None),
            P(("groups", "blk"), None, None),
            P(("groups", "blk"), None),
            P(("groups", "blk", "det"), "sub", None),
            P(("groups", "blk", "det"), "sub", None),
            P(("groups", "blk", "det"), "sub", None),
        ),
        out_specs=(
            P(("groups", "blk", "det"), "sub"),
            P(("groups", "blk", "det"), "sub", None, None),
        ),
        check_vma=False,
    )
```

```python
import functools
import math

import jax
import jax.numpy as jnp
import numpy as np
from jax import lax
from jax.experimental import pallas as pl
from jax.experimental.pallas import tpu as pltpu
from jax.sharding import PartitionSpec as P

MESH = pl.DeviceIdType.MESH
NMAJ = 16
NMIN = 128
NCUT = 16
STEPS = 8
GROUP = 8
BATCH = 8
PRE = 1


def unit_circle(index, period):
    angle = (index % period) * (2.0 * math.pi / period)
    return np.cos(angle), np.sin(angle)


def host_tables(n_sub):
    bf16 = jnp.bfloat16
    major = np.arange(NMAJ)
    minor = np.arange(NMIN)
    cos16, sin16 = unit_circle(major[:, None] * major[None, :], NMAJ)
    eye = np.eye(GROUP)
    first = np.concatenate([np.kron(eye, cos16), np.kron(eye, sin16)], axis=1).astype(bf16)
    twc, tws = unit_circle(major[:, None] * minor[None, :], NMAJ * NMIN)
    twiddle = np.concatenate([twc, tws], axis=1).astype(np.float32)
    n_half = NMIN // n_sub
    second = []
    for half in range(n_sub):
        steps = half * n_half + np.arange(n_half)
        cosine, sine = unit_circle(steps[:, None] * minor[None, :], NMIN)
        real_rows = np.concatenate([cosine, -sine], axis=1)
        imag_rows = np.concatenate([sine, cosine], axis=1)
        second.append(np.concatenate([real_rows, imag_rows], axis=0))
    second = np.stack(second).astype(bf16)
    times = np.arange(NMAJ * STEPS)
    cosine, sine = unit_circle(minor[:, None] * times[None, :], NMAJ * NMIN)
    tile_dft = np.concatenate(
        [np.concatenate([cosine, sine], axis=1), np.concatenate([-sine, cosine], axis=1)], axis=0
    ).astype(bf16)
    rowc, rows = unit_circle(major[:, None] * (times % NMAJ)[None, :], NMAJ)
    row_phase = np.tile(np.concatenate([rowc, rows], axis=1), (GROUP, 1)).astype(bf16)
    starts = np.arange(NMIN // STEPS) * STEPS
    phc, phs = unit_circle(starts[:, None] * minor[None, :], NMIN)
    tile_phase = np.concatenate([phc, phs], axis=1).astype(np.float32)[:, None, :]
    fixed = np.concatenate([first, row_phase, tile_dft], axis=0)
    wide = np.concatenate([twiddle[:, None, :], tile_phase], axis=0)
    return fixed, second, wide


def swap_blocks(x):
    sub = lax.broadcasted_iota(jnp.int32, x.shape, 0)
    grp = lax.broadcasted_iota(jnp.int32, x.shape, 1) // NMAJ
    rows, lanes = x.shape
    for bit in (1, 2, 4):
        up = pltpu.roll(pltpu.roll(x, rows - bit, 0), NMAJ * bit, 1)
        down = pltpu.roll(pltpu.roll(x, bit, 0), lanes - NMAJ * bit, 1)
        sb, gb = (sub & bit) != 0, (grp & bit) != 0
        x = jnp.where(jnp.logical_and(jnp.logical_not(sb), gb), up,
                      jnp.where(jnp.logical_and(sb, jnp.logical_not(gb)), down, x))
    return x


def conj_product(data, tmpl):
    dr, di = data[..., :NMIN], data[..., NMIN:]
    tr, ti = tmpl[..., :NMIN], tmpl[..., NMIN:]
    return dr * tr + di * ti, di * tr - dr * ti


def gather_kernel(n_blk, n_det, n_sub, *refs):
    (ids_k_in, ids_p_in, ids_t_in, own_in, tmpl_in, cuts_in, fixed_in, second_in, wide_in,
     peak_out, z_out, hot_out, between_out, keep_out, spin_out, rnorm_out, fixed,
     data4, tmpl4, cuts, ids_k, ids_p, ids_t, ids_v, second, wide_tab, cut_rows, norm_tab, turned,
     local_sem, data_send, tmpl_send, cuts_send, cuts_recv, t_recv, ts_recv, x_recv, z_recv, zx_recv,
     xz_recv, cross_recv, s_recv, blk_in, det_in, sub_in) = refs
    f32, bf16 = jnp.float32, jnp.bfloat16
    b = lax.axis_index("blk")
    d = lax.axis_index("det")
    half = lax.axis_index("sub")
    other = n_sub - 1 - half
    pairs = own_in.shape[0]
    kb = tmpl_in.shape[0]
    n_cut = cuts_in.shape[1]
    n_tmpl = n_blk * kb
    n_trig = ids_k_in.shape[2]
    n_grp = n_trig // GROUP
    hp, hk = pairs // n_sub, kb // n_sub
    ha = hp // 2
    own = b * n_det + d
    early, late = (0, ha), (ha, hp - ha)

    moves = [(own_in, data4.at[pl.ds(own * pairs, pairs)]), (tmpl_in, tmpl4.at[pl.ds(b * kb, kb)]),
             (cuts_in, cuts.at[b]), (fixed_in, fixed), (wide_in, wide_tab), (second_in.at[half], second),
             (ids_k_in, ids_k), (ids_p_in, ids_p), (ids_t_in, ids_t), (ids_k_in, ids_v)]
    fetches = [pltpu.make_async_copy(src, dst, local_sem.at[i]) for i, (src, dst) in enumerate(moves)]
    for copy in fetches[:3]:
        copy.start()

    barrier = pltpu.get_barrier_semaphore()

    def tell(sem, where):
        pl.semaphore_signal(sem, inc=1, device_id=where, device_id_type=MESH)

    for q in range(n_blk - 1, 0, -1):
        pl.when(b < q)(functools.partial(tell, barrier, {"blk": q}))
    for c in range(n_det - 1, 0, -1):
        for core in range(n_sub):
            pl.when(d < c)(functools.partial(tell, barrier, {"det": c, "sub": core}))
    pl.when(half == n_sub - 1)(functools.partial(tell, barrier, {"sub": other}))
    lower = b + d * n_sub + (n_sub - 1 - half)
    pl.when(lower > 0)(lambda: pl.semaphore_wait(barrier, lower))
    for q in range(n_blk - 1):
        pl.when(b > q)(functools.partial(tell, blk_in.at[lax.rem(b - q - 1 + n_blk, n_blk)], {"blk": q}))
    for c in range(n_det - 1):
        for core in range(n_sub):
            slot = (lax.rem(d - c - 1 + n_det, n_det), lax.rem(half + core, n_sub))
            pl.when(d > c)(functools.partial(tell, det_in.at[slot], {"det": c, "sub": core}))
    pl.when(half == 0)(functools.partial(tell, sub_in.at[0], {"sub": other}))
    for copy in fetches[3:]:
        copy.start()

    def remote(ref, send, recv, where):
        pltpu.make_async_remote_copy(src_ref=ref, dst_ref=ref, send_sem=send.at[0], recv_sem=recv,
                                     device_id=where, device_id_type=MESH).start()

    def arrived(ref, sem):
        pltpu.make_async_copy(ref, ref, sem).wait()

    def data_part(place, first, count):
        return data4.at[pl.ds(place * pairs + half * hp + first, count)]

    def tmpl_part(place):
        return tmpl4.at[pl.ds(place * kb + half * hk, hk)]

    def column(dx):
        return lax.rem(d + dx, n_det)

    def other_half(place, first, count):
        remote(data_part(place, first, count), data_send, s_recv.at[0], {"sub": other})

    peers = []
    for i in range(n_blk - 1):
        higher = (i + n_blk - b) // n_blk
        q = i + higher
        peers.append((q, higher, lax.rem(q - b - 1 + n_blk, n_blk), lax.rem(b - q - 1 + n_blk, n_blk)))

    def remote_own(first, count, recv, where):
        pltpu.make_async_remote_copy(src_ref=own_in.at[pl.ds(half * hp + first, count)],
                                     dst_ref=data_part(own, first, count), send_sem=data_send.at[0], recv_sem=recv,
                                     device_id=where, device_id_type=MESH).start()

    def send_x(dx):
        remote_own(0, hp, x_recv.at[n_det - 1 - dx], {"det": column(dx)})

    def send_z(q, there):
        where = {"blk": q}
        pltpu.make_async_remote_copy(src_ref=tmpl_in.at[pl.ds(half * hk + 0, hk)], dst_ref=tmpl_part(b),
                                     send_sem=tmpl_send.at[0], recv_sem=t_recv.at[there],
                                     device_id=where, device_id_type=MESH).start()
        remote_own(*early, z_recv.at[0, there], where)
        remote_own(*late, z_recv.at[1, there], where)
        pltpu.make_async_remote_copy(src_ref=cuts_in, dst_ref=cuts.at[b], send_sem=cuts_send.at[0],
                                     recv_sem=cuts_recv.at[0], device_id=where, device_id_type=MESH).start()

    for dx in range(1, n_det):
        pl.when(column(dx) < d)(functools.partial(send_x, dx))
    for q, higher, here, there in peers:
        pl.when(higher == 0)(functools.partial(send_z, q, there))
    for copy in fetches:
        copy.wait()

    n_fixed = NMAJ * GROUP
    wide = data4[pl.ds(own * pairs, pairs)].astype(f32)
    twiddle = wide_tab[:NMAJ].reshape(NMAJ, 2 * NMIN)
    twc = jnp.broadcast_to(twiddle[:, :NMIN][None], (pairs, NMAJ, NMIN)).reshape(pairs * NMAJ, NMIN)
    tws = jnp.broadcast_to(twiddle[:, NMIN:][None], (pairs, NMAJ, NMIN)).reshape(pairs * NMAJ, NMIN)
    n_half = second.shape[0] // 2

    def peak_of(src_b, peak):
        norms, stacks, bents = [], [], []
        for k in range(kb):
            row = tmpl4[src_b * kb + k].astype(f32)
            norm = jnp.sum(jnp.sum(row * row, axis=0, keepdims=True), axis=1, keepdims=True)
            norm_tab[src_b * kb + k] = jnp.broadcast_to(norm, (1, NMIN))
            norms.append(norm)
            real, imag = conj_product(wide, row[None])
            real = real.reshape(pairs * NMAJ, NMIN).astype(bf16)
            imag = imag.reshape(pairs * NMAJ, NMIN).astype(bf16)
            stacks.append(jnp.concatenate(
                [jnp.concatenate([real, imag], axis=1), jnp.concatenate([-imag, real], axis=1)], axis=0
            ))
        sections = [jnp.dot(fixed[:n_fixed, :], stack, preferred_element_type=f32) for stack in stacks]
        for section in sections:
            sr, si = section[:, :NMIN], section[:, NMIN:]
            bents.append(jnp.concatenate([sr * twc - si * tws, sr * tws + si * twc], axis=1).astype(bf16))
        snrs = [lax.dot_general(second[...], bent, (((1,), (1,)), ((), ())), preferred_element_type=f32)
                for bent in bents]
        for snr, norm in zip(snrs, norms):
            power = snr[:n_half] * snr[:n_half] + snr[n_half:] * snr[n_half:]
            peak = jnp.maximum(peak, power * (1.0 / norm))
        return peak

    peak = peak_of(b, jnp.zeros((n_half, pairs * NMAJ), f32))

    def answer_x(dx):
        pl.semaphore_wait(det_in.at[dx - 1, 0], 1)
        send_x(dx)
        pl.semaphore_wait(det_in.at[dx - 1, 1], 1)

    def answer_z(q, here, there):
        pl.semaphore_wait(blk_in.at[here], 1)
        send_z(q, there)

    for dx in range(1, n_det):
        pl.when(column(dx) > d)(functools.partial(answer_x, dx))
    for q, higher, here, there in peers:
        pl.when(higher == 1)(functools.partial(answer_z, q, here, there))
    pl.when(half == n_sub - 1)(lambda: pl.semaphore_wait(sub_in.at[0], 1))

    for dx in range(1, n_det):
        place = b * n_det + column(dx)
        arrived(data_part(place, 0, hp), x_recv.at[dx - 1])
        for q, higher, here, there in peers:
            remote(data_part(place, *late), data_send, xz_recv.at[there, dx - 1], {"blk": q})
        other_half(place, 0, hp)
    for q, higher, here, there in peers:
        arrived(tmpl_part(q), t_recv.at[here])
        remote(tmpl_part(q), tmpl_send, ts_recv.at[here], {"sub": other})
        arrived(data_part(q * n_det + d, *early), z_recv.at[0, here])
        for dx in range(1, n_det):
            block = data_part(q * n_det + d, *early)
            remote(block, data_send, zx_recv.at[here, n_det - 1 - dx], {"det": column(dx)})
            remote(block, data_send, cross_recv.at[0], {"det": column(dx), "sub": other})

    arrived(cuts.at[pl.ds(0, n_blk - 1)], cuts_recv.at[0])
    cut_rows[...] = jnp.zeros(cut_rows.shape, f32)
    cut_rows[:, NCUT - 1:NCUT] = jnp.full((n_tmpl, 1), NMAJ, f32)
    for blk in range(n_blk):
        cut_rows[blk * kb:(blk + 1) * kb, 0:n_cut] = (cuts[blk] >> 7).astype(f32)
        cut_rows[blk * kb:(blk + 1) * kb, 64:64 + n_cut] = (cuts[blk] & (NMIN - 1)).astype(f32)
    is_k = lax.broadcasted_iota(jnp.int32, (n_tmpl, n_trig), 0) == jnp.broadcast_to(ids_v[0], (n_tmpl, n_trig))
    pick_k = is_k.astype(f32).astype(bf16)

    def by_trigger(table):
        return lax.dot_general(pick_k, table, (((0,), (0,)), ((), ())), preferred_element_type=f32)

    trig_cuts = by_trigger(cut_rows[...].astype(bf16))
    lane = lax.broadcasted_iota(jnp.int32, (n_trig, NMIN), 1)
    spread = (
        (lax.broadcasted_iota(jnp.int32, (NMIN, 2 * NMIN), 0) < 64)
        == (lax.broadcasted_iota(jnp.int32, (NMIN, 2 * NMIN), 1) < NMIN)
    ).astype(f32).astype(bf16)
    base = ((lax.broadcasted_iota(jnp.int32, (n_trig, NMIN), 0) % GROUP) * NMAJ).astype(f32)
    at = lane.astype(f32)

    def cut_masks(first, count, last):
        spans = []
        for r in range(first, first + count):
            only = jnp.where((lane & 63) == r, trig_cuts, 0.0).astype(bf16)
            spans.append(jnp.dot(only, spread, preferred_element_type=f32))
        stacks = ([], [], [])
        for i, span in enumerate(spans):
            row = span[:, :NMIN] + base
            marks = (at == row, jnp.logical_and(at >= last, at < row), at < span[:, NMIN:])
            last = row
            for stack, mark in zip(stacks, marks):
                stack.append(mark.astype(f32).reshape(n_grp, GROUP, NMIN))
            if i % 2 == 1:
                rows = slice((first + i - 1) * GROUP, (first + i + 1) * GROUP)
                for stack, out in zip(stacks, (hot_out, between_out, keep_out)):
                    out[:, rows, :] = jnp.concatenate(stack[-2:], axis=1).astype(bf16)
        return last

    last = cut_masks(0, NCUT // 2, base)
    for q, higher, here, there in peers:
        arrived(data_part(q * n_det + d, *late), z_recv.at[1, here])
        other_half(q * n_det + d, 0, hp)
    cut_masks(NCUT // 2, NCUT // 2, last)
    for q in range(n_grp):
        spin_out[q] = jnp.dot(hot_out[q], fixed[n_fixed:2 * n_fixed, :], preferred_element_type=f32)

    def prepare(n, carry):
        k = ids_k[0, 0, n]
        row = tmpl4[k].astype(f32)
        phase = wide_tab[NMAJ + half * ((wide_tab.shape[0] - NMAJ) // n_sub) + ids_t[0, 0, n]]
        pc, ps = phase[:, :NMIN], phase[:, NMIN:]
        tr, ti = row[:, :NMIN], row[:, NMIN:]
        turned[n, :, :NMIN] = tr * pc + ti * ps
        turned[n, :, NMIN:] = tr * ps - ti * pc
        return carry

    def relayed():
        for q, higher, here, there in peers:
            for dx in range(1, n_det):
                place = q * n_det + column(dx)
                arrived(data_part(place, *late), xz_recv.at[here, dx - 1])
                other_half(place, *late)

    for i, (q, higher, here, there) in enumerate(peers):
        if i == PRE:
            relayed()
        arrived(tmpl4.at[pl.ds(q * kb + other * hk, hk)], ts_recv.at[here])
        peak = peak_of(q, peak)
    if len(peers) <= PRE:
        relayed()
    lax.fori_loop(0, n_trig, prepare, 0, unroll=16)

    rest = 1.0 / norm_tab[...].reshape(n_tmpl, NMIN)
    scale = jnp.zeros((n_trig, NMIN), f32)
    for _ in range(3):
        piece = rest.astype(bf16)
        rest = rest - piece.astype(f32)
        scale = scale + by_trigger(piece)
    rnorm_out[...] = scale

    swapped = swap_blocks(jnp.sqrt(peak))
    for u in range(n_half // 8):
        peak_out[:, u * 128:(u + 1) * 128] = swapped[8 * u:8 * u + 8, :]

    n_data = (n_blk * n_det - 1) * hp
    n_cross = (n_blk - 1) * (n_det - 1) * ha
    arrived(data4.at[pl.ds(0, n_data - n_cross)], s_recv.at[0])
    arrived(data4.at[pl.ds(0, n_cross)], cross_recv.at[0])
    for q, higher, here, there in peers:
        for dx in range(1, n_det):
            arrived(data_part(q * n_det + column(dx), *early), zx_recv.at[here, dx - 1])

    def filtered(n, carry):
        rows = data4[ids_p[0, 0, n]].astype(f32)
        dr, di = rows[:, :NMIN], rows[:, NMIN:]
        wr, wi = turned[n, :, :NMIN], turned[n, :, NMIN:]
        z_out[n] = jnp.concatenate([dr * wr - di * wi, dr * wi + di * wr], axis=1).astype(bf16)
        return carry

    lax.fori_loop(0, n_trig, filtered, 0, unroll=16)

    some = data4.at[pl.ds(0, 2 * n_data)]
    pltpu.make_async_copy(some, some, data_send.at[0]).wait()
    some = tmpl4.at[pl.ds(0, 2 * (n_blk - 1) * hk)]
    pltpu.make_async_copy(some, some, tmpl_send.at[0]).wait()
    some = cuts.at[pl.ds(0, n_blk - 1)]
    pltpu.make_async_copy(some, some, cuts_send.at[0]).wait()


def chi_kernel(z_in, hot_in, between_in, keep_in, spin_in, rnorm_in, fixed, peak_in, peak_out, chi_out, chi_rows, sem):
    f32, bf16 = jnp.float32, jnp.bfloat16
    n_grp = hot_in.shape[0]
    n_fixed = NMAJ * GROUP
    save_peak = pltpu.make_async_copy(peak_in, peak_out, sem.at[0])
    save_peak.start()
    at = lax.broadcasted_iota(jnp.int32, (GROUP * NCUT, NMIN), 1)
    row = lax.broadcasted_iota(jnp.int32, (GROUP * NCUT, NMIN), 0)
    step = ((at == row).astype(f32) - (at == row - GROUP).astype(f32)).astype(bf16)
    own_rows = lax.broadcasted_iota(jnp.int32, (2 * GROUP, NMIN), 0)
    whole = (lax.broadcasted_iota(jnp.int32, (2 * GROUP, NMIN), 1) // NMAJ == own_rows).astype(f32).astype(bf16)
    whole = jnp.concatenate([whole, jnp.zeros_like(whole)], axis=1)
    own_turn = fixed[n_fixed:2 * n_fixed, :].astype(f32)

    def rotate(v, w):
        vr, vi, wr, wi = v[:, :NMIN], v[:, NMIN:], w[:, :NMIN], w[:, NMIN:]
        return jnp.concatenate([vr * wr - vi * wi, vr * wi + vi * wr], axis=1).astype(bf16)

    def one_batch(t):
        rows = GROUP * NMAJ
        qs = [t * BATCH + i for i in range(BATCH)]
        zs = [z_in[pl.ds(q * GROUP, GROUP)].reshape(rows, 2 * NMIN) for q in qs]
        picks = [jnp.dot(hot_in[q], z, preferred_element_type=f32) for q, z in zip(qs, zs)]
        parts = []
        for q, pick in zip(qs, picks):
            keep = keep_in[q]
            parts.append(pick.astype(bf16) * jnp.concatenate([keep, keep], axis=1))
        moved = [jnp.dot(jnp.concatenate([z, part], axis=0), fixed[2 * n_fixed:, :], preferred_element_type=f32) for z, part in zip(zs, parts)]
        turned = [jnp.concatenate([rotate(m[:rows], own_turn), rotate(m[rows:], spin_in[q])], axis=0) for q, m in zip(qs, moved)]
        bins = []
        for q, turn in zip(qs, turned):
            mix = jnp.concatenate([jnp.concatenate([between_in[q], step], axis=1), whole], axis=0)
            bins.append(jnp.dot(mix, turn, preferred_element_type=f32))
        for q, bn in zip(qs, bins):
            br, bi = bn[:rows, :NMIN], bn[:rows, NMIN:]
            energy = jnp.sum((br * br + bi * bi).reshape(NCUT, GROUP, NMIN), axis=0)
            tr, ti = bn[rows:rows + GROUP, :NMIN], bn[rows:rows + GROUP, NMIN:]
            loud = tr * tr + ti * ti
            at_q = q * GROUP
            rnorm = rnorm_in[pl.ds(at_q, GROUP), :]
            reduced = jnp.maximum(energy - loud * (1.0 / NCUT), 0.0) * (NCUT / (2.0 * NCUT - 2.0)) * rnorm
            rho = jnp.sqrt(loud * rnorm)
            bend = jnp.exp(jnp.log((1.0 + reduced * reduced * reduced) * 0.5) * (-1.0 / 6.0))
            chi_rows[pl.ds(at_q, GROUP), :] = jnp.where(reduced > 1.0, rho * bend, rho)

    saves = []
    for t in range(n_grp // BATCH):
        one_batch(t)
        part = pl.ds(t * BATCH * GROUP, BATCH * GROUP)
        saves.append(pltpu.make_async_copy(chi_rows.at[part], chi_out.at[0, 0, part], sem.at[1 + t]))
        saves[-1].start()
    save_peak.wait()
    for save in saves:
        save.wait()


def fused(sizes, ids_k, ids_p, ids_t, own, tmpl, cuts, tables):
    n_blk, n_det, n_sub = sizes
    fixed, second, wide = tables
    n_tmpl = n_blk * tmpl.shape[0]
    n_trig = ids_k.shape[-1]
    n_grp = n_trig // GROUP
    hbm = pl.BlockSpec(memory_space=pltpu.HBM)
    vmem = pl.BlockSpec(memory_space=pltpu.VMEM)
    dma = pltpu.SemaphoreType.DMA
    f32, bf16 = jnp.float32, jnp.bfloat16
    n_half = second.shape[1] // 2
    peak_shape = (own.shape[0], n_half * NMAJ)
    rows = GROUP * NCUT
    made = [
        (peak_shape, f32),
        ((n_trig, NMAJ, 2 * NMIN), bf16),
        ((n_grp, rows, NMIN), bf16),
        ((n_grp, rows, NMIN), bf16),
        ((n_grp, rows, NMIN), bf16),
        ((n_grp, rows, 2 * NMIN), f32),
        ((n_trig, NMIN), f32),
        (fixed.shape, fixed.dtype),
    ]
    scratch = [
        pltpu.VMEM((n_blk * n_det * own.shape[0],) + own.shape[1:], own.dtype),
        pltpu.VMEM((n_tmpl,) + tmpl.shape[1:], tmpl.dtype),
        pltpu.VMEM((n_blk,) + cuts.shape, cuts.dtype),
    ]
    scratch += [pltpu.SMEM(ids_k.shape, jnp.int32)] * 3
    scratch += [
        pltpu.VMEM(ids_k.shape, jnp.int32),
        pltpu.VMEM(second.shape[1:], second.dtype),
        pltpu.VMEM(wide.shape, wide.dtype),
        pltpu.VMEM((n_tmpl, NMIN), f32),
        pltpu.VMEM((n_tmpl, 1, NMIN), f32),
        pltpu.VMEM((n_trig, NMAJ, 2 * NMIN), f32),
        dma((10,)), dma((1,)), dma((1,)), dma((1,)), dma((1,)),
        dma((n_blk - 1,)), dma((n_blk - 1,)), dma((n_det - 1,)), dma((2, n_blk - 1)),
        dma((n_blk - 1, n_det - 1)), dma((n_blk - 1, n_det - 1)), dma((1,)), dma((1,)),
        pltpu.SemaphoreType.REGULAR((n_blk - 1,)), pltpu.SemaphoreType.REGULAR((n_det - 1, 2)),
        pltpu.SemaphoreType.REGULAR((1,)),
    ]
    made_refs = pl.pallas_call(
        functools.partial(gather_kernel, n_blk, n_det, n_sub),
        out_shape=[pltpu.VMEM(shape, dtype) for shape, dtype in made],
        in_specs=[hbm] * 9,
        out_specs=[vmem] * len(made),
        scratch_shapes=scratch,
        compiler_params=pltpu.CompilerParams(
            collective_id=0, has_side_effects=True, vmem_limit_bytes=32 * 1024 * 1024
        ),
        name="gather_and_peak",
    )(*(pltpu.with_memory_space_constraint(x, pltpu.HBM)
        for x in (ids_k, ids_p, ids_t, own, tmpl, cuts, fixed, second, wide)))
    return pl.pallas_call(
        chi_kernel,
        out_shape=(
            jax.ShapeDtypeStruct(peak_shape, f32),
            jax.ShapeDtypeStruct(ids_k.shape + (STEPS * NMAJ,), f32),
        ),
        in_specs=[vmem] * len(made),
        out_specs=(hbm, hbm),
        scratch_shapes=[pltpu.VMEM((n_trig, STEPS * NMAJ), f32), dma((1 + n_grp // BATCH,))],
        compiler_params=pltpu.CompilerParams(vmem_limit_bytes=24 * 1024 * 1024),
        name="chi",
    )(*made_refs[1:], made_refs[0])


def body(sizes, data, templates, bin_cuts, trig_template, trig_pair, trig_tile):
    tables = tuple(jnp.asarray(t) for t in host_tables(sizes[2]))
    peak, chi = fused(sizes, trig_template, trig_pair, trig_tile, data, templates, bin_cuts, tables)
    return peak, chi


def solution(mesh):
    sizes = (mesh.shape["blk"], mesh.shape["det"], mesh.shape["sub"])
    return jax.shard_map(
        functools.partial(body, sizes),
        mesh=mesh,
        in_specs=(
            P(("groups", "blk", "det"), None, None),
            P(("groups", "blk"), None, None),
            P(("groups", "blk"), None),
            P(("groups", "blk", "det"), "sub", None),
            P(("groups", "blk", "det"), "sub", None),
            P(("groups", "blk", "det"), "sub", None),
        ),
        out_specs=(
            P(("groups", "blk", "det"), "sub"),
            P(("groups", "blk", "det"), "sub", None, None),
        ),
        check_vma=False,
    )
```

```python
import functools
import math

import jax
import jax.numpy as jnp
import numpy as np
from jax import lax
from jax.experimental import pallas as pl
from jax.experimental.pallas import tpu as pltpu
from jax.sharding import PartitionSpec as P

MESH = pl.DeviceIdType.MESH
NMAJ = 16
NMIN = 128
NCUT = 16
STEPS = 8
GROUP = 8
BATCH = 8
PRE = 1


def unit_circle(index, period):
    angle = (index % period) * (2.0 * math.pi / period)
    return np.cos(angle), np.sin(angle)


def host_tables(n_sub):
    bf16 = jnp.bfloat16
    major = np.arange(NMAJ)
    minor = np.arange(NMIN)
    cos16, sin16 = unit_circle(major[:, None] * major[None, :], NMAJ)
    eye = np.eye(GROUP)
    first = np.concatenate([np.kron(eye, cos16), np.kron(eye, sin16)], axis=1).astype(bf16)
    twc, tws = unit_circle(major[:, None] * minor[None, :], NMAJ * NMIN)
    twiddle = np.concatenate([twc, tws], axis=1).astype(np.float32)
    n_half = NMIN // n_sub
    second = []
    for half in range(n_sub):
        steps = half * n_half + np.arange(n_half)
        cosine, sine = unit_circle(steps[:, None] * minor[None, :], NMIN)
        real_rows = np.concatenate([cosine, -sine], axis=1)
        imag_rows = np.concatenate([sine, cosine], axis=1)
        second.append(np.concatenate([real_rows, imag_rows], axis=0))
    second = np.stack(second).astype(bf16)
    times = np.arange(NMAJ * STEPS)
    cosine, sine = unit_circle(minor[:, None] * times[None, :], NMAJ * NMIN)
    tile_dft = np.concatenate(
        [np.concatenate([cosine, sine], axis=1), np.concatenate([-sine, cosine], axis=1)], axis=0
    ).astype(bf16)
    rowc, rows = unit_circle(major[:, None] * (times % NMAJ)[None, :], NMAJ)
    row_phase = np.tile(np.concatenate([rowc, rows], axis=1), (GROUP, 1)).astype(bf16)
    starts = np.arange(NMIN // STEPS) * STEPS
    phc, phs = unit_circle(starts[:, None] * minor[None, :], NMIN)
    tile_phase = np.concatenate([phc, phs], axis=1).astype(np.float32)[:, None, :]
    fixed = np.concatenate([first, row_phase, tile_dft], axis=0)
    wide = np.concatenate([twiddle[:, None, :], tile_phase], axis=0)
    return fixed, second, wide


def swap_blocks(x):
    sub = lax.broadcasted_iota(jnp.int32, x.shape, 0)
    grp = lax.broadcasted_iota(jnp.int32, x.shape, 1) // NMAJ
    rows, lanes = x.shape
    for bit in (1, 2, 4):
        up = pltpu.roll(pltpu.roll(x, rows - bit, 0), NMAJ * bit, 1)
        down = pltpu.roll(pltpu.roll(x, bit, 0), lanes - NMAJ * bit, 1)
        sb, gb = (sub & bit) != 0, (grp & bit) != 0
        x = jnp.where(jnp.logical_and(jnp.logical_not(sb), gb), up,
                      jnp.where(jnp.logical_and(sb, jnp.logical_not(gb)), down, x))
    return x


def conj_product(data, tmpl):
    dr, di = data[..., :NMIN], data[..., NMIN:]
    tr, ti = tmpl[..., :NMIN], tmpl[..., NMIN:]
    return dr * tr + di * ti, di * tr - dr * ti


def gather_kernel(n_blk, n_det, n_sub, *refs):
    (ids_k_in, ids_p_in, ids_t_in, own_in, tmpl_in, cuts_in, fixed_in, second_in, wide_in,
     peak_out, z_out, hot_out, between_out, keep_out, spin_out, rnorm_out, fixed,
     data4, tmpl4, cuts, ids_k, ids_p, ids_t, ids_v, second, wide_tab, cut_rows, norm_tab, turned,
     local_sem, data_send, tmpl_send, cuts_send, cuts_recv, t_recv, ts_recv, x_recv, z_recv, zx_recv,
     xz_recv, cross_recv, s_recv, blk_in, det_in, sub_in) = refs
    f32, bf16 = jnp.float32, jnp.bfloat16
    b = lax.axis_index("blk")
    d = lax.axis_index("det")
    half = lax.axis_index("sub")
    other = n_sub - 1 - half
    pairs = own_in.shape[0]
    kb = tmpl_in.shape[0]
    n_cut = cuts_in.shape[1]
    n_tmpl = n_blk * kb
    n_trig = ids_k_in.shape[2]
    n_grp = n_trig // GROUP
    hp, hk = pairs // n_sub, kb // n_sub
    ha = hp // 2
    own = b * n_det + d
    early, late = (0, ha), (ha, hp - ha)

    moves = [(own_in, data4.at[pl.ds(own * pairs, pairs)]), (tmpl_in, tmpl4.at[pl.ds(b * kb, kb)]),
             (cuts_in, cuts.at[b]), (fixed_in, fixed), (wide_in, wide_tab), (second_in.at[half], second),
             (ids_k_in, ids_k), (ids_p_in, ids_p), (ids_t_in, ids_t), (ids_k_in, ids_v)]
    fetches = [pltpu.make_async_copy(src, dst, local_sem.at[i]) for i, (src, dst) in enumerate(moves)]
    for copy in fetches[:3]:
        copy.start()

    barrier = pltpu.get_barrier_semaphore()

    def tell(sem, where):
        pl.semaphore_signal(sem, inc=1, device_id=where, device_id_type=MESH)

    for q in range(n_blk - 1, 0, -1):
        pl.when(b < q)(functools.partial(tell, barrier, {"blk": q}))
    for c in range(n_det - 1, 0, -1):
        for core in range(n_sub):
            pl.when(d < c)(functools.partial(tell, barrier, {"det": c, "sub": core}))
    pl.when(half == n_sub - 1)(functools.partial(tell, barrier, {"sub": other}))
    lower = b + d * n_sub + (n_sub - 1 - half)
    pl.when(lower > 0)(lambda: pl.semaphore_wait(barrier, lower))
    for q in range(n_blk - 1):
        pl.when(b > q)(functools.partial(tell, blk_in.at[lax.rem(b - q - 1 + n_blk, n_blk)], {"blk": q}))
    for c in range(n_det - 1):
        for core in range(n_sub):
            slot = (lax.rem(d - c - 1 + n_det, n_det), lax.rem(half + core, n_sub))
            pl.when(d > c)(functools.partial(tell, det_in.at[slot], {"det": c, "sub": core}))
    pl.when(half == 0)(functools.partial(tell, sub_in.at[0], {"sub": other}))
    for copy in fetches[3:]:
        copy.start()

    def remote(ref, send, recv, where):
        pltpu.make_async_remote_copy(src_ref=ref, dst_ref=ref, send_sem=send.at[0], recv_sem=recv,
                                     device_id=where, device_id_type=MESH).start()

    def arrived(ref, sem):
        pltpu.make_async_copy(ref, ref, sem).wait()

    def data_part(place, first, count):
        return data4.at[pl.ds(place * pairs + half * hp + first, count)]

    def tmpl_part(place):
        return tmpl4.at[pl.ds(place * kb + half * hk, hk)]

    def column(dx):
        return lax.rem(d + dx, n_det)

    def other_half(place, first, count):
        remote(data_part(place, first, count), data_send, s_recv.at[0], {"sub": other})

    peers = []
    for i in range(n_blk - 1):
        higher = (i + n_blk - b) // n_blk
        q = i + higher
        peers.append((q, higher, lax.rem(q - b - 1 + n_blk, n_blk), lax.rem(b - q - 1 + n_blk, n_blk)))

    def remote_own(first, count, recv, where):
        pltpu.make_async_remote_copy(src_ref=own_in.at[pl.ds(half * hp + first, count)],
                                     dst_ref=data_part(own, first, count), send_sem=data_send.at[0], recv_sem=recv,
                                     device_id=where, device_id_type=MESH).start()

    def send_x(dx):
        remote_own(0, hp, x_recv.at[n_det - 1 - dx], {"det": column(dx)})

    def send_z(q, there):
        where = {"blk": q}
        remote_own(*early, z_recv.at[0, there], where)
        pltpu.make_async_remote_copy(src_ref=tmpl_in.at[pl.ds(half * hk + 0, hk)], dst_ref=tmpl_part(b),
                                     send_sem=tmpl_send.at[0], recv_sem=t_recv.at[there],
                                     device_id=where, device_id_type=MESH).start()
        remote_own(*late, z_recv.at[1, there], where)
        pltpu.make_async_remote_copy(src_ref=cuts_in, dst_ref=cuts.at[b], send_sem=cuts_send.at[0],
                                     recv_sem=cuts_recv.at[0], device_id=where, device_id_type=MESH).start()

    for dx in range(1, n_det):
        pl.when(column(dx) < d)(functools.partial(send_x, dx))
    for q, higher, here, there in peers:
        pl.when(higher == 0)(functools.partial(send_z, q, there))
    for copy in fetches:
        copy.wait()

    n_fixed = NMAJ * GROUP
    wide = data4[pl.ds(own * pairs, pairs)].astype(f32)
    twiddle = wide_tab[:NMAJ].reshape(NMAJ, 2 * NMIN)
    twc = jnp.broadcast_to(twiddle[:, :NMIN][None], (pairs, NMAJ, NMIN)).reshape(pairs * NMAJ, NMIN)
    tws = jnp.broadcast_to(twiddle[:, NMIN:][None], (pairs, NMAJ, NMIN)).reshape(pairs * NMAJ, NMIN)
    n_half = second.shape[0] // 2

    def peak_of(src_b, peak):
        norms, stacks, bents = [], [], []
        for k in range(kb):
            row = tmpl4[src_b * kb + k].astype(f32)
            norm = jnp.sum(jnp.sum(row * row, axis=0, keepdims=True), axis=1, keepdims=True)
            norm_tab[src_b * kb + k] = jnp.broadcast_to(norm, (1, NMIN))
            norms.append(norm)
            real, imag = conj_product(wide, row[None])
            real = real.reshape(pairs * NMAJ, NMIN).astype(bf16)
            imag = imag.reshape(pairs * NMAJ, NMIN).astype(bf16)
            stacks.append(jnp.concatenate(
                [jnp.concatenate([real, imag], axis=1), jnp.concatenate([-imag, real], axis=1)], axis=0
            ))
        sections = [jnp.dot(fixed[:n_fixed, :], stack, preferred_element_type=f32) for stack in stacks]
        for section in sections:
            sr, si = section[:, :NMIN], section[:, NMIN:]
            bents.append(jnp.concatenate([sr * twc - si * tws, sr * tws + si * twc], axis=1).astype(bf16))
        snrs = [lax.dot_general(second[...], bent, (((1,), (1,)), ((), ())), preferred_element_type=f32)
                for bent in bents]
        for snr, norm in zip(snrs, norms):
            power = snr[:n_half] * snr[:n_half] + snr[n_half:] * snr[n_half:]
            peak = jnp.maximum(peak, power * (1.0 / norm))
        return peak

    peak = peak_of(b, jnp.zeros((n_half, pairs * NMAJ), f32))

    def answer_x(dx):
        pl.semaphore_wait(det_in.at[dx - 1, 0], 1)
        send_x(dx)
        pl.semaphore_wait(det_in.at[dx - 1, 1], 1)

    def answer_z(q, here, there):
        pl.semaphore_wait(blk_in.at[here], 1)
        send_z(q, there)

    for dx in range(1, n_det):
        pl.when(column(dx) > d)(functools.partial(answer_x, dx))
    for q, higher, here, there in peers:
        pl.when(higher == 1)(functools.partial(answer_z, q, here, there))
    pl.when(half == n_sub - 1)(lambda: pl.semaphore_wait(sub_in.at[0], 1))

    for dx in range(1, n_det):
        place = b * n_det + column(dx)
        arrived(data_part(place, 0, hp), x_recv.at[dx - 1])
        for q, higher, here, there in peers:
            remote(data_part(place, *late), data_send, xz_recv.at[there, dx - 1], {"blk": q})
        other_half(place, 0, hp)
    for q, higher, here, there in peers:
        arrived(data_part(q * n_det + d, *early), z_recv.at[0, here])
        for dx in range(1, n_det):
            block = data_part(q * n_det + d, *early)
            remote(block, data_send, zx_recv.at[here, n_det - 1 - dx], {"det": column(dx)})
            remote(block, data_send, cross_recv.at[0], {"det": column(dx), "sub": other})
        arrived(tmpl_part(q), t_recv.at[here])
        remote(tmpl_part(q), tmpl_send, ts_recv.at[here], {"sub": other})

    arrived(cuts.at[pl.ds(0, n_blk - 1)], cuts_recv.at[0])
    cut_rows[...] = jnp.zeros(cut_rows.shape, f32)
    cut_rows[:, NCUT - 1:NCUT] = jnp.full((n_tmpl, 1), NMAJ, f32)
    for blk in range(n_blk):
        cut_rows[blk * kb:(blk + 1) * kb, 0:n_cut] = (cuts[blk] >> 7).astype(f32)
        cut_rows[blk * kb:(blk + 1) * kb, 64:64 + n_cut] = (cuts[blk] & (NMIN - 1)).astype(f32)
    is_k = lax.broadcasted_iota(jnp.int32, (n_tmpl, n_trig), 0) == jnp.broadcast_to(ids_v[0], (n_tmpl, n_trig))
    pick_k = is_k.astype(f32).astype(bf16)

    def by_trigger(table):
        return lax.dot_general(pick_k, table, (((0,), (0,)), ((), ())), preferred_element_type=f32)

    trig_cuts = by_trigger(cut_rows[...].astype(bf16))
    lane = lax.broadcasted_iota(jnp.int32, (n_trig, NMIN), 1)
    spread = (
        (lax.broadcasted_iota(jnp.int32, (NMIN, 2 * NMIN), 0) < 64)
        == (lax.broadcasted_iota(jnp.int32, (NMIN, 2 * NMIN), 1) < NMIN)
    ).astype(f32).astype(bf16)
    base = ((lax.broadcasted_iota(jnp.int32, (n_trig, NMIN), 0) % GROUP) * NMAJ).astype(f32)
    at = lane.astype(f32)

    def cut_masks(first, count, last):
        spans = []
        for r in range(first, first + count):
            only = jnp.where((lane & 63) == r, trig_cuts, 0.0).astype(bf16)
            spans.append(jnp.dot(only, spread, preferred_element_type=f32))
        stacks = ([], [], [])
        for i, span in enumerate(spans):
            row = span[:, :NMIN] + base
            marks = (at == row, jnp.logical_and(at >= last, at < row), at < span[:, NMIN:])
            last = row
            for stack, mark in zip(stacks, marks):
                stack.append(mark.astype(f32).reshape(n_grp, GROUP, NMIN))
            if i % 2 == 1:
                rows = slice((first + i - 1) * GROUP, (first + i + 1) * GROUP)
                for stack, out in zip(stacks, (hot_out, between_out, keep_out)):
                    out[:, rows, :] = jnp.concatenate(stack[-2:], axis=1).astype(bf16)
        return last

    last = cut_masks(0, NCUT // 2, base)
    for q, higher, here, there in peers:
        arrived(data_part(q * n_det + d, *late), z_recv.at[1, here])
        other_half(q * n_det + d, 0, hp)
    cut_masks(NCUT // 2, NCUT // 2, last)
    for q in range(n_grp):
        spin_out[q] = jnp.dot(hot_out[q], fixed[n_fixed:2 * n_fixed, :], preferred_element_type=f32)

    def prepare(n, carry):
        k = ids_k[0, 0, n]
        row = tmpl4[k].astype(f32)
        phase = wide_tab[NMAJ + half * ((wide_tab.shape[0] - NMAJ) // n_sub) + ids_t[0, 0, n]]
        pc, ps = phase[:, :NMIN], phase[:, NMIN:]
        tr, ti = row[:, :NMIN], row[:, NMIN:]
        turned[n, :, :NMIN] = tr * pc + ti * ps
        turned[n, :, NMIN:] = tr * ps - ti * pc
        return carry

    def relayed():
        for q, higher, here, there in peers:
            for dx in range(1, n_det):
                place = q * n_det + column(dx)
                arrived(data_part(place, *late), xz_recv.at[here, dx - 1])
                other_half(place, *late)

    for i, (q, higher, here, there) in enumerate(peers):
        if i == PRE:
            relayed()
        arrived(tmpl4.at[pl.ds(q * kb + other * hk, hk)], ts_recv.at[here])
        peak = peak_of(q, peak)
    if len(peers) <= PRE:
        relayed()
    lax.fori_loop(0, n_trig, prepare, 0, unroll=16)

    rest = 1.0 / norm_tab[...].reshape(n_tmpl, NMIN)
    scale = jnp.zeros((n_trig, NMIN), f32)
    for _ in range(3):
        piece = rest.astype(bf16)
        rest = rest - piece.astype(f32)
        scale = scale + by_trigger(piece)
    rnorm_out[...] = scale

    swapped = swap_blocks(jnp.sqrt(peak))
    for u in range(n_half // 8):
        peak_out[:, u * 128:(u + 1) * 128] = swapped[8 * u:8 * u + 8, :]

    n_data = (n_blk * n_det - 1) * hp
    n_cross = (n_blk - 1) * (n_det - 1) * ha
    arrived(data4.at[pl.ds(0, n_data - n_cross)], s_recv.at[0])
    arrived(data4.at[pl.ds(0, n_cross)], cross_recv.at[0])
    for q, higher, here, there in peers:
        for dx in range(1, n_det):
            arrived(data_part(q * n_det + column(dx), *early), zx_recv.at[here, dx - 1])

    def filtered(n, carry):
        rows = data4[ids_p[0, 0, n]].astype(f32)
        dr, di = rows[:, :NMIN], rows[:, NMIN:]
        wr, wi = turned[n, :, :NMIN], turned[n, :, NMIN:]
        z_out[n] = jnp.concatenate([dr * wr - di * wi, dr * wi + di * wr], axis=1).astype(bf16)
        return carry

    lax.fori_loop(0, n_trig, filtered, 0, unroll=32)

    some = data4.at[pl.ds(0, 2 * n_data)]
    pltpu.make_async_copy(some, some, data_send.at[0]).wait()
    some = tmpl4.at[pl.ds(0, 2 * (n_blk - 1) * hk)]
    pltpu.make_async_copy(some, some, tmpl_send.at[0]).wait()
    some = cuts.at[pl.ds(0, n_blk - 1)]
    pltpu.make_async_copy(some, some, cuts_send.at[0]).wait()


def chi_kernel(z_in, hot_in, between_in, keep_in, spin_in, rnorm_in, fixed, peak_in, peak_out, chi_out, chi_rows, sem):
    f32, bf16 = jnp.float32, jnp.bfloat16
    n_grp = hot_in.shape[0]
    n_fixed = NMAJ * GROUP
    save_peak = pltpu.make_async_copy(peak_in, peak_out, sem.at[0])
    save_peak.start()
    at = lax.broadcasted_iota(jnp.int32, (GROUP * NCUT, NMIN), 1)
    row = lax.broadcasted_iota(jnp.int32, (GROUP * NCUT, NMIN), 0)
    step = ((at == row).astype(f32) - (at == row - GROUP).astype(f32)).astype(bf16)
    own_rows = lax.broadcasted_iota(jnp.int32, (2 * GROUP, NMIN), 0)
    whole = (lax.broadcasted_iota(jnp.int32, (2 * GROUP, NMIN), 1) // NMAJ == own_rows).astype(f32).astype(bf16)
    whole = jnp.concatenate([whole, jnp.zeros_like(whole)], axis=1)
    own_turn = fixed[n_fixed:2 * n_fixed, :].astype(f32)

    def rotate(v, w):
        vr, vi, wr, wi = v[:, :NMIN], v[:, NMIN:], w[:, :NMIN], w[:, NMIN:]
        return jnp.concatenate([vr * wr - vi * wi, vr * wi + vi * wr], axis=1).astype(bf16)

    def one_batch(t):
        rows = GROUP * NMAJ
        qs = [t * BATCH + i for i in range(BATCH)]
        zs = [z_in[pl.ds(q * GROUP, GROUP)].reshape(rows, 2 * NMIN) for q in qs]
        picks = [jnp.dot(hot_in[q], z, preferred_element_type=f32) for q, z in zip(qs, zs)]
        parts = []
        for q, pick in zip(qs, picks):
            keep = keep_in[q]
            parts.append(pick.astype(bf16) * jnp.concatenate([keep, keep], axis=1))
        moved = [jnp.dot(jnp.concatenate([z, part], axis=0), fixed[2 * n_fixed:, :], preferred_element_type=f32) for z, part in zip(zs, parts)]
        turned = [jnp.concatenate([rotate(m[:rows], own_turn), rotate(m[rows:], spin_in[q])], axis=0) for q, m in zip(qs, moved)]
        bins = []
        for q, turn in zip(qs, turned):
            mix = jnp.concatenate([jnp.concatenate([between_in[q], step], axis=1), whole], axis=0)
            bins.append(jnp.dot(mix, turn, preferred_element_type=f32))
        for q, bn in zip(qs, bins):
            br, bi = bn[:rows, :NMIN], bn[:rows, NMIN:]
            energy = jnp.sum((br * br + bi * bi).reshape(NCUT, GROUP, NMIN), axis=0)
            tr, ti = bn[rows:rows + GROUP, :NMIN], bn[rows:rows + GROUP, NMIN:]
            loud = tr * tr + ti * ti
            at_q = q * GROUP
            rnorm = rnorm_in[pl.ds(at_q, GROUP), :]
            reduced = jnp.maximum(energy - loud * (1.0 / NCUT), 0.0) * (NCUT / (2.0 * NCUT - 2.0)) * rnorm
            rho = jnp.sqrt(loud * rnorm)
            bend = jnp.exp(jnp.log((1.0 + reduced * reduced * reduced) * 0.5) * (-1.0 / 6.0))
            chi_rows[pl.ds(at_q, GROUP), :] = jnp.where(reduced > 1.0, rho * bend, rho)

    saves = []
    for t in range(n_grp // BATCH):
        one_batch(t)
        part = pl.ds(t * BATCH * GROUP, BATCH * GROUP)
        saves.append(pltpu.make_async_copy(chi_rows.at[part], chi_out.at[0, 0, part], sem.at[1 + t]))
        saves[-1].start()
    save_peak.wait()
    for save in saves:
        save.wait()


def fused(sizes, ids_k, ids_p, ids_t, own, tmpl, cuts, tables):
    n_blk, n_det, n_sub = sizes
    fixed, second, wide = tables
    n_tmpl = n_blk * tmpl.shape[0]
    n_trig = ids_k.shape[-1]
    n_grp = n_trig // GROUP
    hbm = pl.BlockSpec(memory_space=pltpu.HBM)
    vmem = pl.BlockSpec(memory_space=pltpu.VMEM)
    dma = pltpu.SemaphoreType.DMA
    f32, bf16 = jnp.float32, jnp.bfloat16
    n_half = second.shape[1] // 2
    peak_shape = (own.shape[0], n_half * NMAJ)
    rows = GROUP * NCUT
    made = [
        (peak_shape, f32),
        ((n_trig, NMAJ, 2 * NMIN), bf16),
        ((n_grp, rows, NMIN), bf16),
        ((n_grp, rows, NMIN), bf16),
        ((n_grp, rows, NMIN), bf16),
        ((n_grp, rows, 2 * NMIN), f32),
        ((n_trig, NMIN), f32),
        (fixed.shape, fixed.dtype),
    ]
    scratch = [
        pltpu.VMEM((n_blk * n_det * own.shape[0],) + own.shape[1:], own.dtype),
        pltpu.VMEM((n_tmpl,) + tmpl.shape[1:], tmpl.dtype),
        pltpu.VMEM((n_blk,) + cuts.shape, cuts.dtype),
    ]
    scratch += [pltpu.SMEM(ids_k.shape, jnp.int32)] * 3
    scratch += [
        pltpu.VMEM(ids_k.shape, jnp.int32),
        pltpu.VMEM(second.shape[1:], second.dtype),
        pltpu.VMEM(wide.shape, wide.dtype),
        pltpu.VMEM((n_tmpl, NMIN), f32),
        pltpu.VMEM((n_tmpl, 1, NMIN), f32),
        pltpu.VMEM((n_trig, NMAJ, 2 * NMIN), f32),
        dma((10,)), dma((1,)), dma((1,)), dma((1,)), dma((1,)),
        dma((n_blk - 1,)), dma((n_blk - 1,)), dma((n_det - 1,)), dma((2, n_blk - 1)),
        dma((n_blk - 1, n_det - 1)), dma((n_blk - 1, n_det - 1)), dma((1,)), dma((1,)),
        pltpu.SemaphoreType.REGULAR((n_blk - 1,)), pltpu.SemaphoreType.REGULAR((n_det - 1, 2)),
        pltpu.SemaphoreType.REGULAR((1,)),
    ]
    made_refs = pl.pallas_call(
        functools.partial(gather_kernel, n_blk, n_det, n_sub),
        out_shape=[pltpu.VMEM(shape, dtype) for shape, dtype in made],
        in_specs=[hbm] * 9,
        out_specs=[vmem] * len(made),
        scratch_shapes=scratch,
        compiler_params=pltpu.CompilerParams(
            collective_id=0, has_side_effects=True, vmem_limit_bytes=32 * 1024 * 1024
        ),
        name="gather_and_peak",
    )(*(pltpu.with_memory_space_constraint(x, pltpu.HBM)
        for x in (ids_k, ids_p, ids_t, own, tmpl, cuts, fixed, second, wide)))
    return pl.pallas_call(
        chi_kernel,
        out_shape=(
            jax.ShapeDtypeStruct(peak_shape, f32),
            jax.ShapeDtypeStruct(ids_k.shape + (STEPS * NMAJ,), f32),
        ),
        in_specs=[vmem] * len(made),
        out_specs=(hbm, hbm),
        scratch_shapes=[pltpu.VMEM((n_trig, STEPS * NMAJ), f32), dma((1 + n_grp // BATCH,))],
        compiler_params=pltpu.CompilerParams(vmem_limit_bytes=24 * 1024 * 1024),
        name="chi",
    )(*made_refs[1:], made_refs[0])


def body(sizes, data, templates, bin_cuts, trig_template, trig_pair, trig_tile):
    tables = tuple(jnp.asarray(t) for t in host_tables(sizes[2]))
    peak, chi = fused(sizes, trig_template, trig_pair, trig_tile, data, templates, bin_cuts, tables)
    return peak, chi


def solution(mesh):
    sizes = (mesh.shape["blk"], mesh.shape["det"], mesh.shape["sub"])
    return jax.shard_map(
        functools.partial(body, sizes),
        mesh=mesh,
        in_specs=(
            P(("groups", "blk", "det"), None, None),
            P(("groups", "blk"), None, None),
            P(("groups", "blk"), None),
            P(("groups", "blk", "det"), "sub", None),
            P(("groups", "blk", "det"), "sub", None),
            P(("groups", "blk", "det"), "sub", None),
        ),
        out_specs=(
            P(("groups", "blk", "det"), "sub"),
            P(("groups", "blk", "det"), "sub", None, None),
        ),
        check_vma=False,
    )
```

```python
import functools
import math

import jax
import jax.numpy as jnp
import numpy as np
from jax import lax
from jax.experimental import pallas as pl
from jax.experimental.pallas import tpu as pltpu
from jax.sharding import PartitionSpec as P

MESH = pl.DeviceIdType.MESH
NMAJ = 16
NMIN = 128
NCUT = 16
STEPS = 8
GROUP = 8
BATCH = 8
PRE = 1


def unit_circle(index, period):
    angle = (index % period) * (2.0 * math.pi / period)
    return np.cos(angle), np.sin(angle)


def host_tables(n_sub):
    bf16 = jnp.bfloat16
    major = np.arange(NMAJ)
    minor = np.arange(NMIN)
    cos16, sin16 = unit_circle(major[:, None] * major[None, :], NMAJ)
    eye = np.eye(GROUP)
    first = np.concatenate([np.kron(eye, cos16), np.kron(eye, sin16)], axis=1).astype(bf16)
    twc, tws = unit_circle(major[:, None] * minor[None, :], NMAJ * NMIN)
    twiddle = np.concatenate([twc, tws], axis=1).astype(np.float32)
    n_half = NMIN // n_sub
    second = []
    for half in range(n_sub):
        steps = half * n_half + np.arange(n_half)
        cosine, sine = unit_circle(steps[:, None] * minor[None, :], NMIN)
        real_rows = np.concatenate([cosine, -sine], axis=1)
        imag_rows = np.concatenate([sine, cosine], axis=1)
        second.append(np.concatenate([real_rows, imag_rows], axis=0))
    second = np.stack(second).astype(bf16)
    times = np.arange(NMAJ * STEPS)
    cosine, sine = unit_circle(minor[:, None] * times[None, :], NMAJ * NMIN)
    tile_dft = np.concatenate(
        [np.concatenate([cosine, sine], axis=1), np.concatenate([-sine, cosine], axis=1)], axis=0
    ).astype(bf16)
    rowc, rows = unit_circle(major[:, None] * (times % NMAJ)[None, :], NMAJ)
    row_phase = np.tile(np.concatenate([rowc, rows], axis=1), (GROUP, 1)).astype(bf16)
    starts = np.arange(NMIN // STEPS) * STEPS
    phc, phs = unit_circle(starts[:, None] * minor[None, :], NMIN)
    tile_phase = np.concatenate([phc, phs], axis=1).astype(np.float32)[:, None, :]
    fixed = np.concatenate([first, row_phase, tile_dft], axis=0)
    wide = np.concatenate([twiddle[:, None, :], tile_phase], axis=0)
    return fixed, second, wide


def swap_blocks(x):
    sub = lax.broadcasted_iota(jnp.int32, x.shape, 0)
    grp = lax.broadcasted_iota(jnp.int32, x.shape, 1) // NMAJ
    rows, lanes = x.shape
    for bit in (1, 2, 4):
        up = pltpu.roll(pltpu.roll(x, rows - bit, 0), NMAJ * bit, 1)
        down = pltpu.roll(pltpu.roll(x, bit, 0), lanes - NMAJ * bit, 1)
        sb, gb = (sub & bit) != 0, (grp & bit) != 0
        x = jnp.where(jnp.logical_and(jnp.logical_not(sb), gb), up,
                      jnp.where(jnp.logical_and(sb, jnp.logical_not(gb)), down, x))
    return x


def conj_product(data, tmpl):
    dr, di = data[..., :NMIN], data[..., NMIN:]
    tr, ti = tmpl[..., :NMIN], tmpl[..., NMIN:]
    return dr * tr + di * ti, di * tr - dr * ti


def gather_kernel(n_blk, n_det, n_sub, *refs):
    (ids_k_in, ids_p_in, ids_t_in, own_in, tmpl_in, cuts_in, fixed_in, second_in, wide_in,
     peak_out, z_out, hot_out, between_out, keep_out, spin_out, rnorm_out, fixed,
     data4, tmpl4, cuts, ids_k, ids_p, ids_t, ids_v, second, wide_tab, cut_rows, norm_tab, turned,
     local_sem, data_send, tmpl_send, cuts_send, cuts_recv, t_recv, ts_recv, x_recv, z_recv, zx_recv,
     xz_recv, cross_recv, s_recv, blk_in, det_in, sub_in) = refs
    f32, bf16 = jnp.float32, jnp.bfloat16
    b = lax.axis_index("blk")
    d = lax.axis_index("det")
    half = lax.axis_index("sub")
    other = n_sub - 1 - half
    pairs = own_in.shape[0]
    kb = tmpl_in.shape[0]
    n_cut = cuts_in.shape[1]
    n_tmpl = n_blk * kb
    n_trig = ids_k_in.shape[2]
    n_grp = n_trig // GROUP
    hp, hk = pairs // n_sub, kb // n_sub
    ha = hp // 2
    own = b * n_det + d
    early, late = (0, ha), (ha, hp - ha)

    moves = [(own_in, data4.at[pl.ds(own * pairs, pairs)]), (tmpl_in, tmpl4.at[pl.ds(b * kb, kb)]),
             (cuts_in, cuts.at[b]), (fixed_in, fixed), (wide_in, wide_tab), (second_in.at[half], second),
             (ids_k_in, ids_k), (ids_p_in, ids_p), (ids_t_in, ids_t), (ids_k_in, ids_v)]
    fetches = [pltpu.make_async_copy(src, dst, local_sem.at[i]) for i, (src, dst) in enumerate(moves)]
    for copy in fetches[:3]:
        copy.start()

    barrier = pltpu.get_barrier_semaphore()

    def tell(sem, where):
        pl.semaphore_signal(sem, inc=1, device_id=where, device_id_type=MESH)

    for q in range(n_blk - 1, 0, -1):
        pl.when(b < q)(functools.partial(tell, barrier, {"blk": q}))
    for c in range(n_det - 1, 0, -1):
        for core in range(n_sub):
            pl.when(d < c)(functools.partial(tell, barrier, {"det": c, "sub": core}))
    pl.when(half == n_sub - 1)(functools.partial(tell, barrier, {"sub": other}))
    lower = b + d * n_sub + (n_sub - 1 - half)
    pl.when(lower > 0)(lambda: pl.semaphore_wait(barrier, lower))
    for q in range(n_blk - 1):
        pl.when(b > q)(functools.partial(tell, blk_in.at[lax.rem(b - q - 1 + n_blk, n_blk)], {"blk": q}))
    for c in range(n_det - 1):
        for core in range(n_sub):
            slot = (lax.rem(d - c - 1 + n_det, n_det), lax.rem(half + core, n_sub))
            pl.when(d > c)(functools.partial(tell, det_in.at[slot], {"det": c, "sub": core}))
    pl.when(half == 0)(functools.partial(tell, sub_in.at[0], {"sub": other}))
    for copy in fetches[3:]:
        copy.start()

    def remote(ref, send, recv, where):
        pltpu.make_async_remote_copy(src_ref=ref, dst_ref=ref, send_sem=send.at[0], recv_sem=recv,
                                     device_id=where, device_id_type=MESH).start()

    def arrived(ref, sem):
        pltpu.make_async_copy(ref, ref, sem).wait()

    def data_part(place, first, count):
        return data4.at[pl.ds(place * pairs + half * hp + first, count)]

    def tmpl_part(place):
        return tmpl4.at[pl.ds(place * kb + half * hk, hk)]

    def column(dx):
        return lax.rem(d + dx, n_det)

    def other_half(place, first, count):
        remote(data_part(place, first, count), data_send, s_recv.at[0], {"sub": other})

    peers = []
    for i in range(n_blk - 1):
        higher = (i + n_blk - b) // n_blk
        q = i + higher
        peers.append((q, higher, lax.rem(q - b - 1 + n_blk, n_blk), lax.rem(b - q - 1 + n_blk, n_blk)))

    def remote_own(first, count, recv, where):
        pltpu.make_async_remote_copy(src_ref=own_in.at[pl.ds(half * hp + first, count)],
                                     dst_ref=data_part(own, first, count), send_sem=data_send.at[0], recv_sem=recv,
                                     device_id=where, device_id_type=MESH).start()

    def send_x(dx):
        remote_own(0, hp, x_recv.at[n_det - 1 - dx], {"det": column(dx)})

    def send_z(q, there):
        where = {"blk": q}
        remote_own(*early, z_recv.at[0, there], where)
        pltpu.make_async_remote_copy(src_ref=tmpl_in.at[pl.ds(half * hk + 0, hk)], dst_ref=tmpl_part(b),
                                     send_sem=tmpl_send.at[0], recv_sem=t_recv.at[there],
                                     device_id=where, device_id_type=MESH).start()
        remote_own(*late, z_recv.at[1, there], where)
        pltpu.make_async_remote_copy(src_ref=cuts_in, dst_ref=cuts.at[b], send_sem=cuts_send.at[0],
                                     recv_sem=cuts_recv.at[0], device_id=where, device_id_type=MESH).start()

    for dx in range(1, n_det):
        pl.when(column(dx) < d)(functools.partial(send_x, dx))
    for q, higher, here, there in peers:
        pl.when(higher == 0)(functools.partial(send_z, q, there))
    for copy in fetches:
        copy.wait()

    n_fixed = NMAJ * GROUP
    wide = data4[pl.ds(own * pairs, pairs)].astype(f32)
    twiddle = wide_tab[:NMAJ].reshape(NMAJ, 2 * NMIN)
    twc = jnp.broadcast_to(twiddle[:, :NMIN][None], (pairs, NMAJ, NMIN)).reshape(pairs * NMAJ, NMIN)
    tws = jnp.broadcast_to(twiddle[:, NMIN:][None], (pairs, NMAJ, NMIN)).reshape(pairs * NMAJ, NMIN)
    n_half = second.shape[0] // 2

    def peak_of(src_b, peak):
        norms, stacks, bents = [], [], []
        for k in range(kb):
            row = tmpl4[src_b * kb + k].astype(f32)
            norm = jnp.sum(jnp.sum(row * row, axis=0, keepdims=True), axis=1, keepdims=True)
            norm_tab[src_b * kb + k] = jnp.broadcast_to(norm, (1, NMIN))
            norms.append(norm)
            real, imag = conj_product(wide, row[None])
            real = real.reshape(pairs * NMAJ, NMIN).astype(bf16)
            imag = imag.reshape(pairs * NMAJ, NMIN).astype(bf16)
            stacks.append(jnp.concatenate(
                [jnp.concatenate([real, imag], axis=1), jnp.concatenate([-imag, real], axis=1)], axis=0
            ))
        sections = [jnp.dot(fixed[:n_fixed, :], stack, preferred_element_type=f32) for stack in stacks]
        for section in sections:
            sr, si = section[:, :NMIN], section[:, NMIN:]
            bents.append(jnp.concatenate([sr * twc - si * tws, sr * tws + si * twc], axis=1).astype(bf16))
        snrs = [lax.dot_general(second[...], bent, (((1,), (1,)), ((), ())), preferred_element_type=f32)
                for bent in bents]
        for snr, norm in zip(snrs, norms):
            power = snr[:n_half] * snr[:n_half] + snr[n_half:] * snr[n_half:]
            peak = jnp.maximum(peak, power * (1.0 / norm))
        return peak

    peak = peak_of(b, jnp.zeros((n_half, pairs * NMAJ), f32))

    def answer_x(dx):
        pl.semaphore_wait(det_in.at[dx - 1, 0], 1)
        send_x(dx)
        pl.semaphore_wait(det_in.at[dx - 1, 1], 1)

    def answer_z(q, here, there):
        pl.semaphore_wait(blk_in.at[here], 1)
        send_z(q, there)

    for dx in range(1, n_det):
        pl.when(column(dx) > d)(functools.partial(answer_x, dx))
    for q, higher, here, there in peers:
        pl.when(higher == 1)(functools.partial(answer_z, q, here, there))
    pl.when(half == n_sub - 1)(lambda: pl.semaphore_wait(sub_in.at[0], 1))

    for dx in range(1, n_det):
        place = b * n_det + column(dx)
        arrived(data_part(place, 0, hp), x_recv.at[dx - 1])
        for q, higher, here, there in peers:
            remote(data_part(place, *late), data_send, xz_recv.at[there, dx - 1], {"blk": q})
        other_half(place, 0, hp)
    for q, higher, here, there in peers:
        arrived(data_part(q * n_det + d, *early), z_recv.at[0, here])
        for dx in range(1, n_det):
            block = data_part(q * n_det + d, *early)
            remote(block, data_send, zx_recv.at[here, n_det - 1 - dx], {"det": column(dx)})
            remote(block, data_send, cross_recv.at[0], {"det": column(dx), "sub": other})
        arrived(tmpl_part(q), t_recv.at[here])
        remote(tmpl_part(q), tmpl_send, ts_recv.at[here], {"sub": other})

    arrived(cuts.at[pl.ds(0, n_blk - 1)], cuts_recv.at[0])
    cut_rows[...] = jnp.zeros(cut_rows.shape, f32)
    cut_rows[:, NCUT - 1:NCUT] = jnp.full((n_tmpl, 1), NMAJ, f32)
    for blk in range(n_blk):
        cut_rows[blk * kb:(blk + 1) * kb, 0:n_cut] = (cuts[blk] >> 7).astype(f32)
        cut_rows[blk * kb:(blk + 1) * kb, 64:64 + n_cut] = (cuts[blk] & (NMIN - 1)).astype(f32)
    is_k = lax.broadcasted_iota(jnp.int32, (n_tmpl, n_trig), 0) == jnp.broadcast_to(ids_v[0], (n_tmpl, n_trig))
    pick_k = is_k.astype(f32).astype(bf16)

    def by_trigger(table):
        return lax.dot_general(pick_k, table, (((0,), (0,)), ((), ())), preferred_element_type=f32)

    trig_cuts = by_trigger(cut_rows[...].astype(bf16))
    lane = lax.broadcasted_iota(jnp.int32, (n_trig, NMIN), 1)
    spread = (
        (lax.broadcasted_iota(jnp.int32, (NMIN, 2 * NMIN), 0) < 64)
        == (lax.broadcasted_iota(jnp.int32, (NMIN, 2 * NMIN), 1) < NMIN)
    ).astype(f32).astype(bf16)
    base = ((lax.broadcasted_iota(jnp.int32, (n_trig, NMIN), 0) % GROUP) * NMAJ).astype(f32)
    at = lane.astype(f32)

    def cut_masks(first, count, last):
        spans = []
        for r in range(first, first + count):
            only = jnp.where((lane & 63) == r, trig_cuts, 0.0).astype(bf16)
            spans.append(jnp.dot(only, spread, preferred_element_type=f32))
        stacks = ([], [], [])
        for i, span in enumerate(spans):
            row = span[:, :NMIN] + base
            marks = (at == row, jnp.logical_and(at >= last, at < row), at < span[:, NMIN:])
            last = row
            for stack, mark in zip(stacks, marks):
                stack.append(mark.astype(f32).reshape(n_grp, GROUP, NMIN))
            if i % 2 == 1:
                rows = slice((first + i - 1) * GROUP, (first + i + 1) * GROUP)
                for stack, out in zip(stacks, (hot_out, between_out, keep_out)):
                    out[:, rows, :] = jnp.concatenate(stack[-2:], axis=1).astype(bf16)
        return last

    last = cut_masks(0, NCUT // 2, base)
    for q, higher, here, there in peers:
        arrived(data_part(q * n_det + d, *late), z_recv.at[1, here])
        other_half(q * n_det + d, 0, hp)
    cut_masks(NCUT // 2, NCUT // 2, last)
    for q in range(n_grp):
        spin_out[q] = jnp.dot(hot_out[q], fixed[n_fixed:2 * n_fixed, :], preferred_element_type=f32)

    def prepare(n, carry):
        k = ids_k[0, 0, n]
        row = tmpl4[k].astype(f32)
        phase = wide_tab[NMAJ + half * ((wide_tab.shape[0] - NMAJ) // n_sub) + ids_t[0, 0, n]]
        pc, ps = phase[:, :NMIN], phase[:, NMIN:]
        tr, ti = row[:, :NMIN], row[:, NMIN:]
        turned[n, :, :NMIN] = tr * pc + ti * ps
        turned[n, :, NMIN:] = tr * ps - ti * pc
        return carry

    def relayed():
        for q, higher, here, there in peers:
            for dx in range(1, n_det):
                place = q * n_det + column(dx)
                arrived(data_part(place, *late), xz_recv.at[here, dx - 1])
                other_half(place, *late)

    for i, (q, higher, here, there) in enumerate(peers):
        if i == PRE:
            relayed()
        arrived(tmpl4.at[pl.ds(q * kb + other * hk, hk)], ts_recv.at[here])
        peak = peak_of(q, peak)
    if len(peers) <= PRE:
        relayed()
    lax.fori_loop(0, n_trig, prepare, 0, unroll=16)

    rest = 1.0 / norm_tab[...].reshape(n_tmpl, NMIN)
    scale = jnp.zeros((n_trig, NMIN), f32)
    for _ in range(3):
        piece = rest.astype(bf16)
        rest = rest - piece.astype(f32)
        scale = scale + by_trigger(piece)
    rnorm_out[...] = scale

    swapped = swap_blocks(jnp.sqrt(peak))
    for u in range(n_half // 8):
        peak_out[:, u * 128:(u + 1) * 128] = swapped[8 * u:8 * u + 8, :]

    n_data = (n_blk * n_det - 1) * hp
    n_cross = (n_blk - 1) * (n_det - 1) * ha
    arrived(data4.at[pl.ds(0, n_data - n_cross)], s_recv.at[0])
    arrived(data4.at[pl.ds(0, n_cross)], cross_recv.at[0])
    for q, higher, here, there in peers:
        for dx in range(1, n_det):
            arrived(data_part(q * n_det + column(dx), *early), zx_recv.at[here, dx - 1])

    def filtered(n, carry):
        rows = data4[ids_p[0, 0, n]].astype(f32)
        dr, di = rows[:, :NMIN], rows[:, NMIN:]
        wr, wi = turned[n, :, :NMIN], turned[n, :, NMIN:]
        z_out[n] = jnp.concatenate([dr * wr - di * wi, dr * wi + di * wr], axis=1).astype(bf16)
        return carry

    lax.fori_loop(0, n_trig, filtered, 0, unroll=32)

    some = data4.at[pl.ds(0, 2 * n_data)]
    pltpu.make_async_copy(some, some, data_send.at[0]).wait()
    some = tmpl4.at[pl.ds(0, 2 * (n_blk - 1) * hk)]
    pltpu.make_async_copy(some, some, tmpl_send.at[0]).wait()
    some = cuts.at[pl.ds(0, n_blk - 1)]
    pltpu.make_async_copy(some, some, cuts_send.at[0]).wait()


def chi_kernel(z_in, hot_in, between_in, keep_in, spin_in, rnorm_in, fixed, peak_in, peak_out, chi_out, chi_rows, sem):
    f32, bf16 = jnp.float32, jnp.bfloat16
    n_grp = hot_in.shape[0]
    n_fixed = NMAJ * GROUP
    save_peak = pltpu.make_async_copy(peak_in, peak_out, sem.at[0])
    save_peak.start()
    at = lax.broadcasted_iota(jnp.int32, (GROUP * NCUT, NMIN), 1)
    row = lax.broadcasted_iota(jnp.int32, (GROUP * NCUT, NMIN), 0)
    step = ((at == row).astype(f32) - (at == row - GROUP).astype(f32)).astype(bf16)
    own_rows = lax.broadcasted_iota(jnp.int32, (2 * GROUP, NMIN), 0)
    whole = (lax.broadcasted_iota(jnp.int32, (2 * GROUP, NMIN), 1) // NMAJ == own_rows).astype(f32).astype(bf16)
    whole = jnp.concatenate([whole, jnp.zeros_like(whole)], axis=1)
    own_turn = fixed[n_fixed:2 * n_fixed, :].astype(f32)

    def rotate(v, w):
        v, w = v.astype(bf16), w.astype(bf16)
        vr, vi, wr, wi = v[:, :NMIN], v[:, NMIN:], w[:, :NMIN], w[:, NMIN:]
        return jnp.concatenate([vr * wr - vi * wi, vr * wi + vi * wr], axis=1).astype(bf16)

    def one_batch(t):
        rows = GROUP * NMAJ
        qs = [t * BATCH + i for i in range(BATCH)]
        zs = [z_in[pl.ds(q * GROUP, GROUP)].reshape(rows, 2 * NMIN) for q in qs]
        picks = [jnp.dot(hot_in[q], z, preferred_element_type=f32) for q, z in zip(qs, zs)]
        parts = []
        for q, pick in zip(qs, picks):
            keep = keep_in[q]
            parts.append(pick.astype(bf16) * jnp.concatenate([keep, keep], axis=1))
        moved = [jnp.dot(jnp.concatenate([z, part], axis=0), fixed[2 * n_fixed:, :], preferred_element_type=f32) for z, part in zip(zs, parts)]
        turned = [jnp.concatenate([rotate(m[:rows], own_turn), rotate(m[rows:], spin_in[q])], axis=0) for q, m in zip(qs, moved)]
        bins = []
        for q, turn in zip(qs, turned):
            mix = jnp.concatenate([jnp.concatenate([between_in[q], step], axis=1), whole], axis=0)
            bins.append(jnp.dot(mix, turn, preferred_element_type=f32))
        for q, bn in zip(qs, bins):
            br, bi = bn[:rows, :NMIN], bn[:rows, NMIN:]
            energy = jnp.sum((br * br + bi * bi).reshape(NCUT, GROUP, NMIN), axis=0)
            tr, ti = bn[rows:rows + GROUP, :NMIN], bn[rows:rows + GROUP, NMIN:]
            loud = tr * tr + ti * ti
            at_q = q * GROUP
            rnorm = rnorm_in[pl.ds(at_q, GROUP), :]
            reduced = jnp.maximum(energy - loud * (1.0 / NCUT), 0.0) * (NCUT / (2.0 * NCUT - 2.0)) * rnorm
            rho = jnp.sqrt(loud * rnorm)
            bend = jnp.exp(jnp.log((1.0 + reduced * reduced * reduced) * 0.5) * (-1.0 / 6.0))
            chi_rows[pl.ds(at_q, GROUP), :] = jnp.where(reduced > 1.0, rho * bend, rho)

    saves = []
    for t in range(n_grp // BATCH):
        one_batch(t)
        part = pl.ds(t * BATCH * GROUP, BATCH * GROUP)
        saves.append(pltpu.make_async_copy(chi_rows.at[part], chi_out.at[0, 0, part], sem.at[1 + t]))
        saves[-1].start()
    save_peak.wait()
    for save in saves:
        save.wait()


def fused(sizes, ids_k, ids_p, ids_t, own, tmpl, cuts, tables):
    n_blk, n_det, n_sub = sizes
    fixed, second, wide = tables
    n_tmpl = n_blk * tmpl.shape[0]
    n_trig = ids_k.shape[-1]
    n_grp = n_trig // GROUP
    hbm = pl.BlockSpec(memory_space=pltpu.HBM)
    vmem = pl.BlockSpec(memory_space=pltpu.VMEM)
    dma = pltpu.SemaphoreType.DMA
    f32, bf16 = jnp.float32, jnp.bfloat16
    n_half = second.shape[1] // 2
    peak_shape = (own.shape[0], n_half * NMAJ)
    rows = GROUP * NCUT
    made = [
        (peak_shape, f32),
        ((n_trig, NMAJ, 2 * NMIN), bf16),
        ((n_grp, rows, NMIN), bf16),
        ((n_grp, rows, NMIN), bf16),
        ((n_grp, rows, NMIN), bf16),
        ((n_grp, rows, 2 * NMIN), f32),
        ((n_trig, NMIN), f32),
        (fixed.shape, fixed.dtype),
    ]
    scratch = [
        pltpu.VMEM((n_blk * n_det * own.shape[0],) + own.shape[1:], own.dtype),
        pltpu.VMEM((n_tmpl,) + tmpl.shape[1:], tmpl.dtype),
        pltpu.VMEM((n_blk,) + cuts.shape, cuts.dtype),
    ]
    scratch += [pltpu.SMEM(ids_k.shape, jnp.int32)] * 3
    scratch += [
        pltpu.VMEM(ids_k.shape, jnp.int32),
        pltpu.VMEM(second.shape[1:], second.dtype),
        pltpu.VMEM(wide.shape, wide.dtype),
        pltpu.VMEM((n_tmpl, NMIN), f32),
        pltpu.VMEM((n_tmpl, 1, NMIN), f32),
        pltpu.VMEM((n_trig, NMAJ, 2 * NMIN), f32),
        dma((10,)), dma((1,)), dma((1,)), dma((1,)), dma((1,)),
        dma((n_blk - 1,)), dma((n_blk - 1,)), dma((n_det - 1,)), dma((2, n_blk - 1)),
        dma((n_blk - 1, n_det - 1)), dma((n_blk - 1, n_det - 1)), dma((1,)), dma((1,)),
        pltpu.SemaphoreType.REGULAR((n_blk - 1,)), pltpu.SemaphoreType.REGULAR((n_det - 1, 2)),
        pltpu.SemaphoreType.REGULAR((1,)),
    ]
    made_refs = pl.pallas_call(
        functools.partial(gather_kernel, n_blk, n_det, n_sub),
        out_shape=[pltpu.VMEM(shape, dtype) for shape, dtype in made],
        in_specs=[hbm] * 9,
        out_specs=[vmem] * len(made),
        scratch_shapes=scratch,
        compiler_params=pltpu.CompilerParams(
            collective_id=0, has_side_effects=True, vmem_limit_bytes=32 * 1024 * 1024
        ),
        name="gather_and_peak",
    )(*(pltpu.with_memory_space_constraint(x, pltpu.HBM)
        for x in (ids_k, ids_p, ids_t, own, tmpl, cuts, fixed, second, wide)))
    return pl.pallas_call(
        chi_kernel,
        out_shape=(
            jax.ShapeDtypeStruct(peak_shape, f32),
            jax.ShapeDtypeStruct(ids_k.shape + (STEPS * NMAJ,), f32),
        ),
        in_specs=[vmem] * len(made),
        out_specs=(hbm, hbm),
        scratch_shapes=[pltpu.VMEM((n_trig, STEPS * NMAJ), f32), dma((1 + n_grp // BATCH,))],
        compiler_params=pltpu.CompilerParams(vmem_limit_bytes=24 * 1024 * 1024),
        name="chi",
    )(*made_refs[1:], made_refs[0])


def body(sizes, data, templates, bin_cuts, trig_template, trig_pair, trig_tile):
    tables = tuple(jnp.asarray(t) for t in host_tables(sizes[2]))
    peak, chi = fused(sizes, trig_template, trig_pair, trig_tile, data, templates, bin_cuts, tables)
    return peak, chi


def solution(mesh):
    sizes = (mesh.shape["blk"], mesh.shape["det"], mesh.shape["sub"])
    return jax.shard_map(
        functools.partial(body, sizes),
        mesh=mesh,
        in_specs=(
            P(("groups", "blk", "det"), None, None),
            P(("groups", "blk"), None, None),
            P(("groups", "blk"), None),
            P(("groups", "blk", "det"), "sub", None),
            P(("groups", "blk", "det"), "sub", None),
            P(("groups", "blk", "det"), "sub", None),
        ),
        out_specs=(
            P(("groups", "blk", "det"), "sub"),
            P(("groups", "blk", "det"), "sub", None, None),
        ),
        check_vma=False,
    )
```
